128 devices in a mesh: dp: 16 (over z, x_lo, core), mic: 8 (over x_hi, y).
Axes of the slice: x: 4 (x_hi: 2, x_lo: 2; x = x_hi * 2 + x_lo), y: 4, z: 4, core: 2. Of those that a mesh axis runs over, the one named last changes fastest.
Arguments:
- waveform: bfloat16 [2, 32, 65536], P(None, 'mic', 'dp'), may hold values from -12 to 12
- filters: bfloat16 [512, 32], P('mic'), may hold values from -1 to 1
- speech_mask: bfloat16 [2, 256, 4096], P(None, 'mic', 'dp'), may hold values from 0.049804688 to 1
- noise_mask: bfloat16 [2, 256, 4096], P(None, 'mic', 'dp'), may hold values from 0.049804688 to 1
- target: float32 [2, 2, 256, 4096], P(None, None, 'mic', 'dp'), may hold values from -6 to 6
- ref_mic: int32 [2], replicated, may hold values from 0 to 31
Outputs:
- enhanced: float32 [2, 2, 256, 4096], P(None, None, 'mic', 'dp')
- filter_grad: float32 [512, 32], P('mic')
The draws below stay inside these ranges and needn't reach their ends.
All inputs are finite; a program needn't handle non-finite values.
Results may differ from the reference program's by a relative error of at most 0.015.
Values may be sent and summed in bfloat16 or wider, within the bound.
A program may use at most 128 MiB of HBM per device.

```python
import math
import jax
import jax.numpy as jnp
from jax import lax

FILTERS = 512
KERNEL = 32
STRIDE = 16
MICS = 32
BATCH = 2
T_DEV = 256
FREQS = 256
FRAMES = 4096
SAMPLES = 65536


def draw_waveform(key, part):
    keys = jax.random.split(jax.random.fold_in(key, 11), 5)
    block_count = FRAMES // T_DEV
    block_len = STRIDE * T_DEV
    sources = jax.random.normal(keys[0], (BATCH, 3, block_count, block_len), jnp.float32)
    gains = 0.6 * jax.random.normal(keys[1], (BATCH, MICS, block_count, 3), jnp.float32)
    position = (jnp.arange(SAMPLES, dtype=jnp.float32) / SAMPLES).reshape(block_count, block_len)
    noise = jax.random.normal(keys[2], (BATCH, MICS, block_count, block_len), jnp.float32)
    ramp = 1.0 + position
    loudness = jnp.exp(jax.random.uniform(keys[4], (BATCH, 1, block_count, 1), jnp.float32, minval=-1.2, maxval=1.0))
    mixed = gains[:, :, :, 0:1] * sources[:, 0:1] + gains[:, :, :, 1:2] * sources[:, 1:2] + gains[:, :, :, 2:3] * sources[:, 2:3]
    values = mixed * loudness * ramp + 0.5 * noise
    return jnp.clip(values, -12.0, 12.0).reshape(BATCH, MICS, SAMPLES).astype(jnp.bfloat16)


def block_scale(stream_key, dims, cuts, least, largest):
    def one(axis_at, blocks):
        steps = jax.random.uniform(jax.random.fold_in(jax.random.fold_in(stream_key, 6), axis_at), (blocks,), jnp.float32, least / len(cuts), largest / len(cuts))
        return jnp.repeat(jnp.exp(steps), dims[axis_at] // blocks).reshape((-1,) + (1,) * (len(dims) - axis_at - 1))

    factor_of = one(*cuts[0])
    for cut in cuts[1:]:
        factor_of = factor_of * one(*cut)
    return factor_of


def centred(key, extent, scale, bound, cuts=(), kind=jnp.bfloat16):
    entries = scale * jax.random.normal(key, extent, jnp.float32)
    if cuts:
        entries = entries * block_scale(key, extent, cuts, -0.22, 0.18)
    return jnp.clip(entries, -bound, bound).astype(kind)


def setup_inputs(seed: int = 0) -> dict:
    splits = jax.random.split(jax.random.key(seed), 7)
    waveform = draw_waveform(jax.random.fold_in(splits[6], 71), 0)
    filters = centred(splits[1], (FILTERS, KERNEL), KERNEL ** -0.5, 1.0, ((0, 8),))
    speech_mask = jnp.clip(0.049804688 + 0.9501953 * jax.random.uniform(splits[2], (BATCH, FREQS, FRAMES), jnp.float32) ** block_scale(splits[2], (BATCH, FREQS, FRAMES), ((1, 8), (2, 16)), -0.2, 0.2), 0.049804688, 1.0).astype(jnp.bfloat16)
    noise_mask = jnp.clip(0.049804688 + 0.9501953 * jax.random.uniform(splits[3], (BATCH, FREQS, FRAMES), jnp.float32) ** block_scale(splits[3], (BATCH, FREQS, FRAMES), ((1, 8), (2, 16)), -0.2, 0.2), 0.049804688, 1.0).astype(jnp.bfloat16)
    target = centred(splits[4], (BATCH, 2, FREQS, FRAMES), 1.0, 6.0, ((2, 8), (3, 16)), jnp.float32)
    ref_mic = jax.random.randint(splits[5], (BATCH,), 0, MICS).astype(jnp.int32)
    return dict(waveform=waveform, filters=filters, speech_mask=speech_mask, noise_mask=noise_mask, target=target, ref_mic=ref_mic)


LOAD_NOISE = 0.05
LOAD_SPEECH = 0.05
LOSS_SCALE = 64.0

def frame_signal(extended):
    batch, mic_count, samples = extended.shape
    block_count = samples // STRIDE
    pieces = jnp.swapaxes(extended.reshape(batch, mic_count, block_count, STRIDE), 2, 3)
    return jnp.concatenate([pieces[..., :-1], pieces[..., 1:]], axis=2)

def complex_parts(gram):
    mic_count = gram.shape[-1] // 2
    real_sum = gram[..., :mic_count, :mic_count] + gram[..., mic_count:, mic_count:]
    imag_sum = gram[..., mic_count:, :mic_count] - gram[..., :mic_count, mic_count:]
    return (real_sum, imag_sum)

def real_form(real_sum, imag_sum):
    top_rows = jnp.concatenate([real_sum, -imag_sum], axis=-1)
    bottom = jnp.concatenate([imag_sum, real_sum], axis=-1)
    return jnp.concatenate([top_rows, bottom], axis=-2)

def beam_weights(onehot, frame_total, speech_real, speech_imag, noise_real, noise_imag):
    mic_count = speech_real.shape[-1]
    identity = jnp.eye(2 * mic_count, dtype=jnp.float32)
    noise_cov = real_form(noise_real, noise_imag) / frame_total + LOAD_NOISE * identity
    speech_cols = jnp.concatenate([speech_real, speech_imag], axis=-2) / frame_total + LOAD_SPEECH * identity[:, :mic_count]
    factor = jnp.linalg.cholesky(noise_cov)
    halfway = jax.scipy.linalg.solve_triangular(factor, speech_cols, lower=True)
    ratios = jax.scipy.linalg.solve_triangular(factor, halfway, lower=True, trans=1)
    trace_sum = jnp.trace(ratios[..., :mic_count, :], axis1=-2, axis2=-1)
    column = jnp.einsum('bfim,bm->bfi', ratios, onehot, precision=lax.Precision.HIGHEST) / trace_sum[..., None]
    real_part = column[..., :mic_count]
    imag_part = column[..., mic_count:]
    first_row = jnp.concatenate([real_part, imag_part], axis=-1)
    second = jnp.concatenate([-imag_part, real_part], axis=-1)
    return jnp.stack([first_row, second], axis=-2)

def reference(waveform, filters, speech_mask, noise_mask, target, ref_mic):
    highest = lax.Precision.HIGHEST
    padded = jnp.concatenate([waveform, jnp.zeros((BATCH, MICS, STRIDE), jnp.bfloat16)], axis=2)
    frames_wide = frame_signal(padded).astype(jnp.float32)
    onehot = (jnp.arange(MICS, dtype=jnp.int32)[None, :] == ref_mic[:, None]).astype(jnp.float32)
    frame_total = float(FRAMES)
    grad_scale = 2.0 * LOSS_SCALE / (BATCH * FREQS * FRAMES)
    width = math.gcd(FREQS, 16)

    def weigh(speech_real, speech_imag, noise_real, noise_imag):
        return beam_weights(onehot, frame_total, speech_real, speech_imag, noise_real, noise_imag)

    def one_block(block_index):
        offset = block_index * width
        rows_wide = lax.dynamic_slice_in_dim(filters, 2 * offset, 2 * width, 0).astype(jnp.float32)
        encoded = jnp.einsum('rk,bmkt->brmt', rows_wide, frames_wide, precision=highest).astype(jnp.bfloat16)
        stacked_wide = encoded.reshape(BATCH, width, 2 * MICS, FRAMES).astype(jnp.float32)
        speech_block = lax.dynamic_slice_in_dim(speech_mask, offset, width, 1).astype(jnp.float32)[:, :, None, :]
        noise_block = lax.dynamic_slice_in_dim(noise_mask, offset, width, 1).astype(jnp.float32)[:, :, None, :]
        target_block = lax.dynamic_slice_in_dim(target, offset, width, 2)
        speech_part = (stacked_wide * speech_block).astype(jnp.bfloat16).astype(jnp.float32)
        noise_part = (stacked_wide * noise_block).astype(jnp.bfloat16).astype(jnp.float32)
        speech_gram = jnp.einsum('bfit,bfjt->bfij', speech_part, stacked_wide, precision=highest)
        noise_gram = jnp.einsum('bfit,bfjt->bfij', noise_part, stacked_wide, precision=highest)
        sums = complex_parts(speech_gram) + complex_parts(noise_gram)
        weights, pullback = jax.vjp(weigh, sums[0], sums[1], sums[2], sums[3])
        enhanced = jnp.einsum('bfvi,bfit->bvft', weights, stacked_wide, precision=highest)
        grad_wide = grad_scale * (enhanced - target_block)
        beam_grad = jnp.einsum('bvft,bfit->bfvi', grad_wide, stacked_wide, precision=highest)
        part_grads = pullback(beam_grad)
        speech_grad = real_form(part_grads[0], part_grads[1])
        noise_grad = real_form(part_grads[2], part_grads[3])
        stacked_grad = jnp.einsum('bfvi,bvft->bfit', weights, grad_wide, precision=highest)
        stacked_grad = stacked_grad + speech_block * jnp.einsum('bfij,bfjt->bfit', speech_grad, stacked_wide, precision=highest)
        stacked_grad = stacked_grad + jnp.einsum('bfji,bfjt->bfit', speech_grad, speech_part, precision=highest)
        stacked_grad = stacked_grad + noise_block * jnp.einsum('bfij,bfjt->bfit', noise_grad, stacked_wide, precision=highest)
        stacked_grad = stacked_grad + jnp.einsum('bfji,bfjt->bfit', noise_grad, noise_part, precision=highest)
        grad_rows = stacked_grad.astype(jnp.bfloat16).astype(jnp.float32).reshape(BATCH, 2 * width, MICS, FRAMES)
        row_grad = jnp.einsum('brmt,bmkt->rk', grad_rows, frames_wide, precision=highest)
        return (enhanced, row_grad)
    enhanced_all, grads = lax.map(one_block, jnp.arange(FREQS // width, dtype=jnp.int32))
    enhanced = jnp.transpose(enhanced_all, (1, 2, 0, 3, 4)).reshape(BATCH, 2, FREQS, FRAMES)
    return (enhanced, grads.reshape(FILTERS, KERNEL))
```

```python
import jax
import jax.numpy as jnp
from jax import lax
from jax.experimental import pallas as pl
from jax.experimental.pallas import tpu as pltpu
from jax.sharding import PartitionSpec as P

DP = 16
MIC = 8
MICS = 32
TD = 256
LOAD = 0.05
FRAME_TOTAL = 4096.0
GRAD_SCALE = 2.0 * 64.0 / (2 * 256 * FRAME_TOTAL)
F32 = jnp.float32
BF16 = jnp.bfloat16
HIGHEST = lax.Precision.HIGHEST
ROWS = 104
PAY = 72


def iota(shape, axis):
    return lax.broadcasted_iota(jnp.int32, shape, axis)


def dot_f32(a, b):
    return jnp.dot(a, b, precision=HIGHEST, preferred_element_type=F32)


def tile4(x):
    return jnp.concatenate([x, x, x, x], axis=0)


def diagonal_blocks(x):
    rows, lanes = iota((128, 128), 0), iota((128, 128), 1)
    return jnp.where(rows // 32 == lanes // 32, tile4(x), 0.0)


def fold4(x):
    return (x[0:32] + x[32:64]) + (x[64:96] + x[96:128])


def unpack_blocks(packed):
    rows, lanes = iota((128, 128), 0) % 32, iota((128, 128), 1) % 32
    blocks = diagonal_blocks(packed)
    turned = blocks.T
    real = jnp.where(rows <= lanes, blocks, turned)
    imag = jnp.where(rows > lanes, blocks, jnp.where(rows < lanes, -turned, 0.0))
    return real, imag


def complex_right(real, imag):
    return jnp.concatenate(
        [jnp.concatenate([real, imag], axis=1), jnp.concatenate([-imag, real], axis=1)], axis=0
    )


def inverse(a_r, a_i):
    lane = iota((32, 128), 1)
    row = iota((32, 128), 0)
    base = (lane // 32) * 32
    col = lane % 32
    for k in range(32):
        index = base + k
        c_r = jnp.take_along_axis(a_r, index, axis=1)
        c_i = jnp.take_along_axis(a_i, index, axis=1)
        scale = 1.0 / c_r[k : k + 1, :]
        here = col[0:1] == k
        r_r = jnp.where(here, 1.0, a_r[k : k + 1, :]) * scale
        r_i = jnp.where(here, 0.0, a_i[k : k + 1, :]) * scale
        at_col = col == k
        n_r = jnp.where(at_col, 0.0, a_r) - (c_r * r_r - c_i * r_i)
        n_i = jnp.where(at_col, 0.0, a_i) - (c_r * r_i + c_i * r_r)
        at_row = row == k
        a_r = jnp.where(at_row, r_r, n_r)
        a_i = jnp.where(at_row, r_i, n_i)
    return a_r, a_i


def solve(total, pick):
    lane = iota((32, 128), 1)
    row = iota((32, 128), 0)
    eye = jnp.where(row == lane % 32, 1.0, 0.0)
    inv_t = 1.0 / FRAME_TOTAL
    s_r, s_i = [fold4(x) for x in unpack_blocks(total[0:32])]
    n_r, n_i = [fold4(x) for x in unpack_blocks(total[32:64])]
    cb_r, cb_i = unpack_blocks(total[64:96])
    d_r, d_i = total[96:97], total[97:98]
    s_r = s_r * inv_t + LOAD * eye
    s_i = s_i * inv_t
    m_r, m_i = inverse(n_r * inv_t + LOAD * eye, n_i * inv_t)
    right_m = complex_right(diagonal_blocks(m_r), diagonal_blocks(m_i))
    xh = dot_f32(jnp.concatenate([s_r, s_i], axis=1), right_m)
    xh_r, xh_i = xh[:, :128], xh[:, 128:]
    at_ref = row == pick
    conj_c_r = jnp.sum(jnp.where(at_ref, xh_r, 0.0), axis=0, keepdims=True)
    conj_c_i = jnp.sum(jnp.where(at_ref, xh_i, 0.0), axis=0, keepdims=True)
    sref_r = jnp.sum(jnp.where(at_ref, s_r, 0.0), axis=0, keepdims=True)
    sref_i = jnp.sum(jnp.where(at_ref, s_i, 0.0), axis=0, keepdims=True)
    ones = jnp.where(iota((128, 128), 0) // 32 == iota((128, 128), 1) // 32, 1.0, 0.0)
    diag = jnp.sum(xh_r * eye, axis=0, keepdims=True)
    first = dot_f32(
        jnp.concatenate(
            [
                jnp.broadcast_to(diag, (8, 128)),
                m_r * sref_r + m_i * sref_i,
                m_i * sref_r - m_r * sref_i,
            ],
            axis=0,
        ),
        ones,
    )
    inv_tau = 1.0 / first[0:1]
    c_r, c_i = first[8:40], first[40:72]
    w_r = conj_c_r * inv_tau
    w_i = -conj_c_i * inv_tau
    right_c = complex_right(cb_r, -cb_i)
    row8 = jnp.broadcast_to(jnp.concatenate([w_r, w_i], axis=1), (8, 256))
    cw = dot_f32(row8, right_c)
    g_r = GRAD_SCALE * (cw[0:1, :128] - d_r)
    g_i = GRAD_SCALE * (cw[0:1, 128:] - d_i)
    gc_r, gc_i = g_r * inv_tau, g_i * inv_tau
    gw = (g_r * w_r + g_i * w_i) * inv_tau
    second = dot_f32(
        jnp.concatenate(
            [
                jnp.broadcast_to(gw, (8, 128)),
                m_r * gc_r - m_i * gc_i,
                m_r * gc_i + m_i * gc_r,
            ],
            axis=0,
        ),
        ones,
    )
    gt2 = -2.0 * second[0:1]
    u_r, u_i = second[8:40], second[40:72]
    right_xh = complex_right(diagonal_blocks(xh_r), diagonal_blocks(xh_i))
    q = dot_f32(jnp.concatenate([m_r, m_i], axis=1), right_xh)
    uh8 = jnp.broadcast_to(jnp.concatenate([gc_r, -gc_i], axis=1), (8, 256))
    uh = dot_f32(uh8, right_m)
    uh_r, uh_i = uh[0:1, :128], uh[0:1, 128:]
    col_ref = (lane % 32) == pick
    p_r = jnp.where(col_ref, u_r, 0.0) + jnp.where(at_ref, uh_r, 0.0) + gt2 * m_r
    p_i = jnp.where(col_ref, u_i, 0.0) + jnp.where(at_ref, uh_i, 0.0) + gt2 * m_i
    n_r = (u_r * conj_c_r - u_i * conj_c_i) + (c_r * uh_r - c_i * uh_i) + gt2 * q[:, :128]
    n_i = (u_r * conj_c_i + u_i * conj_c_r) + (c_r * uh_i + c_i * uh_r) + gt2 * q[:, 128:]
    upper = row <= lane % 32
    speech = jnp.where(upper, p_r, p_i) * inv_t
    noise = jnp.where(upper, n_r, n_i) * (-inv_t)
    return speech, noise, w_r, w_i


def block_filters(filters):
    lane = iota((32, 256), 1)
    spread = jnp.where(iota((32, 256), 0) == (lane // 128) * 16 + lane % 16, 1.0, 0.0)
    wide = jnp.dot(filters, spread.astype(BF16), preferred_element_type=F32).astype(BF16)
    repeat = jnp.where(iota((512, 64), 0) // 8 == iota((512, 64), 1), 1.0, 0.0).astype(BF16)
    full = jnp.dot(repeat, wide, preferred_element_type=F32)
    keep = iota((512, 256), 0) % 8 == (iota((512, 256), 1) % 128) // 16
    return jnp.where(keep, full, 0.0).astype(BF16)


def split(x):
    high = x.astype(BF16).astype(F32)
    return high, x - high


def nt_dot(a, b):
    return lax.dot_general(a, b, (((1,), (1,)), ((), ())), preferred_element_type=F32)


def body(
    wave_ref, head_ref, filt_ref, smask_ref, nmask_ref, target_ref, pick_ref,
    enh_ref, grad_ref,
    gath, heads, frames, zz, lhs, sb, rb, pay, sgq, fg, tt, ms, mn, fb, ua,
    g_send, g_recv, h_send, h_recv, s_send, s_recv, p_send, p_recv, f_send, f_recv,
):
    d = lax.axis_index("dp")
    mu = lax.axis_index("mic")
    prev = lax.rem(d + DP - 1, DP)
    nxt = lax.rem(d + 1, DP)

    def other_d(j):
        return lax.rem(d + j, DP)

    def other_m(j):
        return lax.rem(mu + j, MIC)

    def remote(src, dst, send, recv, dev_d, dev_m):
        return pltpu.make_async_remote_copy(
            src_ref=src, dst_ref=dst, send_sem=send, recv_sem=recv,
            device_id={"dp": dev_d, "mic": dev_m}, device_id_type=pl.DeviceIdType.MESH,
        )

    barrier = pltpu.get_barrier_semaphore()

    def greet(dev_d, dev_m):
        pl.semaphore_signal(
            barrier, inc=1, device_id={"dp": dev_d, "mic": dev_m},
            device_id_type=pl.DeviceIdType.MESH,
        )

    for j in range(1, MIC):
        greet(d, other_m(j))
        greet(prev, other_m(j))
        greet(nxt, other_m(j))
    for j in range(1, DP):
        greet(other_d(j), mu)

    fb[...] = block_filters(filt_ref[...])
    ms[...] = smask_ref[...].reshape(64, TD).astype(F32)
    mn[...] = nmask_ref[...].reshape(64, TD).astype(F32)

    pl.semaphore_wait(barrier, 3 * (MIC - 1) + DP - 1)

    def wave_copy(j):
        return remote(wave_ref, gath.at[mu], g_send.at[j], g_recv.at[mu], d, other_m(j))

    def head_copy(j):
        return remote(head_ref, heads.at[mu], h_send.at[j], h_recv.at[mu], prev, other_m(j))

    for j in range(1, MIC):
        wave_copy(j).start()
    for j in range(MIC):
        head_copy(j).start()
    gath[mu] = wave_ref[...]
    for j in range(1, MIC):
        src = other_m(j)
        remote(wave_ref, gath.at[src], g_send.at[j], g_recv.at[src], d, src).wait_recv()
    for j in range(MIC):
        src = other_m(j)
        remote(head_ref, heads.at[src], h_send.at[j], h_recv.at[src], prev, src).wait_recv()

    last = d == DP - 1
    eye128 = iota((128, 128), 0) == iota((128, 128), 1)
    low = iota((1, 128), 1) < 64
    end = iota((128, TD), 1) == TD - 1
    for b in range(2):
        for q in range(4):
            x = jnp.concatenate([gath[2 * q, b], gath[2 * q + 1, b]], axis=0).astype(F32)
            head = jnp.where(low, heads[2 * q, b : b + 1, :], heads[2 * q + 1, b : b + 1, :])
            head = jnp.where(last, 0.0, head)
            column = jnp.sum(jnp.where(eye128, head, 0.0), axis=1, keepdims=True)
            moved = jnp.where(end, column, pltpu.roll(x, TD - 1, axis=1))
            frames[b, q, 0:128, :] = x.astype(BF16)
            frames[b, q, 128:256, :] = moved.astype(BF16)

    @pl.loop(0, 4)
    def _(step):
        b = step // 2
        half = step % 2
        a0 = jnp.dot(fb[...], frames[b, 2 * half], preferred_element_type=F32)
        a1 = jnp.dot(fb[...], frames[b, 2 * half + 1], preferred_element_type=F32)
        a0 = a0.reshape(8, 4, 2, 8, TD)
        a1 = a1.reshape(8, 4, 2, 8, TD)
        z = jnp.concatenate([a0, a1], axis=3).astype(BF16)
        rows = pl.ds(pl.multiple_of(16 * half, 16), 16)
        groups = pl.ds(pl.multiple_of(8 * b, 8), 8)
        zz[groups, 0, :, rows, 0:TD] = z[:, :, 0]
        zz[groups, 0, :, rows, TD : 2 * TD] = z[:, :, 1]
        zz[groups, 1, :, rows, 0:TD] = z[:, :, 1]
        zz[groups, 1, :, rows, TD : 2 * TD] = -z[:, :, 0]

    lane32 = iota((32, 128), 1)
    row32 = iota((32, 128), 0)
    upper = row32 <= lane32 % 32
    row8 = iota((8, 128), 0)
    lane8 = iota((8, 128), 1)
    own8 = row8 == lane8 // 32

    def sum_copy(j, o):
        return remote(sb.at[o], rb.at[d], s_send.at[j], s_recv.at[d], o, mu)

    def mask_row(ref, s):
        row = ref[pl.ds(s, 1), :]
        return jnp.concatenate([row, row], axis=1)

    def group_sums(o):
        b = o // 8
        f0 = (o % 8) * 4
        for g in range(4):
            tt[o, g : g + 1, 0:TD] = target_ref[b, 0, pl.ds(f0 + g, 1), :]
            tt[o, g : g + 1, TD : 2 * TD] = target_ref[b, 1, pl.ds(f0 + g, 1), :]
        tt[o, 4:8, :] = jnp.zeros((4, 2 * TD), F32)
        t = tt[o]
        turned = jnp.concatenate([-t[:, TD:], t[:, :TD]], axis=1)
        t_hi, t_lo = split(t)
        u_hi, u_lo = split(turned)
        lhs[768:800, :] = jnp.concatenate([t_hi, u_hi, t_lo, u_lo], axis=0).astype(BF16)
        for g in range(4):
            z = zz[o, 0, g].astype(F32)
            r = zz[o, 1, g].astype(F32)
            m = mask_row(ms, 4 * o + g)
            n = mask_row(mn, 4 * o + g)
            base = 192 * g
            lhs[base : base + 32, :] = (z * m).astype(BF16)
            lhs[base + 32 : base + 64, :] = (r * m).astype(BF16)
            lhs[base + 64 : base + 96, :] = (z * n).astype(BF16)
            lhs[base + 96 : base + 128, :] = (r * n).astype(BF16)
            lhs[base + 128 : base + 160, :] = z.astype(BF16)
            lhs[base + 160 : base + 192, :] = r.astype(BF16)
        right = zz[o, 0].reshape(128, 2 * TD)
        out = nt_dot(lhs[...], right)
        for kind in range(3):
            value = jnp.zeros((32, 128), F32)
            for g in range(4):
                base = 192 * g + 64 * kind
                one = jnp.where(upper, out[base : base + 32], out[base + 32 : base + 64])
                value = jnp.where(lane32 // 32 == g, one, value)
            sb[o, 32 * kind : 32 * kind + 32, :] = value
        d_r = jnp.sum(jnp.where(own8, out[768:776] + out[784:792], 0.0), axis=0, keepdims=True)
        d_i = jnp.sum(jnp.where(own8, out[776:784] + out[792:800], 0.0), axis=0, keepdims=True)
        sb[o, 96:104, :] = jnp.where(row8 == 0, d_r, jnp.where(row8 == 1, d_i, 0.0))

    @pl.loop(1, DP)
    def _(j):
        o = other_d(j)
        group_sums(o)
        sum_copy(j, o).start()

    group_sums(d)
    rb[d] = sb[d]
    for j in range(1, DP):
        src = other_d(j)
        remote(sb.at[d], rb.at[src], s_send.at[j], s_recv.at[src], src, mu).wait_recv()
    total = rb[0]
    for j in range(1, DP):
        total = total + rb[j]
    pick = jnp.where(d < DP // 2, pick_ref[0], pick_ref[1])
    speech, noise, w_r, w_i = solve(total, pick)
    pay[d, 0:32, :] = speech
    pay[d, 32:64, :] = noise
    pay[d, 64:72, :] = jnp.where(row8 == 0, w_r, jnp.where(row8 == 1, w_i, 0.0))

    def pay_copy(j):
        o = other_d(j)
        return remote(pay.at[d], pay.at[d], p_send.at[j], p_recv.at[d], o, mu)

    for j in range(1, DP):
        pay_copy(j).start()

    def group_grads(o):
        b = o // 8
        f0 = (o % 8) * 4
        right = zz[o].reshape(256, 2 * TD)
        w_r = jnp.where(own8, pay[o, 64:65, :], 0.0)
        w_i = jnp.where(own8, pay[o, 65:66, :], 0.0)
        wr_hi, wr_lo = split(w_r)
        wi_hi, wi_lo = split(w_i)
        left = jnp.concatenate(
            [jnp.concatenate([wr_hi, wi_hi], axis=1), jnp.concatenate([wr_lo, wi_lo], axis=1)],
            axis=0,
        ).astype(BF16)
        both = jnp.dot(left, right, preferred_element_type=F32)
        enh = both[0:8] + both[8:16]
        for g in range(4):
            enh_ref[b, 0, pl.ds(f0 + g, 1), :] = enh[g : g + 1, 0:TD]
            enh_ref[b, 1, pl.ds(f0 + g, 1), :] = enh[g : g + 1, TD : 2 * TD]
        e = GRAD_SCALE * (enh - tt[o])
        turned = jnp.concatenate([-e[:, TD:], e[:, :TD]], axis=1)
        e_hi, e_lo = split(e)
        r_hi, r_lo = split(turned)
        e_rows = jnp.concatenate([e_hi, r_hi, e_hi, r_hi, e_lo, r_lo], axis=0).astype(BF16)
        w_rows = jnp.concatenate([wr_hi, wi_hi, wr_lo, wi_lo, wr_hi, wi_hi], axis=0)
        direct = jnp.dot(w_rows.T.astype(BF16), e_rows, preferred_element_type=F32)
        ua[0:128, :] = direct
        s_r, s_i = unpack_blocks(pay[o, 0:32, :])
        n_r, n_i = unpack_blocks(pay[o, 32:64, :])
        mats = jnp.concatenate(
            [jnp.concatenate([s_r, -s_i], axis=1), jnp.concatenate([n_r, -n_i], axis=1)], axis=0
        )
        m_hi, m_lo = split(mats)
        applied = jnp.dot(m_hi.astype(BF16), right, preferred_element_type=F32)
        applied = applied + jnp.dot(m_lo.astype(BF16), right, preferred_element_type=F32)
        ua[128:384, :] = applied
        for g in range(4):
            at = 32 * g
            m = mask_row(ms, 4 * o + g)
            n = mask_row(mn, 4 * o + g)
            sg = (
                ua[at : at + 32, :]
                + m * ua[128 + at : 160 + at, :]
                + n * ua[256 + at : 288 + at, :]
            )
            place = pl.ds(pl.multiple_of(16 * (f0 + g), 16), 16)
            for q in range(4):
                piece = sg[8 * q : 8 * q + 8]
                sgq[b, q, place, :] = jnp.concatenate(
                    [piece[:, :TD], piece[:, TD:]], axis=0
                ).astype(BF16)

    group_grads(d)

    @pl.loop(1, DP)
    def _(j):
        o = other_d(j)
        remote(pay.at[d], pay.at[o], p_send.at[j], p_recv.at[o], o, mu).wait_recv()
        group_grads(o)

    acc = jnp.zeros((512, 256), F32)
    for b in range(2):
        for q in range(4):
            acc = acc + nt_dot(sgq[b, q], frames[b, q])
    keep = iota((512, 256), 0) % 8 == (iota((512, 256), 1) % 128) // 16
    rows = jnp.sum(jnp.where(keep, acc, 0.0).reshape(64, 8, 256), axis=1)
    at, lane = iota((256, 128), 0), iota((256, 128), 1)
    tap = (at // 128) * 16 + at % 16
    part = jnp.zeros((16, 128), F32)
    for p in range(4):
        place = jnp.where((lane // 32 == p) & (lane % 32 == tap), 1.0, 0.0)
        part = part + dot_f32(rows[16 * p : 16 * p + 16], place)
    fg[d] = part

    def grad_copy(j):
        return remote(fg.at[d], fg.at[d], f_send.at[j], f_recv.at[d], other_d(j), mu)

    for j in range(1, DP):
        grad_copy(j).start()
    for j in range(1, DP):
        src = other_d(j)
        remote(fg.at[d], fg.at[src], f_send.at[j], f_recv.at[src], src, mu).wait_recv()
    result = fg[0]
    for j in range(1, DP):
        result = result + fg[j]
    grad_ref[...] = result

    for j in range(1, MIC):
        wave_copy(j).wait_send()
    for j in range(MIC):
        head_copy(j).wait_send()
    for j in range(1, DP):
        sum_copy(j, other_d(j)).wait_send()
        pay_copy(j).wait_send()
        grad_copy(j).wait_send()


def local(waveform, filters, speech_mask, noise_mask, target, ref_mic):
    wave = waveform.reshape(2, 4, TD, 16).transpose(0, 1, 3, 2).reshape(2, 64, TD)
    head = waveform[:, :, :16].reshape(2, 64).astype(F32)
    head = jnp.pad(jnp.concatenate([head, head], axis=1), ((0, 6), (0, 0)))
    vmem = pl.BlockSpec(memory_space=pltpu.VMEM)
    dma = pltpu.SemaphoreType.DMA
    enhanced, grad = pl.pallas_call(
        body,
        out_shape=(
            jax.ShapeDtypeStruct((2, 2, 32, TD), F32),
            jax.ShapeDtypeStruct((16, 128), F32),
        ),
        in_specs=[vmem] * 6 + [pl.BlockSpec(memory_space=pltpu.SMEM)],
        out_specs=(vmem, vmem),
        scratch_shapes=[
            pltpu.VMEM((MIC, 2, 64, TD), BF16),
            pltpu.VMEM((MIC, 8, 128), F32),
            pltpu.VMEM((2, 4, 256, TD), BF16),
            pltpu.VMEM((16, 2, 4, 32, 2 * TD), BF16),
            pltpu.VMEM((800, 2 * TD), BF16),
            pltpu.VMEM((DP, ROWS, 128), F32),
            pltpu.VMEM((DP, ROWS, 128), F32),
            pltpu.VMEM((DP, PAY, 128), F32),
            pltpu.VMEM((2, 4, 512, TD), BF16),
            pltpu.VMEM((DP, 16, 128), F32),
            pltpu.VMEM((DP, 8, 2 * TD), F32),
            pltpu.VMEM((64, TD), F32),
            pltpu.VMEM((64, TD), F32),
            pltpu.VMEM((512, 256), BF16),
            pltpu.VMEM((384, 2 * TD), F32),
            dma((MIC,)), dma((MIC,)), dma((MIC,)), dma((MIC,)),
            dma((DP,)), dma((DP,)), dma((DP,)), dma((DP,)), dma((DP,)), dma((DP,)),
        ],
        compiler_params=pltpu.CompilerParams(
            collective_id=0, has_side_effects=True, vmem_limit_bytes=60 * 1024 * 1024
        ),
    )(wave, head, filters, speech_mask, noise_mask, target, ref_mic)
    filter_grad = grad.reshape(16, 4, 32).transpose(1, 0, 2).reshape(64, 32)
    return (enhanced, filter_grad)


def solution(mesh):
    in_specs = (
        P(None, "mic", "dp"),
        P("mic", None),
        P(None, "mic", "dp"),
        P(None, "mic", "dp"),
        P(None, None, "mic", "dp"),
        P(),
    )
    out_specs = (P(None, None, "mic", "dp"), P("mic", None))
    return jax.shard_map(local, mesh=mesh, in_specs=in_specs, out_specs=out_specs, check_vma=False)
```

```python
import jax
import jax.numpy as jnp
from jax import lax
from jax.experimental import pallas as pl
from jax.experimental.pallas import tpu as pltpu
from jax.sharding import PartitionSpec as P

DP = 16
MIC = 8
MICS = 32
TD = 256
LOAD = 0.05
FRAME_TOTAL = 4096.0
GRAD_SCALE = 2.0 * 64.0 / (2 * 256 * FRAME_TOTAL)
F32 = jnp.float32
BF16 = jnp.bfloat16
HIGHEST = lax.Precision.HIGHEST
ROWS = 104
PAY = 72


def iota(shape, axis):
    return lax.broadcasted_iota(jnp.int32, shape, axis)


def dot_f32(a, b):
    return jnp.dot(a, b, precision=HIGHEST, preferred_element_type=F32)


def tile4(x):
    return jnp.concatenate([x, x, x, x], axis=0)


def diagonal_blocks(x):
    rows, lanes = iota((128, 128), 0), iota((128, 128), 1)
    return jnp.where(rows // 32 == lanes // 32, tile4(x), 0.0)


def fold4(x):
    return (x[0:32] + x[32:64]) + (x[64:96] + x[96:128])


def unpack_blocks(packed):
    rows, lanes = iota((128, 128), 0) % 32, iota((128, 128), 1) % 32
    blocks = diagonal_blocks(packed)
    turned = blocks.T
    real = jnp.where(rows <= lanes, blocks, turned)
    imag = jnp.where(rows > lanes, blocks, jnp.where(rows < lanes, -turned, 0.0))
    return real, imag


def complex_right(real, imag):
    return jnp.concatenate(
        [jnp.concatenate([real, imag], axis=1), jnp.concatenate([-imag, real], axis=1)], axis=0
    )


def inverse(a_r, a_i):
    lane = iota((32, 128), 1)
    row = iota((32, 128), 0)
    base = (lane // 32) * 32
    col = lane % 32
    for k in range(32):
        index = base + k
        c_r = jnp.take_along_axis(a_r, index, axis=1)
        c_i = jnp.take_along_axis(a_i, index, axis=1)
        scale = 1.0 / c_r[k : k + 1, :]
        here = col[0:1] == k
        r_r = jnp.where(here, 1.0, a_r[k : k + 1, :]) * scale
        r_i = jnp.where(here, 0.0, a_i[k : k + 1, :]) * scale
        at_col = col == k
        n_r = jnp.where(at_col, 0.0, a_r) - (c_r * r_r - c_i * r_i)
        n_i = jnp.where(at_col, 0.0, a_i) - (c_r * r_i + c_i * r_r)
        at_row = row == k
        a_r = jnp.where(at_row, r_r, n_r)
        a_i = jnp.where(at_row, r_i, n_i)
    return a_r, a_i


def solve(total, pick):
    lane = iota((32, 128), 1)
    row = iota((32, 128), 0)
    eye = jnp.where(row == lane % 32, 1.0, 0.0)
    inv_t = 1.0 / FRAME_TOTAL
    s_r, s_i = [fold4(x) for x in unpack_blocks(total[0:32])]
    n_r, n_i = [fold4(x) for x in unpack_blocks(total[32:64])]
    cb_r, cb_i = unpack_blocks(total[64:96])
    d_r, d_i = total[96:97], total[97:98]
    s_r = s_r * inv_t + LOAD * eye
    s_i = s_i * inv_t
    m_r, m_i = inverse(n_r * inv_t + LOAD * eye, n_i * inv_t)
    right_m = complex_right(diagonal_blocks(m_r), diagonal_blocks(m_i))
    xh = dot_f32(jnp.concatenate([s_r, s_i], axis=1), right_m)
    xh_r, xh_i = xh[:, :128], xh[:, 128:]
    at_ref = row == pick
    conj_c_r = jnp.sum(jnp.where(at_ref, xh_r, 0.0), axis=0, keepdims=True)
    conj_c_i = jnp.sum(jnp.where(at_ref, xh_i, 0.0), axis=0, keepdims=True)
    sref_r = jnp.sum(jnp.where(at_ref, s_r, 0.0), axis=0, keepdims=True)
    sref_i = jnp.sum(jnp.where(at_ref, s_i, 0.0), axis=0, keepdims=True)
    ones = jnp.where(iota((128, 128), 0) // 32 == iota((128, 128), 1) // 32, 1.0, 0.0)
    diag = jnp.sum(xh_r * eye, axis=0, keepdims=True)
    first = dot_f32(
        jnp.concatenate(
            [
                jnp.broadcast_to(diag, (8, 128)),
                m_r * sref_r + m_i * sref_i,
                m_i * sref_r - m_r * sref_i,
            ],
            axis=0,
        ),
        ones,
    )
    inv_tau = 1.0 / first[0:1]
    c_r, c_i = first[8:40], first[40:72]
    w_r = conj_c_r * inv_tau
    w_i = -conj_c_i * inv_tau
    right_c = complex_right(cb_r, -cb_i)
    row8 = jnp.broadcast_to(jnp.concatenate([w_r, w_i], axis=1), (8, 256))
    cw = dot_f32(row8, right_c)
    g_r = GRAD_SCALE * (cw[0:1, :128] - d_r)
    g_i = GRAD_SCALE * (cw[0:1, 128:] - d_i)
    gc_r, gc_i = g_r * inv_tau, g_i * inv_tau
    gw = (g_r * w_r + g_i * w_i) * inv_tau
    second = dot_f32(
        jnp.concatenate(
            [
                jnp.broadcast_to(gw, (8, 128)),
                m_r * gc_r - m_i * gc_i,
                m_r * gc_i + m_i * gc_r,
            ],
            axis=0,
        ),
        ones,
    )
    gt2 = -2.0 * second[0:1]
    u_r, u_i = second[8:40], second[40:72]
    right_xh = complex_right(diagonal_blocks(xh_r), diagonal_blocks(xh_i))
    q = dot_f32(jnp.concatenate([m_r, m_i], axis=1), right_xh)
    uh8 = jnp.broadcast_to(jnp.concatenate([gc_r, -gc_i], axis=1), (8, 256))
    uh = dot_f32(uh8, right_m)
    uh_r, uh_i = uh[0:1, :128], uh[0:1, 128:]
    col_ref = (lane % 32) == pick
    p_r = jnp.where(col_ref, u_r, 0.0) + jnp.where(at_ref, uh_r, 0.0) + gt2 * m_r
    p_i = jnp.where(col_ref, u_i, 0.0) + jnp.where(at_ref, uh_i, 0.0) + gt2 * m_i
    n_r = (u_r * conj_c_r - u_i * conj_c_i) + (c_r * uh_r - c_i * uh_i) + gt2 * q[:, :128]
    n_i = (u_r * conj_c_i + u_i * conj_c_r) + (c_r * uh_i + c_i * uh_r) + gt2 * q[:, 128:]
    upper = row <= lane % 32
    speech = jnp.where(upper, p_r, p_i) * inv_t
    noise = jnp.where(upper, n_r, n_i) * (-inv_t)
    return speech, noise, w_r, w_i


def block_filters(filters):
    lane = iota((32, 256), 1)
    spread = jnp.where(iota((32, 256), 0) == (lane // 128) * 16 + lane % 16, 1.0, 0.0)
    wide = jnp.dot(filters, spread.astype(BF16), preferred_element_type=F32).astype(BF16)
    repeat = jnp.where(iota((512, 64), 0) // 8 == iota((512, 64), 1), 1.0, 0.0).astype(BF16)
    full = jnp.dot(repeat, wide, preferred_element_type=F32)
    keep = iota((512, 256), 0) % 8 == (iota((512, 256), 1) % 128) // 16
    return jnp.where(keep, full, 0.0).astype(BF16)


def split(x):
    high = x.astype(BF16).astype(F32)
    return high, x - high


def nt_dot(a, b):
    return lax.dot_general(a, b, (((1,), (1,)), ((), ())), preferred_element_type=F32)


def body(
    wave_ref, head_ref, filt_ref, smask_ref, nmask_ref, target_ref, pick_ref,
    enh_ref, grad_ref,
    gath, heads, frames, zz, lhs, sb, rb, pay, sgq, fg, tt, ms, mn, fb, ua,
    g_send, g_recv, h_send, h_recv, s_send, s_recv, p_send, p_recv, f_send, f_recv,
):
    d = lax.axis_index("dp")
    mu = lax.axis_index("mic")
    prev = lax.rem(d + DP - 1, DP)
    nxt = lax.rem(d + 1, DP)
    at_z, at_x, at_c = d // 4, (d // 2) % 2, d % 2

    def rel(dz, dx, dc):
        return ((at_z + dz) % 4) * 4 + ((at_x + dx) % 2) * 2 + (at_c + dc) % 2

    def table(i, values):
        out = values[0]
        for k in range(1, len(values)):
            out = jnp.where(i == k, values[k], out)
        return out

    core, side, up, down = rel(0, 0, 1), rel(0, 1, 0), rel(1, 0, 0), rel(3, 0, 0)

    def other_d(j):
        return lax.rem(d + j, DP)

    def other_m(j):
        return lax.rem(mu + j, MIC)

    def remote(src, dst, send, recv, dev_d, dev_m):
        return pltpu.make_async_remote_copy(
            src_ref=src, dst_ref=dst, send_sem=send, recv_sem=recv,
            device_id={"dp": dev_d, "mic": dev_m}, device_id_type=pl.DeviceIdType.MESH,
        )

    barrier = pltpu.get_barrier_semaphore()

    def greet(dev_d, dev_m):
        pl.semaphore_signal(
            barrier, inc=1, device_id={"dp": dev_d, "mic": dev_m},
            device_id_type=pl.DeviceIdType.MESH,
        )

    for j in range(1, MIC):
        greet(d, other_m(j))
    for peer in (core, side, up, down, prev, nxt):
        greet(peer, mu)

    fb[...] = block_filters(filt_ref[...])
    ms[...] = smask_ref[...].reshape(64, TD).astype(F32)
    mn[...] = nmask_ref[...].reshape(64, TD).astype(F32)

    pl.semaphore_wait(barrier, MIC + 5)

    def wave_copy(j):
        return remote(wave_ref, gath.at[mu], g_send.at[j], g_recv.at[mu], d, other_m(j))

    def head_copy(j):
        return remote(heads.at[mu], heads.at[mu], h_send.at[j], h_recv.at[mu], d, other_m(j))

    def head_first():
        return remote(head_ref, heads.at[mu], h_send.at[0], h_recv.at[mu], prev, mu)

    head_first().start()
    for j in range(1, MIC):
        wave_copy(j).start()
    gath[mu] = wave_ref[...]
    head_first().wait_recv()
    for j in range(1, MIC):
        head_copy(j).start()
    for j in range(1, MIC):
        src = other_m(j)
        remote(wave_ref, gath.at[src], g_send.at[j], g_recv.at[src], d, src).wait_recv()
    for j in range(1, MIC):
        src = other_m(j)
        remote(heads.at[mu], heads.at[src], h_send.at[j], h_recv.at[src], d, src).wait_recv()

    last = d == DP - 1
    eye128 = iota((128, 128), 0) == iota((128, 128), 1)
    low = iota((1, 128), 1) < 64
    end = iota((128, TD), 1) == TD - 1
    for b in range(2):
        for q in range(4):
            x = jnp.concatenate([gath[2 * q, b], gath[2 * q + 1, b]], axis=0).astype(F32)
            head = jnp.where(low, heads[2 * q, b : b + 1, :], heads[2 * q + 1, b : b + 1, :])
            head = jnp.where(last, 0.0, head)
            column = jnp.sum(jnp.where(eye128, head, 0.0), axis=1, keepdims=True)
            moved = jnp.where(end, column, pltpu.roll(x, TD - 1, axis=1))
            frames[b, q, 0:128, :] = x.astype(BF16)
            frames[b, q, 128:256, :] = moved.astype(BF16)

    @pl.loop(0, 4)
    def _(step):
        b = step // 2
        half = step % 2
        a0 = jnp.dot(fb[...], frames[b, 2 * half], preferred_element_type=F32)
        a1 = jnp.dot(fb[...], frames[b, 2 * half + 1], preferred_element_type=F32)
        a0 = a0.reshape(8, 4, 2, 8, TD)
        a1 = a1.reshape(8, 4, 2, 8, TD)
        z = jnp.concatenate([a0, a1], axis=3).astype(BF16)
        rows = pl.ds(pl.multiple_of(16 * half, 16), 16)
        groups = pl.ds(pl.multiple_of(8 * b, 8), 8)
        zz[groups, 0, :, rows, 0:TD] = z[:, :, 0]
        zz[groups, 0, :, rows, TD : 2 * TD] = z[:, :, 1]
        zz[groups, 1, :, rows, 0:TD] = z[:, :, 1]
        zz[groups, 1, :, rows, TD : 2 * TD] = -z[:, :, 0]

    lane32 = iota((32, 128), 1)
    row32 = iota((32, 128), 0)
    upper = row32 <= lane32 % 32
    row8 = iota((8, 128), 0)
    lane8 = iota((8, 128), 1)
    own8 = row8 == lane8 // 32

    def mask_row(ref, s):
        row = ref[pl.ds(s, 1), :]
        return jnp.concatenate([row, row], axis=1)

    def group_sums(o):
        b = o // 8
        f0 = (o % 8) * 4
        for g in range(4):
            tt[o, g : g + 1, 0:TD] = target_ref[b, 0, pl.ds(f0 + g, 1), :]
            tt[o, g : g + 1, TD : 2 * TD] = target_ref[b, 1, pl.ds(f0 + g, 1), :]
        tt[o, 4:8, :] = jnp.zeros((4, 2 * TD), F32)
        t = tt[o]
        turned = jnp.concatenate([-t[:, TD:], t[:, :TD]], axis=1)
        t_hi, t_lo = split(t)
        u_hi, u_lo = split(turned)
        lhs[768:800, :] = jnp.concatenate([t_hi, u_hi, t_lo, u_lo], axis=0).astype(BF16)
        for g in range(4):
            z = zz[o, 0, g].astype(F32)
            r = zz[o, 1, g].astype(F32)
            m = mask_row(ms, 4 * o + g)
            n = mask_row(mn, 4 * o + g)
            base = 192 * g
            lhs[base : base + 32, :] = (z * m).astype(BF16)
            lhs[base + 32 : base + 64, :] = (r * m).astype(BF16)
            lhs[base + 64 : base + 96, :] = (z * n).astype(BF16)
            lhs[base + 96 : base + 128, :] = (r * n).astype(BF16)
            lhs[base + 128 : base + 160, :] = z.astype(BF16)
            lhs[base + 160 : base + 192, :] = r.astype(BF16)
        right = zz[o, 0].reshape(128, 2 * TD)
        out = nt_dot(lhs[...], right)
        for kind in range(3):
            value = jnp.zeros((32, 128), F32)
            for g in range(4):
                base = 192 * g + 64 * kind
                one = jnp.where(upper, out[base : base + 32], out[base + 32 : base + 64])
                value = jnp.where(lane32 // 32 == g, one, value)
            sb[o, 32 * kind : 32 * kind + 32, :] = value
        d_r = jnp.sum(jnp.where(own8, out[768:776] + out[784:792], 0.0), axis=0, keepdims=True)
        d_i = jnp.sum(jnp.where(own8, out[776:784] + out[792:800], 0.0), axis=0, keepdims=True)
        sb[o, 96:104, :] = jnp.where(row8 == 0, d_r, jnp.where(row8 == 1, d_i, 0.0))

    def sum_copy(o, slot, sem, dev):
        return remote(sb.at[o], rb.at[slot], s_send.at[sem], s_recv.at[slot], dev, mu)

    def add_slot(o, slot):
        sum_copy(o, slot, slot, core).wait_recv()
        sb[o] = sb[o] + rb[slot]

    order = [(2, 0, 1), (2, 1, 1), (2, 0, 0), (2, 1, 0), (3, 0, 1), (1, 1, 1), (1, 0, 1), (3, 1, 1),
             (3, 0, 0), (1, 1, 0), (1, 0, 0), (3, 1, 0), (0, 1, 1), (0, 0, 1), (0, 1, 0), (0, 0, 0)]

    @pl.loop(0, DP)
    def _(i):
        dz = table(i, [k[0] for k in order])
        dx = table(i, [k[1] for k in order])
        dc = table(i, [k[2] for k in order])
        o = rel(dz, dx, dc)
        slot = o // 2
        group_sums(o)

        @pl.when(dc == 1)
        def _():
            sum_copy(o, slot, slot, core).start()

        @pl.when(dc == 0)
        def _():
            add_slot(o, slot)

        @pl.when(i == 2)
        def _():
            sum_copy(o, 8, 8, up).start()

        @pl.when(i == 3)
        def _():
            sum_copy(o, 9, 9, down).start()

        @pl.when(i == 8)
        def _():
            sum_copy(o, 12, 10, down).start()

        @pl.when(i == 9)
        def _():
            sum_copy(o, 13, 11, up).start()

        @pl.when(i == 10)
        def _():
            add_slot(o, 8)
            sum_copy(o, 10, 12, up).start()

        @pl.when(i == 11)
        def _():
            add_slot(o, 9)
            sum_copy(o, 11, 13, down).start()

    across = rel(0, 1, 0)
    add_slot(across, 13)
    add_slot(across, 11)
    sum_copy(across, 14, 14, side).start()
    add_slot(d, 12)
    add_slot(d, 10)
    add_slot(d, 14)
    total = sb[d]
    pick = jnp.where(d < DP // 2, pick_ref[0], pick_ref[1])
    speech, noise, w_r, w_i = solve(total, pick)
    pay[d, 0:32, :] = speech
    pay[d, 32:64, :] = noise
    pay[d, 64:72, :] = jnp.where(row8 == 0, w_r, jnp.where(row8 == 1, w_i, 0.0))

    def pay_copy(o, sem, dev):
        return remote(pay.at[o], pay.at[o], p_send.at[sem], p_recv.at[o], dev, mu)

    for k, dev in enumerate((side, up, down, core)):
        pay_copy(d, k, dev).start()

    def group_grads(o):
        b = o // 8
        f0 = (o % 8) * 4
        right = zz[o].reshape(256, 2 * TD)
        w_r = jnp.where(own8, pay[o, 64:65, :], 0.0)
        w_i = jnp.where(own8, pay[o, 65:66, :], 0.0)
        wr_hi, wr_lo = split(w_r)
        wi_hi, wi_lo = split(w_i)
        left = jnp.concatenate(
            [jnp.concatenate([wr_hi, wi_hi], axis=1), jnp.concatenate([wr_lo, wi_lo], axis=1)],
            axis=0,
        ).astype(BF16)
        both = jnp.dot(left, right, preferred_element_type=F32)
        enh = both[0:8] + both[8:16]
        for g in range(4):
            enh_ref[b, 0, pl.ds(f0 + g, 1), :] = enh[g : g + 1, 0:TD]
            enh_ref[b, 1, pl.ds(f0 + g, 1), :] = enh[g : g + 1, TD : 2 * TD]
        e = GRAD_SCALE * (enh - tt[o])
        turned = jnp.concatenate([-e[:, TD:], e[:, :TD]], axis=1)
        e_hi, e_lo = split(e)
        r_hi, r_lo = split(turned)
        e_rows = jnp.concatenate([e_hi, r_hi, e_hi, r_hi, e_lo, r_lo], axis=0).astype(BF16)
        w_rows = jnp.concatenate([wr_hi, wi_hi, wr_lo, wi_lo, wr_hi, wi_hi], axis=0)
        direct = jnp.dot(w_rows.T.astype(BF16), e_rows, preferred_element_type=F32)
        ua[0:128, :] = direct
        s_r, s_i = unpack_blocks(pay[o, 0:32, :])
        n_r, n_i = unpack_blocks(pay[o, 32:64, :])
        mats = jnp.concatenate(
            [jnp.concatenate([s_r, -s_i], axis=1), jnp.concatenate([n_r, -n_i], axis=1)], axis=0
        )
        m_hi, m_lo = split(mats)
        applied = jnp.dot(m_hi.astype(BF16), right, preferred_element_type=F32)
        applied = applied + jnp.dot(m_lo.astype(BF16), right, preferred_element_type=F32)
        ua[128:384, :] = applied
        for g in range(4):
            at = 32 * g
            m = mask_row(ms, 4 * o + g)
            n = mask_row(mn, 4 * o + g)
            sg = (
                ua[at : at + 32, :]
                + m * ua[128 + at : 160 + at, :]
                + n * ua[256 + at : 288 + at, :]
            )
            place = pl.ds(pl.multiple_of(16 * (f0 + g), 16), 16)
            for q in range(4):
                piece = sg[8 * q : 8 * q + 8]
                sgq[b, q, place, :] = jnp.concatenate(
                    [piece[:, :TD], piece[:, TD:]], axis=0
                ).astype(BF16)

    spread = [(0, 0, 0), (0, 0, 1), (0, 1, 0), (3, 0, 0), (1, 0, 0), (3, 1, 0), (1, 1, 0), (2, 0, 0),
              (2, 1, 0), (0, 1, 1), (3, 0, 1), (1, 0, 1), (3, 1, 1), (1, 1, 1), (2, 0, 1), (2, 1, 1)]

    @pl.loop(0, DP)
    def _(i):
        dz = table(i, [k[0] for k in spread])
        dx = table(i, [k[1] for k in spread])
        dc = table(i, [k[2] for k in spread])
        o = rel(dz, dx, dc)

        @pl.when(i > 0)
        def _():
            pay_copy(o, 0, core).wait_recv()

        @pl.when(i == 2)
        def _():
            pay_copy(o, 4, up).start()
            pay_copy(o, 5, down).start()

        @pl.when(i == 3)
        def _():
            pay_copy(o, 6, up).start()

        @pl.when(i == 6)
        def _():
            pay_copy(o, 7, down).start()

        @pl.when((i >= 2) & (i <= 8))
        def _():
            pay_copy(o, 6 + i, core).start()

        group_grads(o)

    acc = jnp.zeros((512, 256), F32)
    for b in range(2):
        for q in range(4):
            acc = acc + nt_dot(sgq[b, q], frames[b, q])
    keep = iota((512, 256), 0) % 8 == (iota((512, 256), 1) % 128) // 16
    rows = jnp.sum(jnp.where(keep, acc, 0.0).reshape(64, 8, 256), axis=1)
    at, lane = iota((256, 128), 0), iota((256, 128), 1)
    tap = (at // 128) * 16 + at % 16
    part = jnp.zeros((16, 128), F32)
    for p in range(4):
        place = jnp.where((lane // 32 == p) & (lane % 32 == tap), 1.0, 0.0)
        part = part + dot_f32(rows[16 * p : 16 * p + 16], place)
    fg[d] = part

    def grad_copy(j):
        return remote(fg.at[d], fg.at[d], f_send.at[j], f_recv.at[d], other_d(j), mu)

    for j in range(1, DP):
        grad_copy(j).start()
    for j in range(1, DP):
        src = other_d(j)
        remote(fg.at[d], fg.at[src], f_send.at[j], f_recv.at[src], src, mu).wait_recv()
    result = fg[0]
    for j in range(1, DP):
        result = result + fg[j]
    grad_ref[...] = result

    head_first().wait_send()
    for j in range(1, MIC):
        wave_copy(j).wait_send()
        head_copy(j).wait_send()
    for j in range(DP - 1):
        sum_copy(d, 0, j, core).wait_send()
        pay_copy(d, j, core).wait_send()
    for j in range(1, DP):
        grad_copy(j).wait_send()


def local(waveform, filters, speech_mask, noise_mask, target, ref_mic):
    wave = waveform.reshape(2, 4, TD, 16).transpose(0, 1, 3, 2).reshape(2, 64, TD)
    head = waveform[:, :, :16].reshape(2, 64).astype(F32)
    head = jnp.pad(jnp.concatenate([head, head], axis=1), ((0, 6), (0, 0)))
    vmem = pl.BlockSpec(memory_space=pltpu.VMEM)
    dma = pltpu.SemaphoreType.DMA
    enhanced, grad = pl.pallas_call(
        body,
        out_shape=(
            jax.ShapeDtypeStruct((2, 2, 32, TD), F32),
            jax.ShapeDtypeStruct((16, 128), F32),
        ),
        in_specs=[vmem] * 6 + [pl.BlockSpec(memory_space=pltpu.SMEM)],
        out_specs=(vmem, vmem),
        scratch_shapes=[
            pltpu.VMEM((MIC, 2, 64, TD), BF16),
            pltpu.VMEM((MIC, 8, 128), F32),
            pltpu.VMEM((2, 4, 256, TD), BF16),
            pltpu.VMEM((16, 2, 4, 32, 2 * TD), BF16),
            pltpu.VMEM((800, 2 * TD), BF16),
            pltpu.VMEM((DP, ROWS, 128), F32),
            pltpu.VMEM((DP - 1, ROWS, 128), F32),
            pltpu.VMEM((DP, PAY, 128), F32),
            pltpu.VMEM((2, 4, 512, TD), BF16),
            pltpu.VMEM((DP, 16, 128), F32),
            pltpu.VMEM((DP, 8, 2 * TD), F32),
            pltpu.VMEM((64, TD), F32),
            pltpu.VMEM((64, TD), F32),
            pltpu.VMEM((512, 256), BF16),
            pltpu.VMEM((384, 2 * TD), F32),
            dma((MIC,)), dma((MIC,)), dma((MIC,)), dma((MIC,)),
            dma((DP,)), dma((DP,)), dma((DP,)), dma((DP,)), dma((DP,)), dma((DP,)),
        ],
        compiler_params=pltpu.CompilerParams(
            collective_id=0, has_side_effects=True, vmem_limit_bytes=60 * 1024 * 1024
        ),
    )(wave, head, filters, speech_mask, noise_mask, target, ref_mic)
    filter_grad = grad.reshape(16, 4, 32).transpose(1, 0, 2).reshape(64, 32)
    return (enhanced, filter_grad)


def solution(mesh):
    in_specs = (
        P(None, "mic", "dp"),
        P("mic", None),
        P(None, "mic", "dp"),
        P(None, "mic", "dp"),
        P(None, None, "mic", "dp"),
        P(),
    )
    out_specs = (P(None, None, "mic", "dp"), P("mic", None))
    return jax.shard_map(local, mesh=mesh, in_specs=in_specs, out_specs=out_specs, check_vma=False)
```

```python
import jax
import jax.numpy as jnp
from jax import lax
from jax.experimental import pallas as pl
from jax.experimental.pallas import tpu as pltpu
from jax.sharding import PartitionSpec as P

DP = 16
MIC = 8
MICS = 32
TD = 256
LOAD = 0.05
FRAME_TOTAL = 4096.0
GRAD_SCALE = 2.0 * 64.0 / (2 * 256 * FRAME_TOTAL)
F32 = jnp.float32
BF16 = jnp.bfloat16
HIGHEST = lax.Precision.HIGHEST
ROWS = 104
PAY = 72


def iota(shape, axis):
    return lax.broadcasted_iota(jnp.int32, shape, axis)


def dot_f32(a, b):
    return jnp.dot(a, b, precision=HIGHEST, preferred_element_type=F32)


def tile4(x):
    return jnp.concatenate([x, x, x, x], axis=0)


def diagonal_blocks(x):
    rows, lanes = iota((128, 128), 0), iota((128, 128), 1)
    return jnp.where(rows // 32 == lanes // 32, tile4(x), 0.0)


def fold4(x):
    return (x[0:32] + x[32:64]) + (x[64:96] + x[96:128])


def unpack_blocks(packed):
    rows, lanes = iota((128, 128), 0) % 32, iota((128, 128), 1) % 32
    blocks = diagonal_blocks(packed)
    turned = blocks.T
    real = jnp.where(rows <= lanes, blocks, turned)
    imag = jnp.where(rows > lanes, blocks, jnp.where(rows < lanes, -turned, 0.0))
    return real, imag


def complex_right(real, imag):
    return jnp.concatenate(
        [jnp.concatenate([real, imag], axis=1), jnp.concatenate([-imag, real], axis=1)], axis=0
    )


def inverse(a_r, a_i):
    lane = iota((32, 128), 1)
    row = iota((32, 128), 0)
    base = (lane // 32) * 32
    col = lane % 32
    for k in range(32):
        index = base + k
        c_r = jnp.take_along_axis(a_r, index, axis=1)
        c_i = jnp.take_along_axis(a_i, index, axis=1)
        scale = 1.0 / c_r[k : k + 1, :]
        here = col[0:1] == k
        r_r = jnp.where(here, 1.0, a_r[k : k + 1, :]) * scale
        r_i = jnp.where(here, 0.0, a_i[k : k + 1, :]) * scale
        at_col = col == k
        n_r = jnp.where(at_col, 0.0, a_r) - (c_r * r_r - c_i * r_i)
        n_i = jnp.where(at_col, 0.0, a_i) - (c_r * r_i + c_i * r_r)
        at_row = row == k
        a_r = jnp.where(at_row, r_r, n_r)
        a_i = jnp.where(at_row, r_i, n_i)
    return a_r, a_i


def solve(total, pick):
    lane = iota((32, 128), 1)
    row = iota((32, 128), 0)
    eye = jnp.where(row == lane % 32, 1.0, 0.0)
    inv_t = 1.0 / FRAME_TOTAL
    s_r, s_i = [fold4(x) for x in unpack_blocks(total[0:32])]
    n_r, n_i = [fold4(x) for x in unpack_blocks(total[32:64])]
    cb_r, cb_i = unpack_blocks(total[64:96])
    d_r, d_i = total[96:97], total[97:98]
    s_r = s_r * inv_t + LOAD * eye
    s_i = s_i * inv_t
    m_r, m_i = inverse(n_r * inv_t + LOAD * eye, n_i * inv_t)
    right_m = complex_right(diagonal_blocks(m_r), diagonal_blocks(m_i))
    xh = dot_f32(jnp.concatenate([s_r, s_i], axis=1), right_m)
    xh_r, xh_i = xh[:, :128], xh[:, 128:]
    at_ref = row == pick
    conj_c_r = jnp.sum(jnp.where(at_ref, xh_r, 0.0), axis=0, keepdims=True)
    conj_c_i = jnp.sum(jnp.where(at_ref, xh_i, 0.0), axis=0, keepdims=True)
    sref_r = jnp.sum(jnp.where(at_ref, s_r, 0.0), axis=0, keepdims=True)
    sref_i = jnp.sum(jnp.where(at_ref, s_i, 0.0), axis=0, keepdims=True)
    ones = jnp.where(iota((128, 128), 0) // 32 == iota((128, 128), 1) // 32, 1.0, 0.0)
    diag = jnp.sum(xh_r * eye, axis=0, keepdims=True)
    first = dot_f32(
        jnp.concatenate(
            [
                jnp.broadcast_to(diag, (8, 128)),
                m_r * sref_r + m_i * sref_i,
                m_i * sref_r - m_r * sref_i,
            ],
            axis=0,
        ),
        ones,
    )
    inv_tau = 1.0 / first[0:1]
    c_r, c_i = first[8:40], first[40:72]
    w_r = conj_c_r * inv_tau
    w_i = -conj_c_i * inv_tau
    right_c = complex_right(cb_r, -cb_i)
    row8 = jnp.broadcast_to(jnp.concatenate([w_r, w_i], axis=1), (8, 256))
    cw = dot_f32(row8, right_c)
    g_r = GRAD_SCALE * (cw[0:1, :128] - d_r)
    g_i = GRAD_SCALE * (cw[0:1, 128:] - d_i)
    gc_r, gc_i = g_r * inv_tau, g_i * inv_tau
    gw = (g_r * w_r + g_i * w_i) * inv_tau
    second = dot_f32(
        jnp.concatenate(
            [
                jnp.broadcast_to(gw, (8, 128)),
                m_r * gc_r - m_i * gc_i,
                m_r * gc_i + m_i * gc_r,
            ],
            axis=0,
        ),
        ones,
    )
    gt2 = -2.0 * second[0:1]
    u_r, u_i = second[8:40], second[40:72]
    right_xh = complex_right(diagonal_blocks(xh_r), diagonal_blocks(xh_i))
    q = dot_f32(jnp.concatenate([m_r, m_i], axis=1), right_xh)
    uh8 = jnp.broadcast_to(jnp.concatenate([gc_r, -gc_i], axis=1), (8, 256))
    uh = dot_f32(uh8, right_m)
    uh_r, uh_i = uh[0:1, :128], uh[0:1, 128:]
    col_ref = (lane % 32) == pick
    p_r = jnp.where(col_ref, u_r, 0.0) + jnp.where(at_ref, uh_r, 0.0) + gt2 * m_r
    p_i = jnp.where(col_ref, u_i, 0.0) + jnp.where(at_ref, uh_i, 0.0) + gt2 * m_i
    n_r = (u_r * conj_c_r - u_i * conj_c_i) + (c_r * uh_r - c_i * uh_i) + gt2 * q[:, :128]
    n_i = (u_r * conj_c_i + u_i * conj_c_r) + (c_r * uh_i + c_i * uh_r) + gt2 * q[:, 128:]
    upper = row <= lane % 32
    speech = jnp.where(upper, p_r, p_i) * inv_t
    noise = jnp.where(upper, n_r, n_i) * (-inv_t)
    return speech, noise, w_r, w_i


def tn_dot(a, b):
    return lax.dot_general(a, b, (((0,), (0,)), ((), ())), preferred_element_type=F32)


def block_filters(filters_t):
    lane = iota((32, 256), 1)
    spread = jnp.where(iota((32, 256), 0) == (lane // 128) * 16 + lane % 16, 1.0, 0.0)
    wide = tn_dot(filters_t, spread.astype(BF16)).astype(BF16)
    repeat = jnp.where(iota((512, 64), 0) // 8 == iota((512, 64), 1), 1.0, 0.0).astype(BF16)
    full = jnp.dot(repeat, wide, preferred_element_type=F32)
    keep = iota((512, 256), 0) % 8 == (iota((512, 256), 1) % 128) // 16
    return jnp.where(keep, full, 0.0).astype(BF16)


def split(x):
    high = x.astype(BF16).astype(F32)
    return high, x - high


def nt_dot(a, b):
    return lax.dot_general(a, b, (((1,), (1,)), ((), ())), preferred_element_type=F32)


def body(
    wave_ref, filt_ref, smask_ref, nmask_ref, target_ref, pick_ref,
    enh_ref, grad_ref,
    wblk, head, gath, heads, frames, zz, yy, lhs, sb, rb, pay, sgq, fg, tt, ms, mn, fb,
    g_send, g_recv, h_send, h_recv, s_send, s_recv, p_send, p_recv, f_send, f_recv,
):
    d = lax.axis_index("dp")
    mu = lax.axis_index("mic")
    prev = lax.rem(d + DP - 1, DP)
    nxt = lax.rem(d + 1, DP)
    at_z, at_x, at_c = d // 4, (d // 2) % 2, d % 2
    chip = d // 2
    core = 2 * chip + 1 - at_c

    def rel(dz, dx, dc):
        return ((at_z + dz) % 4) * 4 + ((at_x + dx) % 2) * 2 + (at_c + dc) % 2

    others = [rel(0, 1, 0), rel(1, 0, 0), rel(3, 0, 0), rel(1, 1, 0), rel(3, 1, 0), rel(2, 0, 0), rel(2, 1, 0)]

    def table(i, values):
        out = values[0]
        for k in range(1, len(values)):
            out = jnp.where(i == k, values[k], out)
        return out

    def other_d(j):
        return lax.rem(d + j, DP)

    def other_m(j):
        return lax.rem(mu + j, MIC)

    def remote(src, dst, send, recv, dev_d, dev_m):
        return pltpu.make_async_remote_copy(
            src_ref=src, dst_ref=dst, send_sem=send, recv_sem=recv,
            device_id={"dp": dev_d, "mic": dev_m}, device_id_type=pl.DeviceIdType.MESH,
        )

    barrier = pltpu.get_barrier_semaphore()

    def greet(dev_d, dev_m):
        pl.semaphore_signal(
            barrier, inc=1, device_id={"dp": dev_d, "mic": dev_m},
            device_id_type=pl.DeviceIdType.MESH,
        )

    for j in range(1, MIC):
        greet(d, other_m(j))
    for peer in others + [core, prev, nxt]:
        greet(peer, mu)

    turn = iota((128, 1024), 0)
    lane = iota((128, 1024), 1)
    choose = (turn % 4 == lane // TD) & (turn // 4 == (lane % TD) // 8)
    choose = jnp.where(choose, 1.0, 0.0).astype(BF16)
    phase = iota((16, 1024), 1) % 8
    for b in range(2):
        rows = wave_ref[b].astype(F32)
        head[4 * b : 4 * b + 4, :] = rows[:, 0:128]
        stacked = jnp.concatenate([rows[:, 128 * r : 128 * r + 128] for r in range(32)], axis=0)
        spread = jnp.dot(stacked.T.astype(BF16), choose, preferred_element_type=F32)
        taps = spread[0:16]
        for k in range(1, 8):
            taps = jnp.where(phase == k, spread[16 * k : 16 * k + 16], taps)
        for m in range(4):
            wblk[b, 16 * m : 16 * m + 16, :] = taps[:, TD * m : TD * m + TD].astype(BF16)

    fb[...] = block_filters(filt_ref[...])
    ms[...] = smask_ref[...].reshape(64, TD).astype(F32)
    mn[...] = nmask_ref[...].reshape(64, TD).astype(F32)
    for o in range(DP):
        for v in range(2):
            tt[o, 8 * v : 8 * v + 4, :] = target_ref[o // 8, v, (o % 8) * 4 : (o % 8) * 4 + 4, :]
            tt[o, 8 * v + 4 : 8 * v + 8, :] = jnp.zeros((4, TD), F32)

    pl.semaphore_wait(barrier, MIC + DP // 2 + 1)

    def wave_copy(b, j, slot, dev):
        return remote(wblk.at[b], gath.at[slot, b], g_send.at[MIC * b + j], g_recv.at[MIC * b + slot], d, dev)

    def head_copy(j, slot, dev):
        return remote(heads.at[mu], heads.at[slot], h_send.at[j], h_recv.at[slot], d, dev)

    def head_first():
        return remote(head, heads.at[mu], h_send.at[0], h_recv.at[mu], prev, mu)

    head_first().start()
    for j in range(1, MIC):
        wave_copy(0, j, mu, other_m(j)).start()
    gath[mu] = wblk[...]
    head_first().wait_recv()
    for j in range(1, MIC):
        head_copy(j, mu, other_m(j)).start()
    for j in range(1, MIC):
        wave_copy(1, j, mu, other_m(j)).start()

    last = d == DP - 1
    tap128 = iota((128, 128), 1) == iota((128, 128), 0) % 16
    end = iota((128, TD), 1) == TD - 1

    def encode(b):
        for q in range(4):
            x = jnp.concatenate([gath[2 * q, b], gath[2 * q + 1, b]], axis=0).astype(F32)
            near = jnp.concatenate(
                [
                    jnp.broadcast_to(heads[2 * q + p, 4 * b + m : 4 * b + m + 1, :], (16, 128))
                    for p in range(2)
                    for m in range(4)
                ],
                axis=0,
            )
            near = jnp.where(last, 0.0, near)
            column = jnp.sum(jnp.where(tap128, near, 0.0), axis=1, keepdims=True)
            moved = jnp.where(end, column, pltpu.roll(x, TD - 1, axis=1))
            frames[b, q, 0:128, :] = x.astype(BF16)
            frames[b, q, 128:256, :] = moved.astype(BF16)
        for half in range(2):
            a0 = jnp.dot(fb[...], frames[b, 2 * half], preferred_element_type=F32)
            a1 = jnp.dot(fb[...], frames[b, 2 * half + 1], preferred_element_type=F32)
            z = jnp.concatenate(
                [a0.reshape(8, 4, 2, 8, TD), a1.reshape(8, 4, 2, 8, TD)], axis=3
            ).astype(BF16)
            for v in range(2):
                zz[8 * b : 8 * b + 8, v, :, 16 * half : 16 * half + 16, :] = z[:, :, v]

    lane32 = iota((32, 128), 1)
    upper = iota((32, 128), 0) <= lane32 % 32
    row8 = iota((8, 128), 0)
    own8 = row8 == iota((8, 128), 1) // 32

    def group_sums(o):
        t_hi, t_lo = split(tt[o])
        lhs[512:768, :] = zz[o].reshape(256, TD)
        lhs[768:800, :] = jnp.concatenate([t_hi, t_lo], axis=0).astype(BF16)
        for g in range(4):
            for k, ref in enumerate((ms, mn)):
                mask = jnp.broadcast_to(ref[pl.ds(4 * o + g, 1), :], (32, TD)).astype(BF16)
                for v in range(2):
                    part = zz[o, v, g] * mask
                    at = 128 * v + 32 * g
                    lhs[256 * k + at : 256 * k + at + 32, :] = part
                    yy[o, k, at : at + 32, :] = part
        out = nt_dot(lhs[...], zz[o].reshape(256, TD))
        for kind in range(3):
            value = jnp.zeros((32, 128), F32)
            for g in range(4):
                re = out[256 * kind + 32 * g : 256 * kind + 32 * g + 32]
                im = out[256 * kind + 128 + 32 * g : 256 * kind + 160 + 32 * g]
                one = jnp.where(upper, re[:, :128] + im[:, 128:], im[:, :128] - re[:, 128:])
                value = jnp.where(lane32 // 32 == g, one, value)
            sb[o, 32 * kind : 32 * kind + 32, :] = value
        t0 = out[768:776] + out[784:792]
        t1 = out[776:784] + out[792:800]
        d_r = jnp.sum(jnp.where(own8, t0[:, :128] + t1[:, 128:], 0.0), axis=0, keepdims=True)
        d_i = jnp.sum(jnp.where(own8, t0[:, 128:] - t1[:, :128], 0.0), axis=0, keepdims=True)
        sb[o, 96:104, :] = jnp.where(row8 == 0, d_r, jnp.where(row8 == 1, d_i, 0.0))

    def sum_copy(o, slot, sem, dev):
        return remote(sb.at[o], rb.at[slot], s_send.at[sem], s_recv.at[slot], dev, mu)

    def add_slot(o, slot):
        sum_copy(o, slot, slot, core).wait_recv()
        sb[o] = sb[o] + rb[slot]

    for b in range(2):
        for j in range(1, MIC):
            wave_copy(b, j, other_m(j), mu).wait_recv()
        if b == 0:
            for j in range(1, MIC):
                head_copy(j, other_m(j), mu).wait_recv()
        encode(b)
        here = jnp.where(at_z // 2 == b, 1, 0)

        @pl.loop(0, 8)
        def _(i):
            mine = table(i, [0, 0, 1, 0, 1, 0, 1, 1])
            k = table(i, [0, 1, 0, 2, 1, 3, 2, 3])
            to = 2 * (2 * b + (at_z + k // 2 + here) % 2) + (at_x + 1 + k) % 2
            o = 2 * to + (at_c + 1 + mine) % 2
            group_sums(o)

            @pl.when(mine == 0)
            def _():
                sum_copy(o, to, to, core).start()

            @pl.when(mine == 1)
            def _():
                add_slot(o, to)

            @pl.when((mine == 1) & (to != chip))
            def _():
                sum_copy(o, 8 + chip, 8 + to, o).start()

    for k in range(7):
        add_slot(d, 8 + others[k] // 2)
    pick = jnp.where(d < DP // 2, pick_ref[0], pick_ref[1])
    speech, noise, w_r, w_i = solve(sb[d], pick)
    pay[d, 0:32, :] = speech
    pay[d, 32:64, :] = noise
    pay[d, 64:72, :] = jnp.where(row8 == 0, w_r, jnp.where(row8 == 1, w_i, 0.0))

    def pay_copy(o, sem, dev):
        return remote(pay.at[o], pay.at[o], p_send.at[sem], p_recv.at[o], dev, mu)

    for k, dev in enumerate([core] + others):
        pay_copy(d, k, dev).start()

    def group_grads(o):
        b = o // 8
        f0 = (o % 8) * 4
        w_r = jnp.where(own8, pay[o, 64:65, :], 0.0)
        w_i = jnp.where(own8, pay[o, 65:66, :], 0.0)
        wr_hi, wr_lo = split(w_r)
        wi_hi, wi_lo = split(w_i)

        def wide(p, q):
            return jnp.concatenate([p, q], axis=1)

        first = jnp.concatenate([wide(wr_hi, wi_hi), wide(-wi_hi, wr_hi)], axis=0)
        second = jnp.concatenate([wide(wr_lo, wi_lo), wide(-wi_lo, wr_lo)], axis=0)
        left = jnp.concatenate([first, second], axis=0)
        both = jnp.dot(left.astype(BF16), zz[o].reshape(256, TD), preferred_element_type=F32)
        enh = both[0:16] + both[16:32]
        for g in range(4):
            enh_ref[b, 0, pl.ds(f0 + g, 1), :] = enh[g : g + 1, :]
            enh_ref[b, 1, pl.ds(f0 + g, 1), :] = enh[8 + g : 9 + g, :]
        e_hi, e_lo = split(GRAD_SCALE * (enh - tt[o]))
        s_r, s_i = unpack_blocks(pay[o, 0:32, :])
        n_r, n_i = unpack_blocks(pay[o, 32:64, :])
        parts = []
        for r, i in ((s_r, s_i), (n_r, n_i)):
            r_hi, r_lo = split(r)
            i_hi, i_lo = split(i)
            for p, q in ((r_hi, i_hi), (r_lo, i_lo)):
                parts.append(jnp.concatenate([wide(p, -q), wide(q, p)], axis=0).astype(BF16))
        e_rows = jnp.concatenate([e_hi, e_hi, e_lo], axis=0).astype(BF16)
        w_cols = jnp.concatenate([first, second, first], axis=0).T.astype(BF16)
        sg = jnp.dot(w_cols, e_rows, preferred_element_type=F32)
        for k in range(2):
            for part in parts[2 * k : 2 * k + 2]:
                sg = sg + jnp.dot(part, yy[o, k], preferred_element_type=F32)
        for g in range(4):
            place = pl.ds(pl.multiple_of(16 * (f0 + g), 16), 16)
            for q in range(4):
                at = 32 * g + 8 * q
                sgq[b, q, place, :] = jnp.concatenate(
                    [sg[at : at + 8], sg[128 + at : 136 + at]], axis=0
                ).astype(BF16)

    spread = [(0, 0, 0), (0, 0, 1), (0, 1, 0), (1, 0, 0), (3, 0, 0), (0, 1, 1), (1, 1, 0), (3, 1, 0),
              (1, 0, 1), (3, 0, 1), (2, 0, 0), (2, 1, 0), (1, 1, 1), (3, 1, 1), (2, 0, 1), (2, 1, 1)]

    @pl.loop(0, DP)
    def _(i):
        dz = table(i, [k[0] for k in spread])
        dx = table(i, [k[1] for k in spread])
        dc = table(i, [k[2] for k in spread])
        o = rel(dz, dx, dc)

        @pl.when(i > 0)
        def _():
            pay_copy(o, 0, core).wait_recv()

        @pl.when((i > 0) & (dc == 0))
        def _():
            pay_copy(o, 8 + o // 2, core).start()

        group_grads(o)

    acc = jnp.zeros((512, 256), F32)
    for b in range(2):
        for q in range(4):
            acc = acc + nt_dot(sgq[b, q], frames[b, q])
    keep = iota((512, 256), 0) % 8 == (iota((512, 256), 1) % 128) // 16
    rows = jnp.sum(jnp.where(keep, acc, 0.0).reshape(64, 8, 256), axis=1)
    at, lane = iota((256, 128), 0), iota((256, 128), 1)
    tap = (at // 128) * 16 + at % 16
    part = jnp.zeros((16, 128), F32)
    for p in range(4):
        place = jnp.where((lane // 32 == p) & (lane % 32 == tap), 1.0, 0.0)
        part = part + dot_f32(rows[16 * p : 16 * p + 16], place)
    fg[d] = part

    def grad_copy(j, slot, dev):
        return remote(fg.at[d], fg.at[slot], f_send.at[j], f_recv.at[slot], dev, mu)

    for j in range(1, DP):
        grad_copy(j, d, other_d(j)).start()
    for j in range(1, DP):
        grad_copy(j, other_d(j), d).wait_recv()
    result = fg[0]
    for j in range(1, DP):
        result = result + fg[j]
    turned = result.T
    grad_ref[...] = jnp.concatenate([turned[32 * p : 32 * p + 32] for p in range(4)], axis=1)

    head_first().wait_send()
    for j in range(1, MIC):
        wave_copy(0, j, mu, mu).wait_send()
        wave_copy(1, j, mu, mu).wait_send()
        head_copy(j, mu, mu).wait_send()
    for k in range(8):
        sum_copy(d, 0, k, core).wait_send()
        pay_copy(d, k, core).wait_send()
    for k in range(7):
        sum_copy(d, 0, 8 + others[k] // 2, core).wait_send()
        pay_copy(d, 8 + others[k] // 2, core).wait_send()
    for j in range(1, DP):
        grad_copy(j, d, d).wait_send()


def local(waveform, filters, speech_mask, noise_mask, target, ref_mic):
    vmem = pl.BlockSpec(memory_space=pltpu.VMEM)
    dma = pltpu.SemaphoreType.DMA
    enhanced, grad = pl.pallas_call(
        body,
        out_shape=(
            jax.ShapeDtypeStruct((2, 2, 32, TD), F32),
            jax.ShapeDtypeStruct((32, 64), F32),
        ),
        in_specs=[vmem] * 5 + [pl.BlockSpec(memory_space=pltpu.SMEM)],
        out_specs=(vmem, vmem),
        scratch_shapes=[
            pltpu.VMEM((2, 64, TD), BF16),
            pltpu.VMEM((8, 128), F32),
            pltpu.VMEM((MIC, 2, 64, TD), BF16),
            pltpu.VMEM((MIC, 8, 128), F32),
            pltpu.VMEM((2, 4, 256, TD), BF16),
            pltpu.VMEM((DP, 2, 4, 32, TD), BF16),
            pltpu.VMEM((DP, 2, 256, TD), BF16),
            pltpu.VMEM((800, TD), BF16),
            pltpu.VMEM((DP, ROWS, 128), F32),
            pltpu.VMEM((DP, ROWS, 128), F32),
            pltpu.VMEM((DP, PAY, 128), F32),
            pltpu.VMEM((2, 4, 512, TD), BF16),
            pltpu.VMEM((DP, 16, 128), F32),
            pltpu.VMEM((DP, 16, TD), F32),
            pltpu.VMEM((64, TD), F32),
            pltpu.VMEM((64, TD), F32),
            pltpu.VMEM((512, 256), BF16),
            dma((2 * MIC,)), dma((2 * MIC,)), dma((MIC,)), dma((MIC,)),
            dma((DP,)), dma((DP,)), dma((DP,)), dma((DP,)), dma((DP,)), dma((DP,)),
        ],
        compiler_params=pltpu.CompilerParams(
            collective_id=0, has_side_effects=True, vmem_limit_bytes=60 * 1024 * 1024
        ),
    )(waveform, filters.T, speech_mask, noise_mask, target, ref_mic)
    return (enhanced, grad.T)


def solution(mesh):
    in_specs = (
        P(None, "mic", "dp"),
        P("mic", None),
        P(None, "mic", "dp"),
        P(None, "mic", "dp"),
        P(None, None, "mic", "dp"),
        P(),
    )
    out_specs = (P(None, None, "mic", "dp"), P("mic", None))
    return jax.shard_map(local, mesh=mesh, in_specs=in_specs, out_specs=out_specs, check_vma=False)
```

```python
import jax
import jax.numpy as jnp
from jax import lax
from jax.experimental import pallas as pl
from jax.experimental.pallas import tpu as pltpu
from jax.sharding import PartitionSpec as P

DP = 16
MIC = 8
MICS = 32
TD = 256
LOAD = 0.05
FRAME_TOTAL = 4096.0
GRAD_SCALE = 2.0 * 64.0 / (2 * 256 * FRAME_TOTAL)
F32 = jnp.float32
BF16 = jnp.bfloat16
HIGHEST = lax.Precision.HIGHEST
ROWS = 104
PAY = 72


def iota(shape, axis):
    return lax.broadcasted_iota(jnp.int32, shape, axis)


def dot_f32(a, b):
    return jnp.dot(a, b, precision=HIGHEST, preferred_element_type=F32)


def tile4(x):
    return jnp.concatenate([x, x, x, x], axis=0)


def diagonal_blocks(x):
    rows, lanes = iota((128, 128), 0), iota((128, 128), 1)
    return jnp.where(rows // 32 == lanes // 32, tile4(x), 0.0)


def fold4(x):
    return (x[0:32] + x[32:64]) + (x[64:96] + x[96:128])


def unpack_blocks(packed):
    rows, lanes = iota((128, 128), 0) % 32, iota((128, 128), 1) % 32
    blocks = diagonal_blocks(packed)
    turned = blocks.T
    real = jnp.where(rows <= lanes, blocks, turned)
    imag = jnp.where(rows > lanes, blocks, jnp.where(rows < lanes, -turned, 0.0))
    return real, imag


def unpack_four(packed):
    row, col = iota((32, 128), 0), iota((32, 128), 1) % 32
    turned = fold4(diagonal_blocks(packed).T)
    real = jnp.where(row <= col, packed, turned)
    negated = jnp.where(row > col, -packed, jnp.where(row < col, turned, 0.0))
    return real, negated


def complex_right(real, imag):
    return jnp.concatenate(
        [jnp.concatenate([real, imag], axis=1), jnp.concatenate([-imag, real], axis=1)], axis=0
    )


def inverse(a_r, a_i):
    lane = iota((32, 128), 1)
    row = iota((32, 128), 0)
    base = (lane // 32) * 32
    col = lane % 32
    for k in range(32):
        index = base + k
        c_r = jnp.take_along_axis(a_r, index, axis=1)
        c_i = jnp.take_along_axis(a_i, index, axis=1)
        scale = 1.0 / c_r[k : k + 1, :]
        here = col[0:1] == k
        r_r = jnp.where(here, 1.0, a_r[k : k + 1, :]) * scale
        r_i = jnp.where(here, 0.0, a_i[k : k + 1, :]) * scale
        at_col = col == k
        n_r = jnp.where(at_col, 0.0, a_r) - (c_r * r_r - c_i * r_i)
        n_i = jnp.where(at_col, 0.0, a_i) - (c_r * r_i + c_i * r_r)
        at_row = row == k
        a_r = jnp.where(at_row, r_r, n_r)
        a_i = jnp.where(at_row, r_i, n_i)
    return a_r, a_i


def solve(total, pick):
    lane = iota((32, 128), 1)
    row = iota((32, 128), 0)
    eye = jnp.where(row == lane % 32, 1.0, 0.0)
    inv_t = 1.0 / FRAME_TOTAL
    s_r, s_i = [fold4(x) for x in unpack_blocks(total[0:32])]
    n_r, n_i = [fold4(x) for x in unpack_blocks(total[32:64])]
    cb_r, cb_i = unpack_blocks(total[64:96])
    d_r, d_i = total[96:97], total[97:98]
    s_r = s_r * inv_t + LOAD * eye
    s_i = s_i * inv_t
    m_r, m_i = inverse(n_r * inv_t + LOAD * eye, n_i * inv_t)
    right_m = complex_right(diagonal_blocks(m_r), diagonal_blocks(m_i))
    xh = dot_f32(jnp.concatenate([s_r, s_i], axis=1), right_m)
    xh_r, xh_i = xh[:, :128], xh[:, 128:]
    at_ref = row == pick
    conj_c_r = jnp.sum(jnp.where(at_ref, xh_r, 0.0), axis=0, keepdims=True)
    conj_c_i = jnp.sum(jnp.where(at_ref, xh_i, 0.0), axis=0, keepdims=True)
    sref_r = jnp.sum(jnp.where(at_ref, s_r, 0.0), axis=0, keepdims=True)
    sref_i = jnp.sum(jnp.where(at_ref, s_i, 0.0), axis=0, keepdims=True)
    ones = jnp.where(iota((128, 128), 0) // 32 == iota((128, 128), 1) // 32, 1.0, 0.0)
    diag = jnp.sum(xh_r * eye, axis=0, keepdims=True)
    first = dot_f32(
        jnp.concatenate(
            [
                jnp.broadcast_to(diag, (8, 128)),
                m_r * sref_r + m_i * sref_i,
                m_i * sref_r - m_r * sref_i,
            ],
            axis=0,
        ),
        ones,
    )
    inv_tau = 1.0 / first[0:1]
    c_r, c_i = first[8:40], first[40:72]
    w_r = conj_c_r * inv_tau
    w_i = -conj_c_i * inv_tau
    right_c = complex_right(cb_r, -cb_i)
    row8 = jnp.broadcast_to(jnp.concatenate([w_r, w_i], axis=1), (8, 256))
    cw = dot_f32(row8, right_c)
    g_r = GRAD_SCALE * (cw[0:1, :128] - d_r)
    g_i = GRAD_SCALE * (cw[0:1, 128:] - d_i)
    gc_r, gc_i = g_r * inv_tau, g_i * inv_tau
    gw = (g_r * w_r + g_i * w_i) * inv_tau
    second = dot_f32(
        jnp.concatenate(
            [
                jnp.broadcast_to(gw, (8, 128)),
                m_r * gc_r - m_i * gc_i,
                m_r * gc_i + m_i * gc_r,
            ],
            axis=0,
        ),
        ones,
    )
    gt2 = -2.0 * second[0:1]
    u_r, u_i = second[8:40], second[40:72]
    right_xh = complex_right(diagonal_blocks(xh_r), diagonal_blocks(xh_i))
    q = dot_f32(jnp.concatenate([m_r, m_i], axis=1), right_xh)
    uh8 = jnp.broadcast_to(jnp.concatenate([gc_r, -gc_i], axis=1), (8, 256))
    uh = dot_f32(uh8, right_m)
    uh_r, uh_i = uh[0:1, :128], uh[0:1, 128:]
    col_ref = (lane % 32) == pick
    p_r = jnp.where(col_ref, u_r, 0.0) + jnp.where(at_ref, uh_r, 0.0) + gt2 * m_r
    p_i = jnp.where(col_ref, u_i, 0.0) + jnp.where(at_ref, uh_i, 0.0) + gt2 * m_i
    n_r = (u_r * conj_c_r - u_i * conj_c_i) + (c_r * uh_r - c_i * uh_i) + gt2 * q[:, :128]
    n_i = (u_r * conj_c_i + u_i * conj_c_r) + (c_r * uh_i + c_i * uh_r) + gt2 * q[:, 128:]
    upper = row <= lane % 32
    speech = jnp.where(upper, p_r, p_i) * inv_t
    noise = jnp.where(upper, n_r, n_i) * (-inv_t)
    return speech, noise, w_r, w_i


def tn_dot(a, b):
    return lax.dot_general(a, b, (((0,), (0,)), ((), ())), preferred_element_type=F32)


def block_filters(filters_t):
    lane = iota((32, 256), 1)
    spread = jnp.where(iota((32, 256), 0) == (lane // 128) * 16 + lane % 16, 1.0, 0.0)
    wide = tn_dot(filters_t, spread.astype(BF16)).astype(BF16)
    repeat = jnp.where(iota((512, 64), 0) // 8 == iota((512, 64), 1), 1.0, 0.0).astype(BF16)
    full = jnp.dot(repeat, wide, preferred_element_type=F32)
    keep = iota((512, 256), 0) % 8 == (iota((512, 256), 1) % 128) // 16
    return jnp.where(keep, full, 0.0).astype(BF16)


def split(x):
    high = x.astype(BF16).astype(F32)
    return high, x - high


def nt_dot(a, b):
    return lax.dot_general(a, b, (((1,), (1,)), ((), ())), preferred_element_type=F32)


def body(
    wave_ref, filt_ref, smask_ref, nmask_ref, target_ref, pick_ref,
    enh_ref, grad_ref,
    wblk, head, gath, heads, frames, zz, yy, lhs, sb, rb, pay, sgq, fg, tt, ms, mn, fb,
    g_send, g_recv, h_send, h_recv, s_send, s_recv, p_send, p_recv, f_send, f_recv,
):
    d = lax.axis_index("dp")
    mu = lax.axis_index("mic")
    prev = lax.rem(d + DP - 1, DP)
    nxt = lax.rem(d + 1, DP)
    at_z, at_x, at_c = d // 4, (d // 2) % 2, d % 2
    chip = d // 2
    core = 2 * chip + 1 - at_c

    def rel(dz, dx, dc):
        return ((at_z + dz) % 4) * 4 + ((at_x + dx) % 2) * 2 + (at_c + dc) % 2

    others = [rel(0, 1, 0), rel(1, 0, 0), rel(3, 0, 0), rel(1, 1, 0), rel(3, 1, 0), rel(2, 0, 0), rel(2, 1, 0)]

    def table(i, values):
        out = values[0]
        for k in range(1, len(values)):
            out = jnp.where(i == k, values[k], out)
        return out

    def other_d(j):
        return lax.rem(d + j, DP)

    def other_m(j):
        return lax.rem(mu + j, MIC)

    def remote(src, dst, send, recv, dev_d, dev_m):
        return pltpu.make_async_remote_copy(
            src_ref=src, dst_ref=dst, send_sem=send, recv_sem=recv,
            device_id={"dp": dev_d, "mic": dev_m}, device_id_type=pl.DeviceIdType.MESH,
        )

    barrier = pltpu.get_barrier_semaphore()

    def greet(dev_d, dev_m):
        pl.semaphore_signal(
            barrier, inc=1, device_id={"dp": dev_d, "mic": dev_m},
            device_id_type=pl.DeviceIdType.MESH,
        )

    for j in range(1, MIC):
        greet(d, other_m(j))
    for peer in others + [core, prev, nxt]:
        greet(peer, mu)

    turn = iota((128, 1024), 0)
    lane = iota((128, 1024), 1)
    choose = (turn % 4 == lane // TD) & (turn // 4 == (lane % TD) // 8)
    choose = jnp.where(choose, 1.0, 0.0).astype(BF16)
    phase = iota((16, 1024), 1) % 8
    for b in range(2):
        rows = wave_ref[b].astype(F32)
        head[4 * b : 4 * b + 4, :] = rows[:, 0:128]
        stacked = jnp.concatenate([rows[:, 128 * r : 128 * r + 128] for r in range(32)], axis=0)
        spread = jnp.dot(stacked.T.astype(BF16), choose, preferred_element_type=F32)
        taps = spread[0:16]
        for k in range(1, 8):
            taps = jnp.where(phase == k, spread[16 * k : 16 * k + 16], taps)
        for m in range(4):
            wblk[b, 16 * m : 16 * m + 16, :] = taps[:, TD * m : TD * m + TD].astype(BF16)

    fb[...] = block_filters(filt_ref[...])
    ms[...] = smask_ref[...].reshape(64, TD).astype(F32)
    mn[...] = nmask_ref[...].reshape(64, TD).astype(F32)
    for o in range(DP):
        for v in range(2):
            tt[o, 8 * v : 8 * v + 4, :] = target_ref[o // 8, v, (o % 8) * 4 : (o % 8) * 4 + 4, :]
            tt[o, 8 * v + 4 : 8 * v + 8, :] = jnp.zeros((4, TD), F32)

    pl.semaphore_wait(barrier, MIC + DP // 2 + 1)

    def wave_copy(b, j, slot, dev):
        return remote(wblk.at[b], gath.at[slot, b], g_send.at[MIC * b + j], g_recv.at[MIC * b + slot], d, dev)

    def head_copy(j, slot, dev):
        return remote(heads.at[mu], heads.at[slot], h_send.at[j], h_recv.at[slot], d, dev)

    def head_first():
        return remote(head, heads.at[mu], h_send.at[0], h_recv.at[mu], prev, mu)

    head_first().start()
    for j in range(1, MIC):
        wave_copy(0, j, mu, other_m(j)).start()
    gath[mu] = wblk[...]
    head_first().wait_recv()
    for j in range(1, MIC):
        head_copy(j, mu, other_m(j)).start()
    for j in range(1, MIC):
        wave_copy(1, j, mu, other_m(j)).start()

    last = d == DP - 1
    tap128 = iota((128, 128), 1) == iota((128, 128), 0) % 16
    end = iota((128, TD), 1) == TD - 1

    def encode(b):
        for q in range(4):
            x = jnp.concatenate([gath[2 * q, b], gath[2 * q + 1, b]], axis=0).astype(F32)
            near = jnp.concatenate(
                [
                    jnp.broadcast_to(heads[2 * q + p, 4 * b + m : 4 * b + m + 1, :], (16, 128))
                    for p in range(2)
                    for m in range(4)
                ],
                axis=0,
            )
            near = jnp.where(last, 0.0, near)
            column = jnp.sum(jnp.where(tap128, near, 0.0), axis=1, keepdims=True)
            moved = jnp.where(end, column, pltpu.roll(x, TD - 1, axis=1))
            piece = slice(TD * (4 * b + q), TD * (4 * b + q) + TD)
            frames[0:128, piece] = x.astype(BF16)
            frames[128:256, piece] = moved.astype(BF16)
        for half in range(2):
            at = TD * (4 * b + 2 * half)
            a0 = jnp.dot(fb[...], frames[:, at : at + TD], preferred_element_type=F32)
            a1 = jnp.dot(fb[...], frames[:, at + TD : at + 2 * TD], preferred_element_type=F32)
            z = jnp.concatenate(
                [a0.reshape(8, 4, 2, 8, TD), a1.reshape(8, 4, 2, 8, TD)], axis=3
            ).astype(BF16)
            for v in range(2):
                zz[8 * b : 8 * b + 8, v, :, 16 * half : 16 * half + 16, :] = z[:, :, v]

    lane32 = iota((32, 128), 1)
    upper = iota((32, 128), 0) <= lane32 % 32
    row8 = iota((8, 128), 0)
    own8 = row8 == iota((8, 128), 1) // 32

    def group_sums(o, w):
        t_hi, t_lo = split(tt[o])
        lhs[w, 512:768, :] = zz[o].reshape(256, TD)
        lhs[w, 768:800, :] = jnp.concatenate([t_hi, t_lo], axis=0).astype(BF16)
        for g in range(4):
            for k, ref in enumerate((ms, mn)):
                mask = jnp.broadcast_to(ref[pl.ds(4 * o + g, 1), :], (32, TD)).astype(BF16)
                for v in range(2):
                    part = zz[o, v, g] * mask
                    at = 128 * v + 32 * g
                    lhs[w, 256 * k + at : 256 * k + at + 32, :] = part
                    row = 64 * k + 32 * ((v + g) % 2)
                    yy[o, g, row : row + 32, :] = part
        out = nt_dot(lhs[w], zz[o].reshape(256, TD))
        for kind in range(3):
            value = jnp.zeros((32, 128), F32)
            for g in range(4):
                re = out[256 * kind + 32 * g : 256 * kind + 32 * g + 32]
                im = out[256 * kind + 128 + 32 * g : 256 * kind + 160 + 32 * g]
                one = jnp.where(upper, re[:, :128] + im[:, 128:], im[:, :128] - re[:, 128:])
                value = jnp.where(lane32 // 32 == g, one, value)
            sb[o, 32 * kind : 32 * kind + 32, :] = value
        t0 = out[768:776] + out[784:792]
        t1 = out[776:784] + out[792:800]
        d_r = jnp.sum(jnp.where(own8, t0[:, :128] + t1[:, 128:], 0.0), axis=0, keepdims=True)
        d_i = jnp.sum(jnp.where(own8, t0[:, 128:] - t1[:, :128], 0.0), axis=0, keepdims=True)
        sb[o, 96:104, :] = jnp.where(row8 == 0, d_r, jnp.where(row8 == 1, d_i, 0.0))

    def sum_copy(o, slot, sem, dev):
        return remote(sb.at[o], rb.at[slot], s_send.at[sem], s_recv.at[slot], dev, mu)

    def add_slot(o, slot):
        sum_copy(o, slot, slot, core).wait_recv()
        sb[o] = sb[o] + rb[slot]

    for b in range(2):
        for j in range(1, MIC):
            wave_copy(b, j, other_m(j), mu).wait_recv()
        if b == 0:
            for j in range(1, MIC):
                head_copy(j, other_m(j), mu).wait_recv()
        encode(b)
        here = jnp.where(at_z // 2 == b, 1, 0)

        def target(k, mine):
            to = 2 * (2 * b + (at_z + k // 2 + here) % 2) + (at_x + 1 + k) % 2
            return to, 2 * to + (at_c + 1 + mine) % 2

        def give(to, o):
            sum_copy(o, to, to, core).start()

        def keep(to, o):
            add_slot(o, to)

            @pl.when(to != chip)
            def _():
                sum_copy(o, 8 + chip, 8 + to, o).start()

        @pl.loop(0, 4)
        def _(i):
            to_a, o_a = target(table(i, [0, 2, 3, 2]), table(i, [0, 0, 0, 1]))
            to_b, o_b = target(table(i, [1, 0, 1, 3]), table(i, [0, 1, 1, 1]))
            group_sums(o_a, 0)
            group_sums(o_b, 1)

            @pl.when(i < 3)
            def _():
                give(to_a, o_a)

            @pl.when(i == 3)
            def _():
                keep(to_a, o_a)

            @pl.when(i == 0)
            def _():
                give(to_b, o_b)

            @pl.when(i > 0)
            def _():
                keep(to_b, o_b)

    for k in range(7):
        add_slot(d, 8 + others[k] // 2)
    pick = jnp.where(d < DP // 2, pick_ref[0], pick_ref[1])
    speech, noise, w_r, w_i = solve(sb[d], pick)
    left_half = lane32 < 64
    pay[d, 0:32, :] = jnp.where(left_half, speech, pltpu.roll(noise, 64, axis=1))
    pay[d, 32:64, :] = jnp.where(left_half, pltpu.roll(speech, 64, axis=1), noise)
    pay[d, 64:72, :] = jnp.where(row8 == 0, w_r, jnp.where(row8 == 1, w_i, 0.0))

    def pay_copy(o, sem, dev):
        return remote(pay.at[o], pay.at[o], p_send.at[sem], p_recv.at[o], dev, mu)

    for k, dev in enumerate([core] + others):
        pay_copy(d, k, dev).start()

    def group_grads(o):
        b = o // 8
        f0 = (o % 8) * 4
        w_r = jnp.where(own8, pay[o, 64:65, :], 0.0)
        w_i = jnp.where(own8, pay[o, 65:66, :], 0.0)
        wr_hi, wr_lo = split(w_r)
        wi_hi, wi_lo = split(w_i)

        def wide(p, q):
            return jnp.concatenate([p, q], axis=1)

        first = jnp.concatenate([wide(wr_hi, wi_hi), wide(-wi_hi, wr_hi)], axis=0)
        second = jnp.concatenate([wide(wr_lo, wi_lo), wide(-wi_lo, wr_lo)], axis=0)
        left = jnp.concatenate([first, second], axis=0)
        both = jnp.dot(left.astype(BF16), zz[o].reshape(256, TD), preferred_element_type=F32)
        enh = both[0:16] + both[16:32]
        for g in range(4):
            enh_ref[b, 0, pl.ds(f0 + g, 1), :] = enh[g : g + 1, :]
            enh_ref[b, 1, pl.ds(f0 + g, 1), :] = enh[8 + g : 9 + g, :]
        e_hi, e_lo = split(GRAD_SCALE * (enh - tt[o]))
        e_rows = jnp.concatenate([e_hi, e_hi, e_lo], axis=0).astype(BF16)
        w_cols = jnp.concatenate([first, second, first], axis=0).T
        even = (lane32 // 32) % 2 == 0
        for g in range(4):
            if g % 2 == 0:
                re, neg = unpack_four(pay[o, 16 * g : 16 * g + 32, :])
            shift = 32 if g % 2 == 0 else 96
            own = even if g % 2 == 0 else ~even
            top = jnp.where(own, re, pltpu.roll(neg, shift, axis=1))
            bottom = jnp.where(own, -neg, pltpu.roll(re, shift, axis=1))
            hi, lo = split(jnp.concatenate([top, bottom], axis=0))
            cols = jnp.concatenate(
                [w_cols[32 * g : 32 * g + 32], w_cols[128 + 32 * g : 160 + 32 * g]], axis=0
            )
            lhs_g = jnp.concatenate([wide(hi, cols), wide(lo, jnp.zeros_like(cols))], axis=0)
            rhs_g = jnp.concatenate([yy[o, g], e_rows], axis=0)
            both = jnp.dot(lhs_g.astype(BF16), rhs_g, preferred_element_type=F32)
            sg = both[0:64] + both[64:128]
            place = pl.ds(pl.multiple_of(16 * (f0 + g), 16), 16)
            for q in range(4):
                sgq[place, pl.ds(pl.multiple_of(TD * (4 * b + q), TD), TD)] = jnp.concatenate(
                    [sg[8 * q : 8 * q + 8], sg[32 + 8 * q : 40 + 8 * q]], axis=0
                ).astype(BF16)

    spread = [
        [(0, 0, 0), (0, 1, 0), (3, 0, 0), (1, 1, 0), (1, 0, 1), (2, 0, 0), (1, 1, 1), (2, 0, 1)],
        [(0, 0, 1), (1, 0, 0), (0, 1, 1), (3, 1, 0), (3, 0, 1), (2, 1, 0), (3, 1, 1), (2, 1, 1)],
    ]

    @pl.loop(0, DP // 2)
    def _(i):
        pair = []
        for column in spread:
            dz = table(i, [k[0] for k in column])
            dx = table(i, [k[1] for k in column])
            dc = table(i, [k[2] for k in column])
            pair.append((rel(dz, dx, dc), dc))
        for o, dc in pair:

            @pl.when(o != d)
            def _():
                pay_copy(o, 0, core).wait_recv()

            @pl.when((o != d) & (dc == 0))
            def _():
                pay_copy(o, 8 + o // 2, core).start()

        for o, dc in pair:
            group_grads(o)

    acc = nt_dot(sgq[...], frames[...])
    keep = iota((512, 256), 0) % 8 == (iota((512, 256), 1) % 128) // 16
    rows = jnp.sum(jnp.where(keep, acc, 0.0).reshape(64, 8, 256), axis=1)
    lane16 = iota((16, 128), 1)
    halves = []
    for half in (rows[:, :128], rows[:, 128:]):
        for step in (64, 32, 16):
            half = half + pltpu.roll(half, step, axis=1)
        halves.append(half)
    part = jnp.zeros((16, 128), F32)
    for p in range(4):
        at = slice(16 * p, 16 * p + 16)
        one = jnp.where((lane16 // 16) % 2 == 0, halves[0][at], halves[1][at])
        part = jnp.where(lane16 // 32 == p, one, part)
    fg[d] = part

    def grad_copy(j, slot, dev):
        return remote(fg.at[d], fg.at[slot], f_send.at[j], f_recv.at[slot], dev, mu)

    for j in range(1, DP):
        grad_copy(j, d, other_d(j)).start()
    for j in range(1, DP):
        grad_copy(j, other_d(j), d).wait_recv()
    result = fg[0]
    for j in range(1, DP):
        result = result + fg[j]
    turned = result.T
    grad_ref[...] = jnp.concatenate([turned[32 * p : 32 * p + 32] for p in range(4)], axis=1)

    head_first().wait_send()
    for j in range(1, MIC):
        wave_copy(0, j, mu, mu).wait_send()
        wave_copy(1, j, mu, mu).wait_send()
        head_copy(j, mu, mu).wait_send()
    for k in range(8):
        sum_copy(d, 0, k, core).wait_send()
        pay_copy(d, k, core).wait_send()
    for k in range(7):
        sum_copy(d, 0, 8 + others[k] // 2, core).wait_send()
        pay_copy(d, 8 + others[k] // 2, core).wait_send()
    for j in range(1, DP):
        grad_copy(j, d, d).wait_send()


def local(waveform, filters, speech_mask, noise_mask, target, ref_mic):
    vmem = pl.BlockSpec(memory_space=pltpu.VMEM)
    dma = pltpu.SemaphoreType.DMA
    enhanced, grad = pl.pallas_call(
        body,
        out_shape=(
            jax.ShapeDtypeStruct((2, 2, 32, TD), F32),
            jax.ShapeDtypeStruct((32, 64), F32),
        ),
        in_specs=[vmem] * 5 + [pl.BlockSpec(memory_space=pltpu.SMEM)],
        out_specs=(vmem, vmem),
        scratch_shapes=[
            pltpu.VMEM((2, 64, TD), BF16),
            pltpu.VMEM((8, 128), F32),
            pltpu.VMEM((MIC, 2, 64, TD), BF16),
            pltpu.VMEM((MIC, 8, 128), F32),
            pltpu.VMEM((256, 8 * TD), BF16),
            pltpu.VMEM((DP, 2, 4, 32, TD), BF16),
            pltpu.VMEM((DP, 4, 128, TD), BF16),
            pltpu.VMEM((2, 800, TD), BF16),
            pltpu.VMEM((DP, ROWS, 128), F32),
            pltpu.VMEM((DP, ROWS, 128), F32),
            pltpu.VMEM((DP, PAY, 128), F32),
            pltpu.VMEM((512, 8 * TD), BF16),
            pltpu.VMEM((DP, 16, 128), F32),
            pltpu.VMEM((DP, 16, TD), F32),
            pltpu.VMEM((64, TD), F32),
            pltpu.VMEM((64, TD), F32),
            pltpu.VMEM((512, 256), BF16),
            dma((2 * MIC,)), dma((2 * MIC,)), dma((MIC,)), dma((MIC,)),
            dma((DP,)), dma((DP,)), dma((DP,)), dma((DP,)), dma((DP,)), dma((DP,)),
        ],
        compiler_params=pltpu.CompilerParams(
            collective_id=0, has_side_effects=True, vmem_limit_bytes=60 * 1024 * 1024
        ),
    )(waveform, filters.T, speech_mask, noise_mask, target, ref_mic)
    return (enhanced, grad.T)


def solution(mesh):
    in_specs = (
        P(None, "mic", "dp"),
        P("mic", None),
        P(None, "mic", "dp"),
        P(None, "mic", "dp"),
        P(None, None, "mic", "dp"),
        P(),
    )
    out_specs = (P(None, None, "mic", "dp"), P("mic", None))
    return jax.shard_map(local, mesh=mesh, in_specs=in_specs, out_specs=out_specs, check_vma=False)
```

```python
import jax
import jax.numpy as jnp
from jax import lax
from jax.experimental import pallas as pl
from jax.experimental.pallas import tpu as pltpu
from jax.sharding import PartitionSpec as P

DP = 16
MIC = 8
MICS = 32
TD = 256
LOAD = 0.05
FRAME_TOTAL = 4096.0
GRAD_SCALE = 2.0 * 64.0 / (2 * 256 * FRAME_TOTAL)
F32 = jnp.float32
BF16 = jnp.bfloat16
ROWS = 104
PAY = 72


def iota(shape, axis):
    return lax.broadcasted_iota(jnp.int32, shape, axis)


def tile4(x):
    return jnp.concatenate([x, x, x, x], axis=0)


def diagonal_blocks(x):
    rows, lanes = iota((128, 128), 0), iota((128, 128), 1)
    return jnp.where(rows // 32 == lanes // 32, tile4(x), 0.0)


def fold4(x):
    return (x[0:32] + x[32:64]) + (x[64:96] + x[96:128])


def unpack_four(packed):
    row, col = iota((32, 128), 0), iota((32, 128), 1) % 32
    turned = fold4(diagonal_blocks(packed).T)
    real = jnp.where(row <= col, packed, turned)
    negated = jnp.where(row > col, -packed, jnp.where(row < col, turned, 0.0))
    return real, negated


def inverse(a_r, a_i):
    lane = iota((32, 128), 1)
    row = iota((32, 128), 0)
    base = (lane // 32) * 32
    col = lane % 32
    for k in range(32):
        index = base + k
        c_r = jnp.take_along_axis(a_r, index, axis=1)
        c_i = jnp.take_along_axis(a_i, index, axis=1)
        scale = 1.0 / c_r[k : k + 1, :]
        here = col[0:1] == k
        r_r = jnp.where(here, 1.0, a_r[k : k + 1, :]) * scale
        r_i = jnp.where(here, 0.0, a_i[k : k + 1, :]) * scale
        at_col = col == k
        n_r = jnp.where(at_col, 0.0, a_r) - (c_r * r_r - c_i * r_i)
        n_i = jnp.where(at_col, 0.0, a_i) - (c_r * r_i + c_i * r_r)
        at_row = row == k
        a_r = jnp.where(at_row, r_r, n_r)
        a_i = jnp.where(at_row, r_i, n_i)
    return a_r, a_i


def thirds(x):
    one = x.astype(BF16).astype(F32)
    two = (x - one).astype(BF16).astype(F32)
    return one, two, x - one - two


def complex_blocks(real, imag):
    keep = iota((128, 128), 0) // 32 == iota((128, 128), 1) // 32
    r = jnp.where(keep, tile4(real), 0.0).astype(BF16)
    i = jnp.where(keep, tile4(imag), 0.0).astype(BF16)
    return jnp.concatenate(
        [jnp.concatenate([r, i], axis=1), jnp.concatenate([-i, r], axis=1)], axis=0
    )


def times(a_r, a_i, b_r, b_i):
    a = thirds(jnp.concatenate([a_r, a_i], axis=1))
    reals, imags = thirds(b_r), thirds(b_i)
    out = None
    for k in range(2, -1, -1):
        rows = jnp.concatenate(a[: 3 - k], axis=0).astype(BF16)
        part = jnp.dot(rows, complex_blocks(reals[k], imags[k]), preferred_element_type=F32)
        for m in range(2 - k, -1, -1):
            one = part[32 * m : 32 * m + 32]
            out = one if out is None else out + one
    return out[:, :128], out[:, 128:]


def group_totals(x):
    ones = jnp.where(iota((128, 128), 0) // 32 == iota((128, 128), 1) // 32, 1.0, 0.0).astype(BF16)
    n = x.shape[0]
    rows = jnp.concatenate(thirds(x), axis=0).astype(BF16)
    out = jnp.dot(rows, ones, preferred_element_type=F32)
    return out[0:n] + (out[n : 2 * n] + out[2 * n :])


def solve(total, pick):
    lane = iota((32, 128), 1)
    row = iota((32, 128), 0)
    eye = row == lane % 32
    inv_t = 1.0 / FRAME_TOTAL

    def column_sum(x):
        return jnp.sum(x, axis=0, keepdims=True)

    s_r, s_neg = unpack_four(total[0:32])
    n_r, n_neg = unpack_four(total[32:64])
    k_r, k_neg = unpack_four(total[64:96])
    d_r, d_i = total[96:97], total[97:98]
    s_r = s_r * inv_t + jnp.where(eye, LOAD, 0.0)
    s_i = s_neg * -inv_t
    m_r, m_i = inverse(n_r * inv_t + jnp.where(eye, LOAD, 0.0), n_neg * -inv_t)
    xh_r, xh_i = times(s_r, s_i, m_r, m_i)
    q_r, q_i = times(m_r, m_i, xh_r, xh_i)
    at_ref = row == pick
    conj_c_r = column_sum(jnp.where(at_ref, xh_r, 0.0))
    conj_c_i = column_sum(jnp.where(at_ref, xh_i, 0.0))
    sref_r = column_sum(jnp.where(at_ref, s_r, 0.0))
    sref_i = column_sum(jnp.where(at_ref, s_i, 0.0))
    diag = column_sum(jnp.where(eye, xh_r, 0.0))
    first = group_totals(
        jnp.concatenate(
            [
                jnp.broadcast_to(diag, (8, 128)),
                m_r * sref_r + m_i * sref_i,
                m_i * sref_r - m_r * sref_i,
            ],
            axis=0,
        )
    )
    inv_tau = 1.0 / first[0:1]
    c_r, c_i = first[8:40], first[40:72]
    w_r = conj_c_r * inv_tau
    w_i = -conj_c_i * inv_tau
    h_r, h_i = c_r * inv_tau, c_i * inv_tau
    g_r = GRAD_SCALE * (column_sum(h_r * k_r - h_i * k_neg) - d_r)
    g_i = GRAD_SCALE * (column_sum(h_i * k_r + h_r * k_neg) - d_i)
    gc_r, gc_i = g_r * inv_tau, g_i * inv_tau
    gw = (g_r * w_r + g_i * w_i) * inv_tau
    second = group_totals(
        jnp.concatenate(
            [
                jnp.broadcast_to(gw, (8, 128)),
                m_r * gc_r - m_i * gc_i,
                m_r * gc_i + m_i * gc_r,
            ],
            axis=0,
        )
    )
    gt2 = -2.0 * second[0:1]
    u_r, u_i = second[8:40], second[40:72]
    uh_r = column_sum(jnp.where(eye, u_r, 0.0))
    uh_i = -column_sum(jnp.where(eye, u_i, 0.0))
    col_ref = (lane % 32) == pick
    p_r = jnp.where(col_ref, u_r, 0.0) + jnp.where(at_ref, uh_r, 0.0) + gt2 * m_r
    p_i = jnp.where(col_ref, u_i, 0.0) + jnp.where(at_ref, uh_i, 0.0) + gt2 * m_i
    n_r = (u_r * conj_c_r - u_i * conj_c_i) + (c_r * uh_r - c_i * uh_i) + gt2 * q_r
    n_i = (u_r * conj_c_i + u_i * conj_c_r) + (c_r * uh_i + c_i * uh_r) + gt2 * q_i
    upper = row <= lane % 32
    speech = jnp.where(upper, p_r, p_i) * inv_t
    noise = jnp.where(upper, n_r, n_i) * (-inv_t)
    return speech, noise, w_r, w_i


def tn_dot(a, b):
    return lax.dot_general(a, b, (((0,), (0,)), ((), ())), preferred_element_type=F32)


def block_filters(filters_t):
    lane = iota((32, 256), 1)
    spread = jnp.where(iota((32, 256), 0) == (lane // 128) * 16 + lane % 16, 1.0, 0.0)
    wide = tn_dot(filters_t, spread.astype(BF16)).astype(BF16)
    repeat = jnp.where(iota((512, 64), 0) // 8 == iota((512, 64), 1), 1.0, 0.0).astype(BF16)
    full = jnp.dot(repeat, wide, preferred_element_type=F32)
    keep = iota((512, 256), 0) % 8 == (iota((512, 256), 1) % 128) // 16
    return jnp.where(keep, full, 0.0).astype(BF16)


def split(x):
    high = x.astype(BF16).astype(F32)
    return high, x - high


def nt_dot(a, b):
    return lax.dot_general(a, b, (((1,), (1,)), ((), ())), preferred_element_type=F32)


def body(
    wave_in, filt_in, smask_in, nmask_in, target_in, pick_ref,
    enh_out, grad_ref,
    wave_ref, filt_ref, smask_ref, nmask_ref, target_ref, enh_ref, in_sem,
    wblk, head, gath, heads, frames, zz, yy, lhs, sb, rb, pay, sgq, fg, tt, ms, mn, fb,
    g_send, g_recv, h_send, h_recv, s_send, s_recv, p_send, p_recv, f_send, f_recv,
):
    d = lax.axis_index("dp")
    mu = lax.axis_index("mic")
    prev = lax.rem(d + DP - 1, DP)
    nxt = lax.rem(d + 1, DP)
    at_z, at_x, at_c = d // 4, (d // 2) % 2, d % 2
    chip = d // 2
    core = 2 * chip + 1 - at_c

    def rel(dz, dx, dc):
        return ((at_z + dz) % 4) * 4 + ((at_x + dx) % 2) * 2 + (at_c + dc) % 2

    others = [rel(0, 1, 0), rel(1, 0, 0), rel(3, 0, 0), rel(1, 1, 0), rel(3, 1, 0), rel(2, 0, 0), rel(2, 1, 0)]

    def table(i, values):
        out = values[0]
        for k in range(1, len(values)):
            out = jnp.where(i == k, values[k], out)
        return out

    def other_d(j):
        return lax.rem(d + j, DP)

    def other_m(j):
        return lax.rem(mu + j, MIC)

    def remote(src, dst, send, recv, dev_d, dev_m):
        return pltpu.make_async_remote_copy(
            src_ref=src, dst_ref=dst, send_sem=send, recv_sem=recv,
            device_id={"dp": dev_d, "mic": dev_m}, device_id_type=pl.DeviceIdType.MESH,
        )

    loads = [
        pltpu.make_async_copy(src, dst, in_sem.at[k])
        for k, (src, dst) in enumerate(
            [
                (wave_in, wave_ref), (filt_in, filt_ref), (smask_in, smask_ref),
                (nmask_in, nmask_ref), (target_in, target_ref),
            ]
        )
    ]
    for load in loads:
        load.start()

    barrier = pltpu.get_barrier_semaphore()

    def greet(dev_d, dev_m):
        pl.semaphore_signal(
            barrier, inc=1, device_id={"dp": dev_d, "mic": dev_m},
            device_id_type=pl.DeviceIdType.MESH,
        )

    for j in range(1, MIC):
        greet(d, other_m(j))
    for peer in others + [core, prev, nxt]:
        greet(peer, mu)

    for load in loads:
        load.wait()

    turn = iota((128, 1024), 0)
    lane = iota((128, 1024), 1)
    choose = (turn % 4 == lane // TD) & (turn // 4 == (lane % TD) // 8)
    choose = jnp.where(choose, 1.0, 0.0).astype(BF16)
    phase = iota((16, 1024), 1) % 8
    for b in range(2):
        rows = wave_ref[b].astype(F32)
        head[4 * b : 4 * b + 4, :] = rows[:, 0:128]
        stacked = jnp.concatenate([rows[:, 128 * r : 128 * r + 128] for r in range(32)], axis=0)
        spread = jnp.dot(stacked.T.astype(BF16), choose, preferred_element_type=F32)
        taps = spread[0:16]
        for k in range(1, 8):
            taps = jnp.where(phase == k, spread[16 * k : 16 * k + 16], taps)
        for m in range(4):
            wblk[b, 16 * m : 16 * m + 16, :] = taps[:, TD * m : TD * m + TD].astype(BF16)

    fb[...] = block_filters(filt_ref[...])
    ms[...] = smask_ref[...].reshape(64, TD).astype(F32)
    mn[...] = nmask_ref[...].reshape(64, TD).astype(F32)
    for o in range(DP):
        for v in range(2):
            tt[o, 8 * v : 8 * v + 4, :] = target_ref[o // 8, v, (o % 8) * 4 : (o % 8) * 4 + 4, :]
            tt[o, 8 * v + 4 : 8 * v + 8, :] = jnp.zeros((4, TD), F32)

    pl.semaphore_wait(barrier, MIC + DP // 2 + 1)

    def wave_copy(b, j, slot, dev):
        return remote(wblk.at[b], gath.at[slot, b], g_send.at[MIC * b + j], g_recv.at[MIC * b + slot], d, dev)

    def head_copy(j, slot, dev):
        return remote(heads.at[mu], heads.at[slot], h_send.at[j], h_recv.at[slot], d, dev)

    def head_first():
        return remote(head, heads.at[mu], h_send.at[0], h_recv.at[mu], prev, mu)

    head_first().start()
    for j in range(1, MIC):
        wave_copy(0, j, mu, other_m(j)).start()
    gath[mu] = wblk[...]
    head_first().wait_recv()
    for j in range(1, MIC):
        head_copy(j, mu, other_m(j)).start()
    for j in range(1, MIC):
        wave_copy(1, j, mu, other_m(j)).start()

    last = d == DP - 1
    tap128 = iota((128, 128), 1) == iota((128, 128), 0) % 16
    end = iota((128, TD), 1) == TD - 1

    def encode(b):
        for q in range(4):
            x = jnp.concatenate([gath[2 * q, b], gath[2 * q + 1, b]], axis=0).astype(F32)
            near = jnp.concatenate(
                [
                    jnp.broadcast_to(heads[2 * q + p, 4 * b + m : 4 * b + m + 1, :], (16, 128))
                    for p in range(2)
                    for m in range(4)
                ],
                axis=0,
            )
            near = jnp.where(last, 0.0, near)
            column = jnp.sum(jnp.where(tap128, near, 0.0), axis=1, keepdims=True)
            moved = jnp.where(end, column, pltpu.roll(x, TD - 1, axis=1))
            piece = slice(TD * (4 * b + q), TD * (4 * b + q) + TD)
            frames[0:128, piece] = x.astype(BF16)
            frames[128:256, piece] = moved.astype(BF16)
        for half in range(2):
            at = TD * (4 * b + 2 * half)
            a0 = jnp.dot(fb[...], frames[:, at : at + TD], preferred_element_type=F32)
            a1 = jnp.dot(fb[...], frames[:, at + TD : at + 2 * TD], preferred_element_type=F32)
            z = jnp.concatenate(
                [a0.reshape(8, 4, 2, 8, TD), a1.reshape(8, 4, 2, 8, TD)], axis=3
            ).astype(BF16)
            for v in range(2):
                zz[8 * b : 8 * b + 8, v, :, 16 * half : 16 * half + 16, :] = z[:, :, v]

    lane32 = iota((32, 128), 1)
    upper = iota((32, 128), 0) <= lane32 % 32
    row8 = iota((8, 128), 0)
    own8 = row8 == iota((8, 128), 1) // 32

    def group_sums(o, w):
        t_hi, t_lo = split(tt[o])
        lhs[w, 512:768, :] = zz[o].reshape(256, TD)
        lhs[w, 768:800, :] = jnp.concatenate([t_hi, t_lo], axis=0).astype(BF16)
        for g in range(4):
            for k, ref in enumerate((ms, mn)):
                mask = jnp.broadcast_to(ref[pl.ds(4 * o + g, 1), :], (32, TD)).astype(BF16)
                for v in range(2):
                    part = zz[o, v, g] * mask
                    at = 128 * v + 32 * g
                    lhs[w, 256 * k + at : 256 * k + at + 32, :] = part
                    row = 64 * k + 32 * ((v + g) % 2)
                    yy[o, g, row : row + 32, :] = part
        out = nt_dot(lhs[w], zz[o].reshape(256, TD))
        for kind in range(3):
            value = jnp.zeros((32, 128), F32)
            for g in range(4):
                re = out[256 * kind + 32 * g : 256 * kind + 32 * g + 32]
                im = out[256 * kind + 128 + 32 * g : 256 * kind + 160 + 32 * g]
                one = jnp.where(upper, re[:, :128] + im[:, 128:], im[:, :128] - re[:, 128:])
                value = jnp.where(lane32 // 32 == g, one, value)
            sb[o, 32 * kind : 32 * kind + 32, :] = value
        t0 = out[768:776] + out[784:792]
        t1 = out[776:784] + out[792:800]
        d_r = jnp.sum(jnp.where(own8, t0[:, :128] + t1[:, 128:], 0.0), axis=0, keepdims=True)
        d_i = jnp.sum(jnp.where(own8, t0[:, 128:] - t1[:, :128], 0.0), axis=0, keepdims=True)
        sb[o, 96:104, :] = jnp.where(row8 == 0, d_r, jnp.where(row8 == 1, d_i, 0.0))

    def sum_copy(o, slot, sem, dev):
        return remote(sb.at[o], rb.at[slot], s_send.at[sem], s_recv.at[slot], dev, mu)

    def add_slot(o, slot):
        sum_copy(o, slot, slot, core).wait_recv()
        sb[o] = sb[o] + rb[slot]

    for b in range(2):
        for j in range(1, MIC):
            wave_copy(b, j, other_m(j), mu).wait_recv()
        if b == 0:
            for j in range(1, MIC):
                head_copy(j, other_m(j), mu).wait_recv()
        encode(b)
        here = jnp.where(at_z // 2 == b, 1, 0)

        def target(k, mine):
            to = 2 * (2 * b + (at_z + k // 2 + here) % 2) + (at_x + 1 + k) % 2
            return to, 2 * to + (at_c + 1 + mine) % 2

        def give(to, o):
            sum_copy(o, to, to, core).start()

        def keep(to, o):
            add_slot(o, to)

            @pl.when(to != chip)
            def _():
                sum_copy(o, 8 + chip, 8 + to, o).start()

        @pl.loop(0, 4)
        def _(i):
            to_a, o_a = target(table(i, [0, 2, 3, 2]), table(i, [0, 0, 0, 1]))
            to_b, o_b = target(table(i, [1, 0, 1, 3]), table(i, [0, 1, 1, 1]))
            group_sums(o_a, 0)
            group_sums(o_b, 1)

            @pl.when(i < 3)
            def _():
                give(to_a, o_a)

            @pl.when(i == 3)
            def _():
                keep(to_a, o_a)

            @pl.when(i == 0)
            def _():
                give(to_b, o_b)

            @pl.when(i > 0)
            def _():
                keep(to_b, o_b)

    for k in range(7):
        add_slot(d, 8 + others[k] // 2)
    pick = jnp.where(d < DP // 2, pick_ref[0], pick_ref[1])
    speech, noise, w_r, w_i = solve(sb[d], pick)
    left_half = lane32 < 64
    pay[d, 0:32, :] = jnp.where(left_half, speech, pltpu.roll(noise, 64, axis=1))
    pay[d, 32:64, :] = jnp.where(left_half, pltpu.roll(speech, 64, axis=1), noise)
    pay[d, 64:72, :] = jnp.where(row8 == 0, w_r, jnp.where(row8 == 1, w_i, 0.0))

    def pay_copy(o, sem, dev):
        return remote(pay.at[o], pay.at[o], p_send.at[sem], p_recv.at[o], dev, mu)

    for k, dev in enumerate([core, others[0]] + others[:0:-1]):
        pay_copy(d, k, dev).start()

    def group_grads(o):
        b = o // 8
        f0 = (o % 8) * 4
        w_r = jnp.where(own8, pay[o, 64:65, :], 0.0)
        w_i = jnp.where(own8, pay[o, 65:66, :], 0.0)
        wr_hi, wr_lo = split(w_r)
        wi_hi, wi_lo = split(w_i)

        def wide(p, q):
            return jnp.concatenate([p, q], axis=1)

        first = jnp.concatenate([wide(wr_hi, wi_hi), wide(-wi_hi, wr_hi)], axis=0)
        second = jnp.concatenate([wide(wr_lo, wi_lo), wide(-wi_lo, wr_lo)], axis=0)
        left = jnp.concatenate([first, second], axis=0)
        both = jnp.dot(left.astype(BF16), zz[o].reshape(256, TD), preferred_element_type=F32)
        enh = both[0:16] + both[16:32]
        for g in range(4):
            enh_ref[b, 0, pl.ds(f0 + g, 1), :] = enh[g : g + 1, :]
            enh_ref[b, 1, pl.ds(f0 + g, 1), :] = enh[8 + g : 9 + g, :]
        e_hi, e_lo = split(GRAD_SCALE * (enh - tt[o]))
        e_rows = jnp.concatenate([e_hi, e_hi, e_lo], axis=0).astype(BF16)
        w_cols = jnp.concatenate([first, second, first], axis=0).T
        even = (lane32 // 32) % 2 == 0
        for g in range(4):
            if g % 2 == 0:
                re, neg = unpack_four(pay[o, 16 * g : 16 * g + 32, :])
            shift = 32 if g % 2 == 0 else 96
            own = even if g % 2 == 0 else ~even
            top = jnp.where(own, re, pltpu.roll(neg, shift, axis=1))
            bottom = jnp.where(own, -neg, pltpu.roll(re, shift, axis=1))
            hi, lo = split(jnp.concatenate([top, bottom], axis=0))
            cols = jnp.concatenate(
                [w_cols[32 * g : 32 * g + 32], w_cols[128 + 32 * g : 160 + 32 * g]], axis=0
            )
            lhs_g = jnp.concatenate([wide(hi, cols), wide(lo, jnp.zeros_like(cols))], axis=0)
            rhs_g = jnp.concatenate([yy[o, g], e_rows], axis=0)
            both = jnp.dot(lhs_g.astype(BF16), rhs_g, preferred_element_type=F32)
            sg = both[0:64] + both[64:128]
            place = pl.ds(pl.multiple_of(16 * (f0 + g), 16), 16)
            for q in range(4):
                sgq[place, pl.ds(pl.multiple_of(TD * (4 * b + q), TD), TD)] = jnp.concatenate(
                    [sg[8 * q : 8 * q + 8], sg[32 + 8 * q : 40 + 8 * q]], axis=0
                ).astype(BF16)

    spread = [
        [(0, 0, 0), (0, 1, 0), (2, 0, 0), (1, 1, 0), (2, 0, 1), (1, 0, 0), (1, 1, 1), (1, 0, 1)],
        [(0, 0, 1), (0, 1, 1), (2, 1, 0), (3, 1, 0), (2, 1, 1), (3, 0, 0), (3, 1, 1), (3, 0, 1)],
    ]

    @pl.loop(0, DP // 2)
    def _(i):
        pair = []
        for column in spread:
            dz = table(i, [k[0] for k in column])
            dx = table(i, [k[1] for k in column])
            dc = table(i, [k[2] for k in column])
            pair.append((rel(dz, dx, dc), dc))
        for o, dc in pair:

            @pl.when(o != d)
            def _():
                pay_copy(o, 0, core).wait_recv()

            @pl.when((o != d) & (dc == 0))
            def _():
                pay_copy(o, 8 + o // 2, core).start()

        for o, dc in pair:
            group_grads(o)

    enh_copy = pltpu.make_async_copy(enh_ref, enh_out, in_sem.at[5])
    enh_copy.start()
    acc = nt_dot(sgq[...], frames[...])
    keep = iota((512, 256), 0) % 8 == (iota((512, 256), 1) % 128) // 16
    rows = jnp.sum(jnp.where(keep, acc, 0.0).reshape(64, 8, 256), axis=1)
    lane16 = iota((16, 128), 1)
    halves = []
    for half in (rows[:, :128], rows[:, 128:]):
        for step in (64, 32, 16):
            half = half + pltpu.roll(half, step, axis=1)
        halves.append(half)
    part = jnp.zeros((16, 128), F32)
    for p in range(4):
        at = slice(16 * p, 16 * p + 16)
        one = jnp.where((lane16 // 16) % 2 == 0, halves[0][at], halves[1][at])
        part = jnp.where(lane16 // 32 == p, one, part)
    fg[d] = part

    def grad_copy(j, slot, dev):
        return remote(fg.at[d], fg.at[slot], f_send.at[j], f_recv.at[slot], dev, mu)

    for j in range(1, DP):
        grad_copy(j, d, other_d(j)).start()
    for j in range(1, DP):
        grad_copy(j, other_d(j), d).wait_recv()
    result = fg[0]
    for j in range(1, DP):
        result = result + fg[j]
    turned = result.T
    grad_ref[...] = jnp.concatenate([turned[32 * p : 32 * p + 32] for p in range(4)], axis=1)

    enh_copy.wait()
    head_first().wait_send()
    for j in range(1, MIC):
        wave_copy(0, j, mu, mu).wait_send()
        wave_copy(1, j, mu, mu).wait_send()
        head_copy(j, mu, mu).wait_send()
    for k in range(8):
        sum_copy(d, 0, k, core).wait_send()
        pay_copy(d, k, core).wait_send()
    for k in range(7):
        sum_copy(d, 0, 8 + others[k] // 2, core).wait_send()
        pay_copy(d, 8 + others[k] // 2, core).wait_send()
    for j in range(1, DP):
        grad_copy(j, d, d).wait_send()


def local(waveform, filters, speech_mask, noise_mask, target, ref_mic):
    vmem = pl.BlockSpec(memory_space=pltpu.VMEM)
    anywhere = pl.BlockSpec(memory_space=pl.ANY)
    dma = pltpu.SemaphoreType.DMA
    enhanced, grad = pl.pallas_call(
        body,
        out_shape=(
            jax.ShapeDtypeStruct((2, 2, 32, TD), F32),
            jax.ShapeDtypeStruct((32, 64), F32),
        ),
        in_specs=[anywhere] * 5 + [pl.BlockSpec(memory_space=pltpu.SMEM)],
        out_specs=(anywhere, vmem),
        scratch_shapes=[
            pltpu.VMEM((2, 4, 16 * TD), BF16),
            pltpu.VMEM((32, 64), BF16),
            pltpu.VMEM((2, 32, TD), BF16),
            pltpu.VMEM((2, 32, TD), BF16),
            pltpu.VMEM((2, 2, 32, TD), F32),
            pltpu.VMEM((2, 2, 32, TD), F32),
            dma((6,)),
            pltpu.VMEM((2, 64, TD), BF16),
            pltpu.VMEM((8, 128), F32),
            pltpu.VMEM((MIC, 2, 64, TD), BF16),
            pltpu.VMEM((MIC, 8, 128), F32),
            pltpu.VMEM((256, 8 * TD), BF16),
            pltpu.VMEM((DP, 2, 4, 32, TD), BF16),
            pltpu.VMEM((DP, 4, 128, TD), BF16),
            pltpu.VMEM((2, 800, TD), BF16),
            pltpu.VMEM((DP, ROWS, 128), F32),
            pltpu.VMEM((DP, ROWS, 128), F32),
            pltpu.VMEM((DP, PAY, 128), F32),
            pltpu.VMEM((512, 8 * TD), BF16),
            pltpu.VMEM((DP, 16, 128), F32),
            pltpu.VMEM((DP, 16, TD), F32),
            pltpu.VMEM((64, TD), F32),
            pltpu.VMEM((64, TD), F32),
            pltpu.VMEM((512, 256), BF16),
            dma((2 * MIC,)), dma((2 * MIC,)), dma((MIC,)), dma((MIC,)),
            dma((DP,)), dma((DP,)), dma((DP,)), dma((DP,)), dma((DP,)), dma((DP,)),
        ],
        compiler_params=pltpu.CompilerParams(
            collective_id=0, has_side_effects=True, vmem_limit_bytes=60 * 1024 * 1024
        ),
    )(waveform, filters.T, speech_mask, noise_mask, target, ref_mic)
    return (enhanced, grad.T)


def solution(mesh):
    in_specs = (
        P(None, "mic", "dp"),
        P("mic", None),
        P(None, "mic", "dp"),
        P(None, "mic", "dp"),
        P(None, None, "mic", "dp"),
        P(),
    )
    out_specs = (P(None, None, "mic", "dp"), P("mic", None))
    return jax.shard_map(local, mesh=mesh, in_specs=in_specs, out_specs=out_specs, check_vma=False)
```

```python
import jax
import jax.numpy as jnp
from jax import lax
from jax.experimental import pallas as pl
from jax.experimental.pallas import tpu as pltpu
from jax.sharding import PartitionSpec as P

DP = 16
MIC = 8
MICS = 32
TD = 256
LOAD = 0.05
FRAME_TOTAL = 4096.0
GRAD_SCALE = 2.0 * 64.0 / (2 * 256 * FRAME_TOTAL)
F32 = jnp.float32
BF16 = jnp.bfloat16
ROWS = 104
PAY = 72


def iota(shape, axis):
    return lax.broadcasted_iota(jnp.int32, shape, axis)


def tile4(x):
    return jnp.concatenate([x, x, x, x], axis=0)


def diagonal_blocks(x):
    rows, lanes = iota((128, 128), 0), iota((128, 128), 1)
    return jnp.where(rows // 32 == lanes // 32, tile4(x), 0.0)


def fold4(x):
    return (x[0:32] + x[32:64]) + (x[64:96] + x[96:128])


def unpack_four(packed):
    row, col = iota((32, 128), 0), iota((32, 128), 1) % 32
    turned = fold4(diagonal_blocks(packed).T)
    real = jnp.where(row <= col, packed, turned)
    negated = jnp.where(row > col, -packed, jnp.where(row < col, turned, 0.0))
    return real, negated


def inverse(a_r, a_i):
    lane = iota((32, 128), 1)
    row = iota((32, 128), 0)
    base = (lane // 32) * 32
    col = lane % 32
    for k in range(32):
        index = base + k
        c_r = jnp.take_along_axis(a_r, index, axis=1)
        c_i = jnp.take_along_axis(a_i, index, axis=1)
        scale = 1.0 / c_r[k : k + 1, :]
        here = col[0:1] == k
        r_r = jnp.where(here, 1.0, a_r[k : k + 1, :]) * scale
        r_i = jnp.where(here, 0.0, a_i[k : k + 1, :]) * scale
        at_col = col == k
        n_r = jnp.where(at_col, 0.0, a_r) - (c_r * r_r - c_i * r_i)
        n_i = jnp.where(at_col, 0.0, a_i) - (c_r * r_i + c_i * r_r)
        at_row = row == k
        a_r = jnp.where(at_row, r_r, n_r)
        a_i = jnp.where(at_row, r_i, n_i)
    return a_r, a_i


def thirds(x):
    one = x.astype(BF16).astype(F32)
    two = (x - one).astype(BF16).astype(F32)
    return one, two, x - one - two


def complex_blocks(real, imag):
    keep = iota((128, 128), 0) // 32 == iota((128, 128), 1) // 32
    r = jnp.where(keep, tile4(real), 0.0).astype(BF16)
    i = jnp.where(keep, tile4(imag), 0.0).astype(BF16)
    return jnp.concatenate(
        [jnp.concatenate([r, i], axis=1), jnp.concatenate([-i, r], axis=1)], axis=0
    )


def times(a_r, a_i, b_r, b_i):
    a = thirds(jnp.concatenate([a_r, a_i], axis=1))
    reals, imags = thirds(b_r), thirds(b_i)
    out = None
    for k in range(2, -1, -1):
        rows = jnp.concatenate(a[: 3 - k], axis=0).astype(BF16)
        part = jnp.dot(rows, complex_blocks(reals[k], imags[k]), preferred_element_type=F32)
        for m in range(2 - k, -1, -1):
            one = part[32 * m : 32 * m + 32]
            out = one if out is None else out + one
    return out[:, :128], out[:, 128:]


def group_totals(x):
    ones = jnp.where(iota((128, 128), 0) // 32 == iota((128, 128), 1) // 32, 1.0, 0.0).astype(BF16)
    n = x.shape[0]
    rows = jnp.concatenate(thirds(x), axis=0).astype(BF16)
    out = jnp.dot(rows, ones, preferred_element_type=F32)
    return out[0:n] + (out[n : 2 * n] + out[2 * n :])


def solve(total, pick):
    lane = iota((32, 128), 1)
    row = iota((32, 128), 0)
    eye = row == lane % 32
    inv_t = 1.0 / FRAME_TOTAL

    def column_sum(x):
        return jnp.sum(x, axis=0, keepdims=True)

    s_r, s_neg = unpack_four(total[0:32])
    n_r, n_neg = unpack_four(total[32:64])
    k_r, k_neg = unpack_four(total[64:96])
    d_r, d_i = total[96:97], total[97:98]
    s_r = s_r * inv_t + jnp.where(eye, LOAD, 0.0)
    s_i = s_neg * -inv_t
    m_r, m_i = inverse(n_r * inv_t + jnp.where(eye, LOAD, 0.0), n_neg * -inv_t)
    xh_r, xh_i = times(s_r, s_i, m_r, m_i)
    q_r, q_i = times(m_r, m_i, xh_r, xh_i)
    at_ref = row == pick
    conj_c_r = column_sum(jnp.where(at_ref, xh_r, 0.0))
    conj_c_i = column_sum(jnp.where(at_ref, xh_i, 0.0))
    sref_r = column_sum(jnp.where(at_ref, s_r, 0.0))
    sref_i = column_sum(jnp.where(at_ref, s_i, 0.0))
    diag = column_sum(jnp.where(eye, xh_r, 0.0))
    first = group_totals(
        jnp.concatenate(
            [
                jnp.broadcast_to(diag, (8, 128)),
                m_r * sref_r + m_i * sref_i,
                m_i * sref_r - m_r * sref_i,
            ],
            axis=0,
        )
    )
    inv_tau = 1.0 / first[0:1]
    c_r, c_i = first[8:40], first[40:72]
    w_r = conj_c_r * inv_tau
    w_i = -conj_c_i * inv_tau
    h_r, h_i = c_r * inv_tau, c_i * inv_tau
    g_r = GRAD_SCALE * (column_sum(h_r * k_r - h_i * k_neg) - d_r)
    g_i = GRAD_SCALE * (column_sum(h_i * k_r + h_r * k_neg) - d_i)
    gc_r, gc_i = g_r * inv_tau, g_i * inv_tau
    gw = (g_r * w_r + g_i * w_i) * inv_tau
    second = group_totals(
        jnp.concatenate(
            [
                jnp.broadcast_to(gw, (8, 128)),
                m_r * gc_r - m_i * gc_i,
                m_r * gc_i + m_i * gc_r,
            ],
            axis=0,
        )
    )
    gt2 = -2.0 * second[0:1]
    u_r, u_i = second[8:40], second[40:72]
    uh_r = column_sum(jnp.where(eye, u_r, 0.0))
    uh_i = -column_sum(jnp.where(eye, u_i, 0.0))
    col_ref = (lane % 32) == pick
    p_r = jnp.where(col_ref, u_r, 0.0) + jnp.where(at_ref, uh_r, 0.0) + gt2 * m_r
    p_i = jnp.where(col_ref, u_i, 0.0) + jnp.where(at_ref, uh_i, 0.0) + gt2 * m_i
    n_r = (u_r * conj_c_r - u_i * conj_c_i) + (c_r * uh_r - c_i * uh_i) + gt2 * q_r
    n_i = (u_r * conj_c_i + u_i * conj_c_r) + (c_r * uh_i + c_i * uh_r) + gt2 * q_i
    upper = row <= lane % 32
    speech = jnp.where(upper, p_r, p_i) * inv_t
    noise = jnp.where(upper, n_r, n_i) * (-inv_t)
    return speech, noise, w_r, w_i


def tn_dot(a, b):
    return lax.dot_general(a, b, (((0,), (0,)), ((), ())), preferred_element_type=F32)


def block_filters(filters_t):
    lane = iota((32, 256), 1)
    spread = jnp.where(iota((32, 256), 0) == (lane // 128) * 16 + lane % 16, 1.0, 0.0)
    wide = tn_dot(filters_t, spread.astype(BF16)).astype(BF16)
    repeat = jnp.where(iota((512, 64), 0) // 8 == iota((512, 64), 1), 1.0, 0.0).astype(BF16)
    full = jnp.dot(repeat, wide, preferred_element_type=F32)
    keep = iota((512, 256), 0) % 8 == (iota((512, 256), 1) % 128) // 16
    return jnp.where(keep, full, 0.0).astype(BF16)


def split(x):
    high = x.astype(BF16).astype(F32)
    return high, x - high


def nt_dot(a, b):
    return lax.dot_general(a, b, (((1,), (1,)), ((), ())), preferred_element_type=F32)


def body(
    wave_in, filt_in, smask_in, nmask_in, target_in, pick_in,
    enh_out, grad_ref,
    wave_ref, filt_ref, smask_ref, nmask_ref, target_ref, pick_ref, enh_ref, in_sem,
    wblk, head, gath, heads, frames, zz, yy, lhs, sb, rb, pay, sgq, fg, tt, ms, mn, fb,
    g_send, g_recv, h_send, h_recv, s_send, s_recv, p_send, p_recv, f_send, f_recv,
):
    d = lax.axis_index("dp")
    mu = lax.axis_index("mic")
    prev = lax.rem(d + DP - 1, DP)
    nxt = lax.rem(d + 1, DP)
    at_z, at_x, at_c = d >> 2, (d >> 1) & 1, d & 1
    chip = d >> 1
    core = d ^ 1

    def rel(dz, dx, dc):
        return ((d + 4 * dz) & 12) | ((d ^ (2 * dx + dc)) & 3)

    others = [rel(0, 1, 0), rel(1, 0, 0), rel(3, 0, 0), rel(1, 1, 0), rel(3, 1, 0), rel(2, 0, 0), rel(2, 1, 0)]

    def table(i, values):
        out = values[0]
        for k in range(1, len(values)):
            out = jnp.where(i == k, values[k], out)
        return out

    def other_d(j):
        return lax.rem(d + j, DP)

    def other_m(j):
        return lax.rem(mu + j, MIC)

    def remote(src, dst, send, recv, dev_d, dev_m):
        return pltpu.make_async_remote_copy(
            src_ref=src, dst_ref=dst, send_sem=send, recv_sem=recv,
            device_id={"dp": dev_d, "mic": dev_m}, device_id_type=pl.DeviceIdType.MESH,
        )

    loads = [
        pltpu.make_async_copy(src, dst, in_sem.at[k])
        for k, (src, dst) in enumerate(
            [
                (wave_in, wave_ref), (filt_in, filt_ref), (smask_in, smask_ref),
                (nmask_in, nmask_ref), (target_in, target_ref), (pick_in, pick_ref),
            ]
        )
    ]
    for load in loads:
        load.start()

    barrier = pltpu.get_barrier_semaphore()

    def greet(dev_d, dev_m):
        pl.semaphore_signal(
            barrier, inc=1, device_id={"dp": dev_d, "mic": dev_m},
            device_id_type=pl.DeviceIdType.MESH,
        )

    for j in range(1, MIC):
        greet(d, other_m(j))
    for peer in others + [core, prev, nxt]:
        greet(peer, mu)

    for load in loads:
        load.wait()

    turn = iota((128, 1024), 0)
    lane = iota((128, 1024), 1)
    choose = (turn % 4 == lane // TD) & (turn // 4 == (lane % TD) // 8)
    choose = jnp.where(choose, 1.0, 0.0).astype(BF16)
    phase = iota((16, 1024), 1) % 8
    for b in range(2):
        rows = wave_ref[b].astype(F32)
        head[4 * b : 4 * b + 4, :] = rows[:, 0:128]
        stacked = jnp.concatenate([rows[:, 128 * r : 128 * r + 128] for r in range(32)], axis=0)
        spread = jnp.dot(stacked.T.astype(BF16), choose, preferred_element_type=F32)
        taps = spread[0:16]
        for k in range(1, 8):
            taps = jnp.where(phase == k, spread[16 * k : 16 * k + 16], taps)
        for m in range(4):
            wblk[b, 16 * m : 16 * m + 16, :] = taps[:, TD * m : TD * m + TD].astype(BF16)

    fb[...] = block_filters(filt_ref[...])
    ms[...] = smask_ref[...].reshape(64, TD).astype(F32)
    mn[...] = nmask_ref[...].reshape(64, TD).astype(F32)
    for o in range(DP):
        for v in range(2):
            tt[o, 8 * v : 8 * v + 4, :] = target_ref[o // 8, v, (o % 8) * 4 : (o % 8) * 4 + 4, :]
            tt[o, 8 * v + 4 : 8 * v + 8, :] = jnp.zeros((4, TD), F32)

    pl.semaphore_wait(barrier, MIC + DP // 2 + 1)

    def wave_copy(b, j, slot, dev):
        return remote(wblk.at[b], gath.at[slot, b], g_send.at[MIC * b + j], g_recv.at[MIC * b + slot], d, dev)

    def head_copy(j, slot, dev):
        return remote(heads.at[mu], heads.at[slot], h_send.at[j], h_recv.at[slot], d, dev)

    def head_first():
        return remote(head, heads.at[mu], h_send.at[0], h_recv.at[mu], prev, mu)

    head_first().start()
    for j in range(1, MIC):
        wave_copy(0, j, mu, other_m(j)).start()
    gath[mu] = wblk[...]
    head_first().wait_recv()
    for j in range(1, MIC):
        head_copy(j, mu, other_m(j)).start()
    for j in range(1, MIC):
        wave_copy(1, j, mu, other_m(j)).start()

    last = d == DP - 1
    tap128 = iota((128, 128), 1) == iota((128, 128), 0) % 16
    end = iota((128, TD), 1) == TD - 1

    def encode(b):
        for q in range(4):
            x = jnp.concatenate([gath[2 * q, b], gath[2 * q + 1, b]], axis=0).astype(F32)
            near = jnp.concatenate(
                [
                    jnp.broadcast_to(heads[2 * q + p, 4 * b + m : 4 * b + m + 1, :], (16, 128))
                    for p in range(2)
                    for m in range(4)
                ],
                axis=0,
            )
            near = jnp.where(last, 0.0, near)
            column = jnp.sum(jnp.where(tap128, near, 0.0), axis=1, keepdims=True)
            moved = jnp.where(end, column, pltpu.roll(x, TD - 1, axis=1))
            piece = slice(TD * (4 * b + q), TD * (4 * b + q) + TD)
            frames[0:128, piece] = x.astype(BF16)
            frames[128:256, piece] = moved.astype(BF16)
        for half in range(2):
            at = TD * (4 * b + 2 * half)
            a0 = jnp.dot(fb[...], frames[:, at : at + TD], preferred_element_type=F32)
            a1 = jnp.dot(fb[...], frames[:, at + TD : at + 2 * TD], preferred_element_type=F32)
            z = jnp.concatenate(
                [a0.reshape(8, 4, 2, 8, TD), a1.reshape(8, 4, 2, 8, TD)], axis=3
            ).astype(BF16)
            for v in range(2):
                zz[8 * b : 8 * b + 8, v, :, 16 * half : 16 * half + 16, :] = z[:, :, v]

    lane32 = iota((32, 128), 1)
    upper = iota((32, 128), 0) <= lane32 % 32
    row8 = iota((8, 128), 0)
    own8 = row8 == iota((8, 128), 1) // 32

    def group_sums(o, w):
        t_hi, t_lo = split(tt[o])
        lhs[w, 512:768, :] = zz[o].reshape(256, TD)
        lhs[w, 768:800, :] = jnp.concatenate([t_hi, t_lo], axis=0).astype(BF16)
        for g in range(4):
            for k, ref in enumerate((ms, mn)):
                mask = jnp.broadcast_to(ref[pl.ds(4 * o + g, 1), :], (32, TD)).astype(BF16)
                for v in range(2):
                    part = zz[o, v, g] * mask
                    at = 128 * v + 32 * g
                    lhs[w, 256 * k + at : 256 * k + at + 32, :] = part
                    row = 64 * k + 32 * ((v + g) % 2)
                    yy[o, g, row : row + 32, :] = part
        out = nt_dot(lhs[w], zz[o].reshape(256, TD))
        for kind in range(3):
            value = jnp.zeros((32, 128), F32)
            for g in range(4):
                re = out[256 * kind + 32 * g : 256 * kind + 32 * g + 32]
                im = out[256 * kind + 128 + 32 * g : 256 * kind + 160 + 32 * g]
                one = jnp.where(upper, re[:, :128] + im[:, 128:], im[:, :128] - re[:, 128:])
                value = jnp.where(lane32 // 32 == g, one, value)
            sb[o, 32 * kind : 32 * kind + 32, :] = value
        t0 = out[768:776] + out[784:792]
        t1 = out[776:784] + out[792:800]
        d_r = jnp.sum(jnp.where(own8, t0[:, :128] + t1[:, 128:], 0.0), axis=0, keepdims=True)
        d_i = jnp.sum(jnp.where(own8, t0[:, 128:] - t1[:, :128], 0.0), axis=0, keepdims=True)
        sb[o, 96:104, :] = jnp.where(row8 == 0, d_r, jnp.where(row8 == 1, d_i, 0.0))

    def sum_copy(o, slot, sem, dev):
        return remote(sb.at[o], rb.at[slot], s_send.at[sem], s_recv.at[slot], dev, mu)

    def add_slot(o, slot):
        sum_copy(o, slot, slot, core).wait_recv()
        sb[o] = sb[o] + rb[slot]

    for b in range(2):
        for j in range(1, MIC):
            wave_copy(b, j, other_m(j), mu).wait_recv()
        if b == 0:
            for j in range(1, MIC):
                head_copy(j, other_m(j), mu).wait_recv()
        encode(b)
        here = jnp.where((at_z >> 1) == b, 1, 0)

        def target(k, mine):
            to = 4 * b + 2 * ((at_z + (k >> 1) + here) & 1) + ((at_x + 1 + k) & 1)
            return to, 2 * to + ((at_c + 1 + mine) & 1)

        def give(to, o):
            sum_copy(o, to, to, core).start()

        def keep(to, o):
            add_slot(o, to)

            @pl.when(to != chip)
            def _():
                sum_copy(o, 8 + chip, 8 + to, o).start()

        @pl.loop(0, 4)
        def _(i):
            to_a, o_a = target(table(i, [0, 2, 3, 2]), table(i, [0, 0, 0, 1]))
            to_b, o_b = target(table(i, [1, 0, 1, 3]), table(i, [0, 1, 1, 1]))
            group_sums(o_a, 0)
            group_sums(o_b, 1)

            @pl.when(i < 3)
            def _():
                give(to_a, o_a)

            @pl.when(i == 3)
            def _():
                keep(to_a, o_a)

            @pl.when(i == 0)
            def _():
                give(to_b, o_b)

            @pl.when(i > 0)
            def _():
                keep(to_b, o_b)

    for k in range(7):
        add_slot(d, 8 + (others[k] >> 1))
    pick = jnp.where(d < DP // 2, pick_ref[0], pick_ref[1])
    speech, noise, w_r, w_i = solve(sb[d], pick)
    left_half = lane32 < 64
    pay[d, 0:32, :] = jnp.where(left_half, speech, pltpu.roll(noise, 64, axis=1))
    pay[d, 32:64, :] = jnp.where(left_half, pltpu.roll(speech, 64, axis=1), noise)
    pay[d, 64:72, :] = jnp.where(row8 == 0, w_r, jnp.where(row8 == 1, w_i, 0.0))

    def pay_copy(o, sem, dev):
        return remote(pay.at[o], pay.at[o], p_send.at[sem], p_recv.at[o], dev, mu)

    for k, dev in enumerate([core, others[0]] + others[:0:-1]):
        pay_copy(d, k, dev).start()

    def group_grads(o):
        b = o >> 3
        f0 = (o & 7) << 2
        w_r = jnp.where(own8, pay[o, 64:65, :], 0.0)
        w_i = jnp.where(own8, pay[o, 65:66, :], 0.0)
        wr_hi, wr_lo = split(w_r)
        wi_hi, wi_lo = split(w_i)

        def wide(p, q):
            return jnp.concatenate([p, q], axis=1)

        first = jnp.concatenate([wide(wr_hi, wi_hi), wide(-wi_hi, wr_hi)], axis=0)
        second = jnp.concatenate([wide(wr_lo, wi_lo), wide(-wi_lo, wr_lo)], axis=0)
        left = jnp.concatenate([first, second], axis=0)
        both = jnp.dot(left.astype(BF16), zz[o].reshape(256, TD), preferred_element_type=F32)
        enh = both[0:16] + both[16:32]
        for g in range(4):
            enh_ref[b, 0, pl.ds(f0 + g, 1), :] = enh[g : g + 1, :]
            enh_ref[b, 1, pl.ds(f0 + g, 1), :] = enh[8 + g : 9 + g, :]
        e_hi, e_lo = split(GRAD_SCALE * (enh - tt[o]))
        e_rows = jnp.concatenate([e_hi, e_hi, e_lo], axis=0).astype(BF16)
        w_cols = jnp.concatenate([first, second, first], axis=0).T
        even = (lane32 // 32) % 2 == 0
        for g in range(4):
            if g % 2 == 0:
                re, neg = unpack_four(pay[o, 16 * g : 16 * g + 32, :])
            shift = 32 if g % 2 == 0 else 96
            own = even if g % 2 == 0 else ~even
            top = jnp.where(own, re, pltpu.roll(neg, shift, axis=1))
            bottom = jnp.where(own, -neg, pltpu.roll(re, shift, axis=1))
            hi, lo = split(jnp.concatenate([top, bottom], axis=0))
            cols = jnp.concatenate(
                [w_cols[32 * g : 32 * g + 32], w_cols[128 + 32 * g : 160 + 32 * g]], axis=0
            )
            lhs_g = jnp.concatenate([wide(hi, cols), wide(lo, jnp.zeros_like(cols))], axis=0)
            rhs_g = jnp.concatenate([yy[o, g], e_rows], axis=0)
            both = jnp.dot(lhs_g.astype(BF16), rhs_g, preferred_element_type=F32)
            sg = both[0:64] + both[64:128]
            place = pl.ds(pl.multiple_of(16 * (f0 + g), 16), 16)
            for q in range(4):
                sgq[place, pl.ds(pl.multiple_of(TD * (4 * b + q), TD), TD)] = jnp.concatenate(
                    [sg[8 * q : 8 * q + 8], sg[32 + 8 * q : 40 + 8 * q]], axis=0
                ).astype(BF16)

    spread = [
        [(0, 0, 0), (0, 1, 0), (2, 0, 0), (1, 1, 0), (2, 0, 1), (1, 0, 0), (1, 1, 1), (1, 0, 1)],
        [(0, 0, 1), (0, 1, 1), (2, 1, 0), (3, 1, 0), (2, 1, 1), (3, 0, 0), (3, 1, 1), (3, 0, 1)],
    ]

    @pl.loop(0, DP // 2)
    def _(i):
        pair = []
        for column in spread:
            code = table(i, [4 * k[0] + 2 * k[1] + k[2] for k in column])
            pair.append((((d + (code & 12)) & 12) | ((d ^ code) & 3), code & 1))
        for o, dc in pair:

            @pl.when(o != d)
            def _():
                pay_copy(o, 0, core).wait_recv()

            @pl.when((o != d) & (dc == 0))
            def _():
                pay_copy(o, 8 + (o >> 1), core).start()

        for o, dc in pair:
            group_grads(o)

    enh_copy = pltpu.make_async_copy(enh_ref, enh_out, in_sem.at[6])
    enh_copy.start()
    acc = nt_dot(sgq[...], frames[...])
    keep = iota((512, 256), 0) % 8 == (iota((512, 256), 1) % 128) // 16
    rows = jnp.sum(jnp.where(keep, acc, 0.0).reshape(64, 8, 256), axis=1)
    lane16 = iota((16, 128), 1)
    halves = []
    for half in (rows[:, :128], rows[:, 128:]):
        for step in (64, 32, 16):
            half = half + pltpu.roll(half, step, axis=1)
        halves.append(half)
    part = jnp.zeros((16, 128), F32)
    for p in range(4):
        at = slice(16 * p, 16 * p + 16)
        one = jnp.where((lane16 // 16) % 2 == 0, halves[0][at], halves[1][at])
        part = jnp.where(lane16 // 32 == p, one, part)
    fg[d] = part

    def grad_copy(j, slot, dev):
        return remote(fg.at[d], fg.at[slot], f_send.at[j], f_recv.at[slot], dev, mu)

    for j in range(1, DP):
        grad_copy(j, d, other_d(j)).start()
    for j in range(1, DP):
        grad_copy(j, other_d(j), d).wait_recv()
    result = fg[0]
    for j in range(1, DP):
        result = result + fg[j]
    turned = result.T
    grad_ref[...] = jnp.concatenate([turned[32 * p : 32 * p + 32] for p in range(4)], axis=1)

    enh_copy.wait()
    head_first().wait_send()
    for j in range(1, MIC):
        wave_copy(0, j, mu, mu).wait_send()
        wave_copy(1, j, mu, mu).wait_send()
        head_copy(j, mu, mu).wait_send()
    for k in range(8):
        sum_copy(d, 0, k, core).wait_send()
        pay_copy(d, k, core).wait_send()
    for k in range(7):
        sum_copy(d, 0, 8 + (others[k] >> 1), core).wait_send()
        pay_copy(d, 8 + (others[k] >> 1), core).wait_send()
    for j in range(1, DP):
        grad_copy(j, d, d).wait_send()


def local(waveform, filters, speech_mask, noise_mask, target, ref_mic):
    held = [
        pltpu.with_memory_space_constraint(v, pltpu.HBM)
        for v in (waveform, filters.T, speech_mask, noise_mask, target, ref_mic)
    ]
    vmem = pl.BlockSpec(memory_space=pltpu.VMEM)
    anywhere = pl.BlockSpec(memory_space=pl.ANY)
    dma = pltpu.SemaphoreType.DMA
    enhanced, grad = pl.pallas_call(
        body,
        out_shape=(
            jax.ShapeDtypeStruct((2, 2, 32, TD), F32),
            jax.ShapeDtypeStruct((32, 64), F32),
        ),
        in_specs=[pl.BlockSpec(memory_space=pltpu.HBM)] * 6,
        out_specs=(anywhere, vmem),
        scratch_shapes=[
            pltpu.VMEM((2, 4, 16 * TD), BF16),
            pltpu.VMEM((32, 64), BF16),
            pltpu.VMEM((2, 32, TD), BF16),
            pltpu.VMEM((2, 32, TD), BF16),
            pltpu.VMEM((2, 2, 32, TD), F32),
            pltpu.SMEM((2,), jnp.int32),
            pltpu.VMEM((2, 2, 32, TD), F32),
            dma((7,)),
            pltpu.VMEM((2, 64, TD), BF16),
            pltpu.VMEM((8, 128), F32),
            pltpu.VMEM((MIC, 2, 64, TD), BF16),
            pltpu.VMEM((MIC, 8, 128), F32),
            pltpu.VMEM((256, 8 * TD), BF16),
            pltpu.VMEM((DP, 2, 4, 32, TD), BF16),
            pltpu.VMEM((DP, 4, 128, TD), BF16),
            pltpu.VMEM((2, 800, TD), BF16),
            pltpu.VMEM((DP, ROWS, 128), F32),
            pltpu.VMEM((DP, ROWS, 128), F32),
            pltpu.VMEM((DP, PAY, 128), F32),
            pltpu.VMEM((512, 8 * TD), BF16),
            pltpu.VMEM((DP, 16, 128), F32),
            pltpu.VMEM((DP, 16, TD), F32),
            pltpu.VMEM((64, TD), F32),
            pltpu.VMEM((64, TD), F32),
            pltpu.VMEM((512, 256), BF16),
            dma((2 * MIC,)), dma((2 * MIC,)), dma((MIC,)), dma((MIC,)),
            dma((DP,)), dma((DP,)), dma((DP,)), dma((DP,)), dma((DP,)), dma((DP,)),
        ],
        compiler_params=pltpu.CompilerParams(
            collective_id=0, has_side_effects=True, vmem_limit_bytes=28 * 1024 * 1024
        ),
    )(*held)
    return (enhanced, grad.T)


def solution(mesh):
    in_specs = (
        P(None, "mic", "dp"),
        P("mic", None),
        P(None, "mic", "dp"),
        P(None, "mic", "dp"),
        P(None, None, "mic", "dp"),
        P(),
    )
    out_specs = (P(None, None, "mic", "dp"), P("mic", None))
    return jax.shard_map(local, mesh=mesh, in_specs=in_specs, out_specs=out_specs, check_vma=False)
```

```python
import jax
import jax.numpy as jnp
from jax import lax
from jax.experimental import pallas as pl
from jax.experimental.pallas import tpu as pltpu
from jax.sharding import PartitionSpec as P

DP = 16
MIC = 8
MICS = 32
TD = 256
LOAD = 0.05
FRAME_TOTAL = 4096.0
GRAD_SCALE = 2.0 * 64.0 / (2 * 256 * FRAME_TOTAL)
F32 = jnp.float32
BF16 = jnp.bfloat16
ROWS = 104
PAY = 72


def iota(shape, axis):
    return lax.broadcasted_iota(jnp.int32, shape, axis)


def tile4(x):
    return jnp.concatenate([x, x, x, x], axis=0)


def diagonal_blocks(x):
    rows, lanes = iota((128, 128), 0), iota((128, 128), 1)
    return jnp.where(rows // 32 == lanes // 32, tile4(x), 0.0)


def fold4(x):
    return (x[0:32] + x[32:64]) + (x[64:96] + x[96:128])


def unpack_four(packed):
    row, col = iota((32, 128), 0), iota((32, 128), 1) % 32
    turned = fold4(diagonal_blocks(packed).T)
    real = jnp.where(row <= col, packed, turned)
    negated = jnp.where(row > col, -packed, jnp.where(row < col, turned, 0.0))
    return real, negated


def inverse(a_r, a_i):
    lane = iota((32, 128), 1)
    row = iota((32, 128), 0)
    base = (lane // 32) * 32
    col = lane % 32
    for k in range(32):
        index = base + k
        c_r = jnp.take_along_axis(a_r, index, axis=1)
        c_i = jnp.take_along_axis(a_i, index, axis=1)
        scale = 1.0 / c_r[k : k + 1, :]
        here = col[0:1] == k
        r_r = jnp.where(here, 1.0, a_r[k : k + 1, :]) * scale
        r_i = jnp.where(here, 0.0, a_i[k : k + 1, :]) * scale
        at_col = col == k
        n_r = jnp.where(at_col, 0.0, a_r) - (c_r * r_r - c_i * r_i)
        n_i = jnp.where(at_col, 0.0, a_i) - (c_r * r_i + c_i * r_r)
        at_row = row == k
        a_r = jnp.where(at_row, r_r, n_r)
        a_i = jnp.where(at_row, r_i, n_i)
    return a_r, a_i


def thirds(x):
    one = x.astype(BF16).astype(F32)
    two = (x - one).astype(BF16).astype(F32)
    return one, two, x - one - two


def complex_blocks(real, imag):
    keep = iota((128, 128), 0) // 32 == iota((128, 128), 1) // 32
    r = jnp.where(keep, tile4(real), 0.0).astype(BF16)
    i = jnp.where(keep, tile4(imag), 0.0).astype(BF16)
    return jnp.concatenate(
        [jnp.concatenate([r, i], axis=1), jnp.concatenate([-i, r], axis=1)], axis=0
    )


def times(a_r, a_i, b_r, b_i):
    a = thirds(jnp.concatenate([a_r, a_i], axis=1))
    reals, imags = thirds(b_r), thirds(b_i)
    out = None
    for k in range(2, -1, -1):
        rows = jnp.concatenate(a[: 3 - k], axis=0).astype(BF16)
        part = jnp.dot(rows, complex_blocks(reals[k], imags[k]), preferred_element_type=F32)
        for m in range(2 - k, -1, -1):
            one = part[32 * m : 32 * m + 32]
            out = one if out is None else out + one
    return out[:, :128], out[:, 128:]


def group_totals(x):
    ones = jnp.where(iota((128, 128), 0) // 32 == iota((128, 128), 1) // 32, 1.0, 0.0).astype(BF16)
    n = x.shape[0]
    rows = jnp.concatenate(thirds(x), axis=0).astype(BF16)
    out = jnp.dot(rows, ones, preferred_element_type=F32)
    return out[0:n] + (out[n : 2 * n] + out[2 * n :])


def solve(total, late, pick):
    lane = iota((32, 128), 1)
    row = iota((32, 128), 0)
    eye = row == lane % 32
    inv_t = 1.0 / FRAME_TOTAL

    def column_sum(x):
        return jnp.sum(x, axis=0, keepdims=True)

    s_r, s_neg = unpack_four(total[0:32])
    n_r, n_neg = unpack_four(total[32:64])
    s_r = s_r * inv_t + jnp.where(eye, LOAD, 0.0)
    s_i = s_neg * -inv_t
    m_r, m_i = inverse(n_r * inv_t + jnp.where(eye, LOAD, 0.0), n_neg * -inv_t)
    xh_r, xh_i = times(s_r, s_i, m_r, m_i)
    q_r, q_i = times(m_r, m_i, xh_r, xh_i)
    at_ref = row == pick
    conj_c_r = column_sum(jnp.where(at_ref, xh_r, 0.0))
    conj_c_i = column_sum(jnp.where(at_ref, xh_i, 0.0))
    sref_r = column_sum(jnp.where(at_ref, s_r, 0.0))
    sref_i = column_sum(jnp.where(at_ref, s_i, 0.0))
    diag = column_sum(jnp.where(eye, xh_r, 0.0))
    first = group_totals(
        jnp.concatenate(
            [
                jnp.broadcast_to(diag, (8, 128)),
                m_r * sref_r + m_i * sref_i,
                m_i * sref_r - m_r * sref_i,
            ],
            axis=0,
        )
    )
    inv_tau = 1.0 / first[0:1]
    c_r, c_i = first[8:40], first[40:72]
    w_r = conj_c_r * inv_tau
    w_i = -conj_c_i * inv_tau
    h_r, h_i = c_r * inv_tau, c_i * inv_tau
    rest = late()
    k_r, k_neg = unpack_four(rest[0:32])
    d_r, d_i = rest[32:33], rest[33:34]
    g_r = GRAD_SCALE * (column_sum(h_r * k_r - h_i * k_neg) - d_r)
    g_i = GRAD_SCALE * (column_sum(h_i * k_r + h_r * k_neg) - d_i)
    gc_r, gc_i = g_r * inv_tau, g_i * inv_tau
    gw = (g_r * w_r + g_i * w_i) * inv_tau
    second = group_totals(
        jnp.concatenate(
            [
                jnp.broadcast_to(gw, (8, 128)),
                m_r * gc_r - m_i * gc_i,
                m_r * gc_i + m_i * gc_r,
            ],
            axis=0,
        )
    )
    gt2 = -2.0 * second[0:1]
    u_r, u_i = second[8:40], second[40:72]
    uh_r = column_sum(jnp.where(eye, u_r, 0.0))
    uh_i = -column_sum(jnp.where(eye, u_i, 0.0))
    col_ref = (lane % 32) == pick
    p_r = jnp.where(col_ref, u_r, 0.0) + jnp.where(at_ref, uh_r, 0.0) + gt2 * m_r
    p_i = jnp.where(col_ref, u_i, 0.0) + jnp.where(at_ref, uh_i, 0.0) + gt2 * m_i
    n_r = (u_r * conj_c_r - u_i * conj_c_i) + (c_r * uh_r - c_i * uh_i) + gt2 * q_r
    n_i = (u_r * conj_c_i + u_i * conj_c_r) + (c_r * uh_i + c_i * uh_r) + gt2 * q_i
    upper = row <= lane % 32
    speech = jnp.where(upper, p_r, p_i) * inv_t
    noise = jnp.where(upper, n_r, n_i) * (-inv_t)
    return speech, noise, w_r, w_i


def tn_dot(a, b):
    return lax.dot_general(a, b, (((0,), (0,)), ((), ())), preferred_element_type=F32)


def block_filters(filters_t):
    lane = iota((32, 256), 1)
    spread = jnp.where(iota((32, 256), 0) == (lane // 128) * 16 + lane % 16, 1.0, 0.0)
    wide = tn_dot(filters_t, spread.astype(BF16)).astype(BF16)
    repeat = jnp.where(iota((512, 64), 0) // 8 == iota((512, 64), 1), 1.0, 0.0).astype(BF16)
    full = jnp.dot(repeat, wide, preferred_element_type=F32)
    keep = iota((512, 256), 0) % 8 == (iota((512, 256), 1) % 128) // 16
    return jnp.where(keep, full, 0.0).astype(BF16)


def split(x):
    high = x.astype(BF16).astype(F32)
    return high, x - high


def nt_dot(a, b):
    return lax.dot_general(a, b, (((1,), (1,)), ((), ())), preferred_element_type=F32)


def body(
    wave_in, filt_in, smask_in, nmask_in, target_in, pick_in,
    enh_out, grad_ref,
    wave_ref, filt_ref, smask_ref, nmask_ref, target_ref, pick_ref, enh_ref, in_sem,
    wblk, head, gath, heads, frames, zz, yy, lhs, sb, rb, pay, sgq, fg, tt, ms, mn, fb,
    g_send, g_recv, h_send, h_recv, s_send, s_recv, p_send, p_recv, f_send, f_recv,
):
    d = lax.axis_index("dp")
    mu = lax.axis_index("mic")
    prev = lax.rem(d + DP - 1, DP)
    nxt = lax.rem(d + 1, DP)
    at_z, at_x, at_c = d >> 2, (d >> 1) & 1, d & 1
    chip = d >> 1
    core = d ^ 1

    def rel(dz, dx, dc):
        return ((d + 4 * dz) & 12) | ((d ^ (2 * dx + dc)) & 3)

    others = [rel(0, 1, 0), rel(1, 0, 0), rel(3, 0, 0), rel(1, 1, 0), rel(3, 1, 0), rel(2, 0, 0), rel(2, 1, 0)]

    def table(i, values):
        out = values[0]
        for k in range(1, len(values)):
            out = jnp.where(i == k, values[k], out)
        return out

    def other_d(j):
        return lax.rem(d + j, DP)

    def other_m(j):
        return lax.rem(mu + j, MIC)

    def remote(src, dst, send, recv, dev_d, dev_m):
        return pltpu.make_async_remote_copy(
            src_ref=src, dst_ref=dst, send_sem=send, recv_sem=recv,
            device_id={"dp": dev_d, "mic": dev_m}, device_id_type=pl.DeviceIdType.MESH,
        )

    loads = [
        pltpu.make_async_copy(src, dst, in_sem.at[k])
        for k, (src, dst) in enumerate(
            [
                (wave_in, wave_ref), (filt_in, filt_ref), (smask_in, smask_ref),
                (nmask_in, nmask_ref), (target_in, target_ref), (pick_in, pick_ref),
            ]
        )
    ]
    for load in loads:
        load.start()

    barrier = pltpu.get_barrier_semaphore()

    def greet(dev_d, dev_m):
        pl.semaphore_signal(
            barrier, inc=1, device_id={"dp": dev_d, "mic": dev_m},
            device_id_type=pl.DeviceIdType.MESH,
        )

    for j in range(1, MIC):
        greet(d, other_m(j))
    for peer in others + [core, prev, nxt]:
        greet(peer, mu)

    for load in loads:
        load.wait()

    turn = iota((128, 1024), 0)
    lane = iota((128, 1024), 1)
    choose = (turn % 4 == lane // TD) & (turn // 4 == (lane % TD) // 8)
    choose = jnp.where(choose, 1.0, 0.0).astype(BF16)
    phase = iota((16, 1024), 1) % 8
    for b in range(2):
        rows = wave_ref[b].astype(F32)
        head[4 * b : 4 * b + 4, :] = rows[:, 0:128]
        stacked = jnp.concatenate([rows[:, 128 * r : 128 * r + 128] for r in range(32)], axis=0)
        spread = jnp.dot(stacked.T.astype(BF16), choose, preferred_element_type=F32)
        taps = spread[0:16]
        for k in range(1, 8):
            taps = jnp.where(phase == k, spread[16 * k : 16 * k + 16], taps)
        for m in range(4):
            wblk[b, 16 * m : 16 * m + 16, :] = taps[:, TD * m : TD * m + TD].astype(BF16)

    fb[...] = block_filters(filt_ref[...])
    ms[...] = smask_ref[...].reshape(64, TD).astype(F32)
    mn[...] = nmask_ref[...].reshape(64, TD).astype(F32)
    for o in range(DP):
        for v in range(2):
            tt[o, 8 * v : 8 * v + 4, :] = target_ref[o // 8, v, (o % 8) * 4 : (o % 8) * 4 + 4, :]
            tt[o, 8 * v + 4 : 8 * v + 8, :] = jnp.zeros((4, TD), F32)

    pl.semaphore_wait(barrier, MIC + DP // 2 + 1)

    def wave_copy(b, j, slot, dev):
        return remote(wblk.at[b], gath.at[slot, b], g_send.at[MIC * b + j], g_recv.at[MIC * b + slot], d, dev)

    def head_copy(j, slot, dev):
        return remote(heads.at[mu], heads.at[slot], h_send.at[j], h_recv.at[slot], d, dev)

    def head_first():
        return remote(head, heads.at[mu], h_send.at[0], h_recv.at[mu], prev, mu)

    head_first().start()
    for j in range(1, MIC):
        wave_copy(0, j, mu, other_m(j)).start()
    gath[mu] = wblk[...]
    head_first().wait_recv()
    for j in range(1, MIC):
        head_copy(j, mu, other_m(j)).start()
    for j in range(1, MIC):
        wave_copy(1, j, mu, other_m(j)).start()

    last = d == DP - 1
    tap128 = iota((128, 128), 1) == iota((128, 128), 0) % 16
    end = iota((128, TD), 1) == TD - 1

    def encode(b):
        for q in range(4):
            x = jnp.concatenate([gath[2 * q, b], gath[2 * q + 1, b]], axis=0).astype(F32)
            near = jnp.concatenate(
                [
                    jnp.broadcast_to(heads[2 * q + p, 4 * b + m : 4 * b + m + 1, :], (16, 128))
                    for p in range(2)
                    for m in range(4)
                ],
                axis=0,
            )
            near = jnp.where(last, 0.0, near)
            column = jnp.sum(jnp.where(tap128, near, 0.0), axis=1, keepdims=True)
            moved = jnp.where(end, column, pltpu.roll(x, TD - 1, axis=1))
            piece = slice(TD * (4 * b + q), TD * (4 * b + q) + TD)
            frames[0:128, piece] = x.astype(BF16)
            frames[128:256, piece] = moved.astype(BF16)
        for half in range(2):
            at = TD * (4 * b + 2 * half)
            a0 = jnp.dot(fb[...], frames[:, at : at + TD], preferred_element_type=F32)
            a1 = jnp.dot(fb[...], frames[:, at + TD : at + 2 * TD], preferred_element_type=F32)
            z = jnp.concatenate(
                [a0.reshape(8, 4, 2, 8, TD), a1.reshape(8, 4, 2, 8, TD)], axis=3
            ).astype(BF16)
            for v in range(2):
                zz[8 * b : 8 * b + 8, v, :, 16 * half : 16 * half + 16, :] = z[:, :, v]

    lane32 = iota((32, 128), 1)
    upper = iota((32, 128), 0) <= lane32 % 32
    row8 = iota((8, 128), 0)
    own8 = row8 == iota((8, 128), 1) // 32

    def packed(out, first):
        value = jnp.zeros((32, 128), F32)
        for g in range(4):
            re = out[first + 32 * g : first + 32 * g + 32]
            im = out[first + 128 + 32 * g : first + 160 + 32 * g]
            one = jnp.where(upper, re[:, :128] + im[:, 128:], im[:, :128] - re[:, 128:])
            value = jnp.where(lane32 // 32 == g, one, value)
        return value

    def masked_sums(o, w):
        for g in range(4):
            for k, ref in enumerate((ms, mn)):
                mask = jnp.broadcast_to(ref[pl.ds(4 * o + g, 1), :], (32, TD)).astype(BF16)
                for v in range(2):
                    part = zz[o, v, g] * mask
                    at = 128 * v + 32 * g
                    lhs[w, 256 * k + at : 256 * k + at + 32, :] = part
                    row = 64 * k + 32 * ((v + g) % 2)
                    yy[o, g, row : row + 32, :] = part
        out = nt_dot(lhs[w], zz[o].reshape(256, TD))
        sb[o, 0:32, :] = packed(out, 0)
        sb[o, 32:64, :] = packed(out, 256)

    def other_sums(o, w):
        t_hi, t_lo = split(tt[o])
        own = zz[o].reshape(256, TD)
        t_rows = jnp.concatenate([t_hi, t_lo], axis=0).astype(BF16)
        out = nt_dot(jnp.concatenate([own, t_rows], axis=0), own)
        sb[o, 64:96, :] = packed(out, 0)
        t0 = out[256:264] + out[272:280]
        t1 = out[264:272] + out[280:288]
        d_r = jnp.sum(jnp.where(own8, t0[:, :128] + t1[:, 128:], 0.0), axis=0, keepdims=True)
        d_i = jnp.sum(jnp.where(own8, t0[:, 128:] - t1[:, :128], 0.0), axis=0, keepdims=True)
        sb[o, 96:104, :] = jnp.where(row8 == 0, d_r, jnp.where(row8 == 1, d_i, 0.0))

    def sum_copy(n, o, slot, sem, dev):
        rows = slice(0, 64) if n == 0 else slice(64, ROWS)
        return remote(
            sb.at[o, rows], rb.at[slot, rows], s_send.at[DP * n + sem], s_recv.at[DP * n + slot],
            dev, mu,
        )

    def add_slot(n, o, slot):
        rows = slice(0, 64) if n == 0 else slice(64, ROWS)
        sum_copy(n, o, slot, slot, core).wait_recv()
        sb[o, rows, :] = sb[o, rows, :] + rb[slot, rows, :]

    def pass_over(n, b, sums):
        here = jnp.where((at_z >> 1) == b, 1, 0)

        def target(k, mine):
            to = 4 * b + 2 * ((at_z + (k >> 1) + here) & 1) + ((at_x + 1 + k) & 1)
            return to, 2 * to + ((at_c + 1 + mine) & 1)

        def give(to, o):
            sum_copy(n, o, to, to, core).start()

        def keep(to, o):
            add_slot(n, o, to)

            @pl.when(to != chip)
            def _():
                sum_copy(n, o, 8 + chip, 8 + to, o).start()

        @pl.loop(0, 4)
        def _(i):
            to_a, o_a = target(table(i, [0, 2, 3, 2]), table(i, [0, 0, 0, 1]))
            to_b, o_b = target(table(i, [1, 0, 1, 3]), table(i, [0, 1, 1, 1]))
            sums(o_a, 0)
            sums(o_b, 1)

            @pl.when(i < 3)
            def _():
                give(to_a, o_a)

            @pl.when(i == 3)
            def _():
                keep(to_a, o_a)

            @pl.when(i == 0)
            def _():
                give(to_b, o_b)

            @pl.when(i > 0)
            def _():
                keep(to_b, o_b)

    for b in range(2):
        for j in range(1, MIC):
            wave_copy(b, j, other_m(j), mu).wait_recv()
        if b == 0:
            for j in range(1, MIC):
                head_copy(j, other_m(j), mu).wait_recv()
        encode(b)
        pass_over(0, b, masked_sums)
    for b in range(2):
        pass_over(1, b, other_sums)

    def collect(n):
        for k in range(7):
            add_slot(n, d, 8 + (others[k] >> 1))
        return sb[d, 0:64, :] if n == 0 else sb[d, 64:ROWS, :]

    pick = jnp.where(d < DP // 2, pick_ref[0], pick_ref[1])
    speech, noise, w_r, w_i = solve(collect(0), lambda: collect(1), pick)
    left_half = lane32 < 64
    pay[d, 0:32, :] = jnp.where(left_half, speech, pltpu.roll(noise, 64, axis=1))
    pay[d, 32:64, :] = jnp.where(left_half, pltpu.roll(speech, 64, axis=1), noise)
    pay[d, 64:72, :] = jnp.where(row8 == 0, w_r, jnp.where(row8 == 1, w_i, 0.0))

    def pay_copy(o, sem, dev):
        return remote(pay.at[o], pay.at[o], p_send.at[sem], p_recv.at[o], dev, mu)

    for k, dev in enumerate([core, others[0]] + others[:0:-1]):
        pay_copy(d, k, dev).start()

    def group_grads(o):
        b = o >> 3
        f0 = (o & 7) << 2
        w_r = jnp.where(own8, pay[o, 64:65, :], 0.0)
        w_i = jnp.where(own8, pay[o, 65:66, :], 0.0)
        wr_hi, wr_lo = split(w_r)
        wi_hi, wi_lo = split(w_i)

        def wide(p, q):
            return jnp.concatenate([p, q], axis=1)

        first = jnp.concatenate([wide(wr_hi, wi_hi), wide(-wi_hi, wr_hi)], axis=0)
        second = jnp.concatenate([wide(wr_lo, wi_lo), wide(-wi_lo, wr_lo)], axis=0)
        left = jnp.concatenate([first, second], axis=0)
        both = jnp.dot(left.astype(BF16), zz[o].reshape(256, TD), preferred_element_type=F32)
        enh = both[0:16] + both[16:32]
        for g in range(4):
            enh_ref[b, 0, pl.ds(f0 + g, 1), :] = enh[g : g + 1, :]
            enh_ref[b, 1, pl.ds(f0 + g, 1), :] = enh[8 + g : 9 + g, :]
        e_hi, e_lo = split(GRAD_SCALE * (enh - tt[o]))
        e_rows = jnp.concatenate([e_hi, e_hi, e_lo], axis=0).astype(BF16)
        w_cols = jnp.concatenate([first, second, first], axis=0).T
        even = (lane32 // 32) % 2 == 0
        for g in range(4):
            if g % 2 == 0:
                re, neg = unpack_four(pay[o, 16 * g : 16 * g + 32, :])
            shift = 32 if g % 2 == 0 else 96
            own = even if g % 2 == 0 else ~even
            top = jnp.where(own, re, pltpu.roll(neg, shift, axis=1))
            bottom = jnp.where(own, -neg, pltpu.roll(re, shift, axis=1))
            hi, lo = split(jnp.concatenate([top, bottom], axis=0))
            cols = jnp.concatenate(
                [w_cols[32 * g : 32 * g + 32], w_cols[128 + 32 * g : 160 + 32 * g]], axis=0
            )
            lhs_g = jnp.concatenate([wide(hi, cols), wide(lo, jnp.zeros_like(cols))], axis=0)
            rhs_g = jnp.concatenate([yy[o, g], e_rows], axis=0)
            both = jnp.dot(lhs_g.astype(BF16), rhs_g, preferred_element_type=F32)
            sg = both[0:64] + both[64:128]
            place = pl.ds(pl.multiple_of(16 * (f0 + g), 16), 16)
            for q in range(4):
                sgq[place, pl.ds(pl.multiple_of(TD * (4 * b + q), TD), TD)] = jnp.concatenate(
                    [sg[8 * q : 8 * q + 8], sg[32 + 8 * q : 40 + 8 * q]], axis=0
                ).astype(BF16)

    spread = [
        [(0, 0, 0), (0, 1, 0), (2, 0, 0), (1, 1, 0), (2, 0, 1), (1, 0, 0), (1, 1, 1), (1, 0, 1)],
        [(0, 0, 1), (0, 1, 1), (2, 1, 0), (3, 1, 0), (2, 1, 1), (3, 0, 0), (3, 1, 1), (3, 0, 1)],
    ]

    @pl.loop(0, DP // 2)
    def _(i):
        pair = []
        for column in spread:
            code = table(i, [4 * k[0] + 2 * k[1] + k[2] for k in column])
            pair.append((((d + (code & 12)) & 12) | ((d ^ code) & 3), code & 1))
        for o, dc in pair:

            @pl.when(o != d)
            def _():
                pay_copy(o, 0, core).wait_recv()

            @pl.when((o != d) & (dc == 0))
            def _():
                pay_copy(o, 8 + (o >> 1), core).start()

        for o, dc in pair:
            group_grads(o)

    enh_copy = pltpu.make_async_copy(enh_ref, enh_out, in_sem.at[6])
    enh_copy.start()
    acc = nt_dot(sgq[...], frames[...])
    keep = iota((512, 256), 0) % 8 == (iota((512, 256), 1) % 128) // 16
    rows = jnp.sum(jnp.where(keep, acc, 0.0).reshape(64, 8, 256), axis=1)
    lane16 = iota((16, 128), 1)
    halves = []
    for half in (rows[:, :128], rows[:, 128:]):
        for step in (64, 32, 16):
            half = half + pltpu.roll(half, step, axis=1)
        halves.append(half)
    part = jnp.zeros((16, 128), F32)
    for p in range(4):
        at = slice(16 * p, 16 * p + 16)
        one = jnp.where((lane16 // 16) % 2 == 0, halves[0][at], halves[1][at])
        part = jnp.where(lane16 // 32 == p, one, part)
    fg[d] = part

    def grad_copy(j, slot, dev):
        return remote(fg.at[d], fg.at[slot], f_send.at[j], f_recv.at[slot], dev, mu)

    for j in range(1, DP):
        grad_copy(j, d, other_d(j)).start()
    for j in range(1, DP):
        grad_copy(j, other_d(j), d).wait_recv()
    result = fg[0]
    for j in range(1, DP):
        result = result + fg[j]
    turned = result.T
    grad_ref[...] = jnp.concatenate([turned[32 * p : 32 * p + 32] for p in range(4)], axis=1)

    enh_copy.wait()
    head_first().wait_send()
    for j in range(1, MIC):
        wave_copy(0, j, mu, mu).wait_send()
        wave_copy(1, j, mu, mu).wait_send()
        head_copy(j, mu, mu).wait_send()
    for k in range(8):
        sum_copy(0, d, 0, k, core).wait_send()
        sum_copy(1, d, 0, k, core).wait_send()
        pay_copy(d, k, core).wait_send()
    for k in range(7):
        sum_copy(0, d, 0, 8 + (others[k] >> 1), core).wait_send()
        sum_copy(1, d, 0, 8 + (others[k] >> 1), core).wait_send()
        pay_copy(d, 8 + (others[k] >> 1), core).wait_send()
    for j in range(1, DP):
        grad_copy(j, d, d).wait_send()


def local(waveform, filters, speech_mask, noise_mask, target, ref_mic):
    held = [
        pltpu.with_memory_space_constraint(v, pltpu.HBM)
        for v in (waveform, filters.T, speech_mask, noise_mask, target, ref_mic)
    ]
    vmem = pl.BlockSpec(memory_space=pltpu.VMEM)
    anywhere = pl.BlockSpec(memory_space=pl.ANY)
    dma = pltpu.SemaphoreType.DMA
    enhanced, grad = pl.pallas_call(
        body,
        out_shape=(
            jax.ShapeDtypeStruct((2, 2, 32, TD), F32),
            jax.ShapeDtypeStruct((32, 64), F32),
        ),
        in_specs=[pl.BlockSpec(memory_space=pltpu.HBM)] * 6,
        out_specs=(anywhere, vmem),
        scratch_shapes=[
            pltpu.VMEM((2, 4, 16 * TD), BF16),
            pltpu.VMEM((32, 64), BF16),
            pltpu.VMEM((2, 32, TD), BF16),
            pltpu.VMEM((2, 32, TD), BF16),
            pltpu.VMEM((2, 2, 32, TD), F32),
            pltpu.SMEM((2,), jnp.int32),
            pltpu.VMEM((2, 2, 32, TD), F32),
            dma((7,)),
            pltpu.VMEM((2, 64, TD), BF16),
            pltpu.VMEM((8, 128), F32),
            pltpu.VMEM((MIC, 2, 64, TD), BF16),
            pltpu.VMEM((MIC, 8, 128), F32),
            pltpu.VMEM((256, 8 * TD), BF16),
            pltpu.VMEM((DP, 2, 4, 32, TD), BF16),
            pltpu.VMEM((DP, 4, 128, TD), BF16),
            pltpu.VMEM((2, 512, TD), BF16),
            pltpu.VMEM((DP, ROWS, 128), F32),
            pltpu.VMEM((DP, ROWS, 128), F32),
            pltpu.VMEM((DP, PAY, 128), F32),
            pltpu.VMEM((512, 8 * TD), BF16),
            pltpu.VMEM((DP, 16, 128), F32),
            pltpu.VMEM((DP, 16, TD), F32),
            pltpu.VMEM((64, TD), F32),
            pltpu.VMEM((64, TD), F32),
            pltpu.VMEM((512, 256), BF16),
            dma((2 * MIC,)), dma((2 * MIC,)), dma((MIC,)), dma((MIC,)),
            dma((2 * DP,)), dma((2 * DP,)), dma((DP,)), dma((DP,)), dma((DP,)), dma((DP,)),
        ],
        compiler_params=pltpu.CompilerParams(
            collective_id=0, has_side_effects=True, vmem_limit_bytes=28 * 1024 * 1024
        ),
    )(*held)
    return (enhanced, grad.T)


def solution(mesh):
    in_specs = (
        P(None, "mic", "dp"),
        P("mic", None),
        P(None, "mic", "dp"),
        P(None, "mic", "dp"),
        P(None, None, "mic", "dp"),
        P(),
    )
    out_specs = (P(None, None, "mic", "dp"), P("mic", None))
    return jax.shard_map(local, mesh=mesh, in_specs=in_specs, out_specs=out_specs, check_vma=False)
```

```python
import jax
import jax.numpy as jnp
from jax import lax
from jax.experimental import pallas as pl
from jax.experimental.pallas import tpu as pltpu
from jax.sharding import PartitionSpec as P

DP = 16
MIC = 8
MICS = 32
TD = 256
LOAD = 0.05
FRAME_TOTAL = 4096.0
GRAD_SCALE = 2.0 * 64.0 / (2 * 256 * FRAME_TOTAL)
F32 = jnp.float32
BF16 = jnp.bfloat16
ROWS = 104
PAY = 72


def iota(shape, axis):
    return lax.broadcasted_iota(jnp.int32, shape, axis)


def tile4(x):
    return jnp.concatenate([x, x, x, x], axis=0)


def diagonal_blocks(x):
    rows, lanes = iota((128, 128), 0), iota((128, 128), 1)
    return jnp.where(rows // 32 == lanes // 32, tile4(x), 0.0)


def fold4(x):
    return (x[0:32] + x[32:64]) + (x[64:96] + x[96:128])


def unpack_four(packed):
    row, col = iota((32, 128), 0), iota((32, 128), 1) % 32
    turned = fold4(diagonal_blocks(packed).T)
    real = jnp.where(row <= col, packed, turned)
    negated = jnp.where(row > col, -packed, jnp.where(row < col, turned, 0.0))
    return real, negated


def inverse(a_r, a_i):
    lane = iota((32, 128), 1)
    row = iota((32, 128), 0)
    base = (lane // 32) * 32
    col = lane % 32
    for k in range(32):
        index = base + k
        c_r = jnp.take_along_axis(a_r, index, axis=1)
        c_i = jnp.take_along_axis(a_i, index, axis=1)
        scale = 1.0 / c_r[k : k + 1, :]
        here = col[0:1] == k
        r_r = jnp.where(here, 1.0, a_r[k : k + 1, :]) * scale
        r_i = jnp.where(here, 0.0, a_i[k : k + 1, :]) * scale
        at_col = col == k
        n_r = jnp.where(at_col, 0.0, a_r) - (c_r * r_r - c_i * r_i)
        n_i = jnp.where(at_col, 0.0, a_i) - (c_r * r_i + c_i * r_r)
        at_row = row == k
        a_r = jnp.where(at_row, r_r, n_r)
        a_i = jnp.where(at_row, r_i, n_i)
    return a_r, a_i


def thirds(x):
    one = x.astype(BF16).astype(F32)
    two = (x - one).astype(BF16).astype(F32)
    return one, two, x - one - two


def complex_blocks(real, imag):
    keep = iota((128, 128), 0) // 32 == iota((128, 128), 1) // 32
    r = jnp.where(keep, tile4(real), 0.0).astype(BF16)
    i = jnp.where(keep, tile4(imag), 0.0).astype(BF16)
    return jnp.concatenate(
        [jnp.concatenate([r, i], axis=1), jnp.concatenate([-i, r], axis=1)], axis=0
    )


def times(a_r, a_i, b_r, b_i):
    a = thirds(jnp.concatenate([a_r, a_i], axis=1))
    reals, imags = thirds(b_r), thirds(b_i)
    out = None
    for k in range(2, -1, -1):
        rows = jnp.concatenate(a[: 3 - k], axis=0).astype(BF16)
        part = jnp.dot(rows, complex_blocks(reals[k], imags[k]), preferred_element_type=F32)
        for m in range(2 - k, -1, -1):
            one = part[32 * m : 32 * m + 32]
            out = one if out is None else out + one
    return out[:, :128], out[:, 128:]


def group_totals(x):
    ones = jnp.where(iota((128, 128), 0) // 32 == iota((128, 128), 1) // 32, 1.0, 0.0).astype(BF16)
    n = x.shape[0]
    rows = jnp.concatenate(thirds(x), axis=0).astype(BF16)
    out = jnp.dot(rows, ones, preferred_element_type=F32)
    return out[0:n] + (out[n : 2 * n] + out[2 * n :])


def solve(total, late, pick):
    lane = iota((32, 128), 1)
    row = iota((32, 128), 0)
    eye = row == lane % 32
    inv_t = 1.0 / FRAME_TOTAL

    def column_sum(x):
        return jnp.sum(x, axis=0, keepdims=True)

    s_r, s_neg = unpack_four(total[0:32])
    n_r, n_neg = unpack_four(total[32:64])
    s_r = s_r * inv_t + jnp.where(eye, LOAD, 0.0)
    s_i = s_neg * -inv_t
    m_r, m_i = inverse(n_r * inv_t + jnp.where(eye, LOAD, 0.0), n_neg * -inv_t)
    xh_r, xh_i = times(s_r, s_i, m_r, m_i)
    q_r, q_i = times(m_r, m_i, xh_r, xh_i)
    at_ref = row == pick
    conj_c_r = column_sum(jnp.where(at_ref, xh_r, 0.0))
    conj_c_i = column_sum(jnp.where(at_ref, xh_i, 0.0))
    sref_r = column_sum(jnp.where(at_ref, s_r, 0.0))
    sref_i = column_sum(jnp.where(at_ref, s_i, 0.0))
    diag = column_sum(jnp.where(eye, xh_r, 0.0))
    first = group_totals(
        jnp.concatenate(
            [
                jnp.broadcast_to(diag, (8, 128)),
                m_r * sref_r + m_i * sref_i,
                m_i * sref_r - m_r * sref_i,
            ],
            axis=0,
        )
    )
    inv_tau = 1.0 / first[0:1]
    c_r, c_i = first[8:40], first[40:72]
    w_r = conj_c_r * inv_tau
    w_i = -conj_c_i * inv_tau
    h_r, h_i = c_r * inv_tau, c_i * inv_tau
    rest = late()
    k_r, k_neg = unpack_four(rest[0:32])
    d_r, d_i = rest[32:33], rest[33:34]
    g_r = GRAD_SCALE * (column_sum(h_r * k_r - h_i * k_neg) - d_r)
    g_i = GRAD_SCALE * (column_sum(h_i * k_r + h_r * k_neg) - d_i)
    gc_r, gc_i = g_r * inv_tau, g_i * inv_tau
    gw = (g_r * w_r + g_i * w_i) * inv_tau
    second = group_totals(
        jnp.concatenate(
            [
                jnp.broadcast_to(gw, (8, 128)),
                m_r * gc_r - m_i * gc_i,
                m_r * gc_i + m_i * gc_r,
            ],
            axis=0,
        )
    )
    gt2 = -2.0 * second[0:1]
    u_r, u_i = second[8:40], second[40:72]
    uh_r = column_sum(jnp.where(eye, u_r, 0.0))
    uh_i = -column_sum(jnp.where(eye, u_i, 0.0))
    col_ref = (lane % 32) == pick
    p_r = jnp.where(col_ref, u_r, 0.0) + jnp.where(at_ref, uh_r, 0.0) + gt2 * m_r
    p_i = jnp.where(col_ref, u_i, 0.0) + jnp.where(at_ref, uh_i, 0.0) + gt2 * m_i
    n_r = (u_r * conj_c_r - u_i * conj_c_i) + (c_r * uh_r - c_i * uh_i) + gt2 * q_r
    n_i = (u_r * conj_c_i + u_i * conj_c_r) + (c_r * uh_i + c_i * uh_r) + gt2 * q_i
    upper = row <= lane % 32
    speech = jnp.where(upper, p_r, p_i) * inv_t
    noise = jnp.where(upper, n_r, n_i) * (-inv_t)
    return speech, noise, w_r, w_i


def tn_dot(a, b):
    return lax.dot_general(a, b, (((0,), (0,)), ((), ())), preferred_element_type=F32)


def block_filters(filters_t):
    lane = iota((32, 256), 1)
    spread = jnp.where(iota((32, 256), 0) == (lane // 128) * 16 + lane % 16, 1.0, 0.0)
    wide = tn_dot(filters_t, spread.astype(BF16)).astype(BF16)
    repeat = jnp.where(iota((512, 64), 0) // 8 == iota((512, 64), 1), 1.0, 0.0).astype(BF16)
    full = jnp.dot(repeat, wide, preferred_element_type=F32)
    keep = iota((512, 256), 0) % 8 == (iota((512, 256), 1) % 128) // 16
    return jnp.where(keep, full, 0.0).astype(BF16)


def split(x):
    high = x.astype(BF16).astype(F32)
    return high, x - high


def nt_dot(a, b):
    return lax.dot_general(a, b, (((1,), (1,)), ((), ())), preferred_element_type=F32)


def body(
    wave_in, filt_in, smask_in, nmask_in, target_in, pick_in,
    enh_out, grad_ref,
    wave_ref, filt_ref, smask_ref, nmask_ref, target_ref, pick_ref, enh_ref, in_sem,
    wblk, head, gath, heads, frames, zz, yy, lhs, sb, rb, pay, sgq, fg, tt, ms, mn, fb,
    g_send, g_recv, h_send, h_recv, s_send, s_recv, p_send, p_recv, f_send, f_recv,
):
    d = lax.axis_index("dp")
    mu = lax.axis_index("mic")
    prev = lax.rem(d + DP - 1, DP)
    nxt = lax.rem(d + 1, DP)
    at_z, at_x, at_c = d >> 2, (d >> 1) & 1, d & 1
    chip = d >> 1
    core = d ^ 1

    def rel(dz, dx, dc):
        return ((d + 4 * dz) & 12) | ((d ^ (2 * dx + dc)) & 3)

    others = [rel(0, 1, 0), rel(1, 0, 0), rel(3, 0, 0), rel(1, 1, 0), rel(3, 1, 0), rel(2, 0, 0), rel(2, 1, 0)]

    def table(i, values):
        out = values[0]
        for k in range(1, len(values)):
            out = jnp.where(i == k, values[k], out)
        return out

    def other_d(j):
        return lax.rem(d + j, DP)

    def other_m(j):
        return lax.rem(mu + j, MIC)

    def remote(src, dst, send, recv, dev_d, dev_m):
        return pltpu.make_async_remote_copy(
            src_ref=src, dst_ref=dst, send_sem=send, recv_sem=recv,
            device_id={"dp": dev_d, "mic": dev_m}, device_id_type=pl.DeviceIdType.MESH,
        )

    loads = [
        pltpu.make_async_copy(src, dst, in_sem.at[k])
        for k, (src, dst) in enumerate(
            [
                (wave_in, wave_ref), (filt_in, filt_ref), (smask_in, smask_ref),
                (nmask_in, nmask_ref), (target_in, target_ref), (pick_in, pick_ref),
            ]
        )
    ]
    for load in loads:
        load.start()

    barrier = pltpu.get_barrier_semaphore()

    def greet(dev_d, dev_m):
        pl.semaphore_signal(
            barrier, inc=1, device_id={"dp": dev_d, "mic": dev_m},
            device_id_type=pl.DeviceIdType.MESH,
        )

    for j in range(1, MIC):
        greet(d, other_m(j))
    for peer in others + [core, prev, nxt]:
        greet(peer, mu)

    for load in loads:
        load.wait()

    turn = iota((128, 1024), 0)
    lane = iota((128, 1024), 1)
    choose = (turn % 4 == lane // TD) & (turn // 4 == (lane % TD) // 8)
    choose = jnp.where(choose, 1.0, 0.0).astype(BF16)
    phase = iota((16, 1024), 1) % 8
    for b in range(2):
        rows = wave_ref[b].astype(F32)
        head[4 * b : 4 * b + 4, :] = rows[:, 0:128]
        stacked = jnp.concatenate([rows[:, 128 * r : 128 * r + 128] for r in range(32)], axis=0)
        spread = jnp.dot(stacked.T.astype(BF16), choose, preferred_element_type=F32)
        taps = spread[0:16]
        for k in range(1, 8):
            taps = jnp.where(phase == k, spread[16 * k : 16 * k + 16], taps)
        for m in range(4):
            wblk[b, 16 * m : 16 * m + 16, :] = taps[:, TD * m : TD * m + TD].astype(BF16)

    fb[...] = block_filters(filt_ref[...])
    ms[...] = smask_ref[...].reshape(64, TD).astype(F32)
    mn[...] = nmask_ref[...].reshape(64, TD).astype(F32)
    for o in range(DP):
        for v in range(2):
            tt[o, 8 * v : 8 * v + 4, :] = target_ref[o // 8, v, (o % 8) * 4 : (o % 8) * 4 + 4, :]
            tt[o, 8 * v + 4 : 8 * v + 8, :] = jnp.zeros((4, TD), F32)

    pl.semaphore_wait(barrier, MIC + DP // 2 + 1)

    def wave_copy(b, j, slot, dev):
        return remote(wblk.at[b], gath.at[slot, b], g_send.at[MIC * b + j], g_recv.at[MIC * b + slot], d, dev)

    def head_copy(j, slot, dev):
        return remote(heads.at[mu], heads.at[slot], h_send.at[j], h_recv.at[slot], d, dev)

    def head_first():
        return remote(head, heads.at[mu], h_send.at[0], h_recv.at[mu], prev, mu)

    head_first().start()
    for j in range(1, MIC):
        wave_copy(0, j, mu, other_m(j)).start()
    gath[mu] = wblk[...]
    head_first().wait_recv()
    for j in range(1, MIC):
        head_copy(j, mu, other_m(j)).start()
    for j in range(1, MIC):
        wave_copy(1, j, mu, other_m(j)).start()

    last = d == DP - 1
    tap128 = iota((128, 128), 1) == iota((128, 128), 0) % 16
    end = iota((128, 128), 1) == 127

    def prepare(b):
        for q in range(4):
            x = jnp.concatenate([gath[2 * q, b], gath[2 * q + 1, b]], axis=0).astype(F32)
            piece = slice(TD * (4 * b + q), TD * (4 * b + q) + TD)
            frames[0:128, piece] = x.astype(BF16)
            frames[128:256, piece] = pltpu.roll(x, TD - 1, axis=1).astype(BF16)

    def encode(b):
        for q in range(4):
            near = jnp.concatenate(
                [
                    jnp.broadcast_to(heads[2 * q + p, 4 * b + m : 4 * b + m + 1, :], (16, 128))
                    for p in range(2)
                    for m in range(4)
                ],
                axis=0,
            )
            near = jnp.where(last, 0.0, near)
            column = jnp.sum(jnp.where(tap128, near, 0.0), axis=1, keepdims=True)
            piece = slice(TD * (4 * b + q) + 128, TD * (4 * b + q) + TD)
            tail = frames[128:256, piece].astype(F32)
            frames[128:256, piece] = jnp.where(end, column, tail).astype(BF16)
        for half in range(2):
            at = TD * (4 * b + 2 * half)
            a0 = jnp.dot(fb[...], frames[:, at : at + TD], preferred_element_type=F32)
            a1 = jnp.dot(fb[...], frames[:, at + TD : at + 2 * TD], preferred_element_type=F32)
            z = jnp.concatenate(
                [a0.reshape(8, 4, 2, 8, TD), a1.reshape(8, 4, 2, 8, TD)], axis=3
            ).astype(BF16)
            for v in range(2):
                zz[8 * b : 8 * b + 8, v, :, 16 * half : 16 * half + 16, :] = z[:, :, v]

    lane32 = iota((32, 128), 1)
    upper = iota((32, 128), 0) <= lane32 % 32
    row8 = iota((8, 128), 0)
    own8 = row8 == iota((8, 128), 1) // 32

    def packed(out, first):
        value = jnp.zeros((32, 128), F32)
        for g in range(4):
            re = out[first + 32 * g : first + 32 * g + 32]
            im = out[first + 128 + 32 * g : first + 160 + 32 * g]
            one = jnp.where(upper, re[:, :128] + im[:, 128:], im[:, :128] - re[:, 128:])
            value = jnp.where(lane32 // 32 == g, one, value)
        return value

    def masked_sums(o, w):
        for g in range(4):
            for k, ref in enumerate((ms, mn)):
                mask = jnp.broadcast_to(ref[pl.ds(4 * o + g, 1), :], (32, TD)).astype(BF16)
                for v in range(2):
                    part = zz[o, v, g] * mask
                    at = 128 * v + 32 * g
                    lhs[w, 256 * k + at : 256 * k + at + 32, :] = part
                    row = 64 * k + 32 * ((v + g) % 2)
                    yy[o, g, row : row + 32, :] = part
        out = nt_dot(lhs[w], zz[o].reshape(256, TD))
        sb[o, 0:32, :] = packed(out, 0)
        sb[o, 32:64, :] = packed(out, 256)

    def other_sums(o, w):
        t_hi, t_lo = split(tt[o])
        own = zz[o].reshape(256, TD)
        t_rows = jnp.concatenate([t_hi, t_lo], axis=0).astype(BF16)
        out = nt_dot(jnp.concatenate([own, t_rows], axis=0), own)
        sb[o, 64:96, :] = packed(out, 0)
        t0 = out[256:264] + out[272:280]
        t1 = out[264:272] + out[280:288]
        d_r = jnp.sum(jnp.where(own8, t0[:, :128] + t1[:, 128:], 0.0), axis=0, keepdims=True)
        d_i = jnp.sum(jnp.where(own8, t0[:, 128:] - t1[:, :128], 0.0), axis=0, keepdims=True)
        sb[o, 96:104, :] = jnp.where(row8 == 0, d_r, jnp.where(row8 == 1, d_i, 0.0))

    def sum_copy(n, o, slot, sem, dev):
        rows = slice(0, 64) if n == 0 else slice(64, ROWS)
        return remote(
            sb.at[o, rows], rb.at[slot, rows], s_send.at[DP * n + sem], s_recv.at[DP * n + slot],
            dev, mu,
        )

    def add_slot(n, o, slot):
        rows = slice(0, 64) if n == 0 else slice(64, ROWS)
        sum_copy(n, o, slot, slot, core).wait_recv()
        sb[o, rows, :] = sb[o, rows, :] + rb[slot, rows, :]

    def pass_over(n, b, sums):
        here = jnp.where((at_z >> 1) == b, 1, 0)

        def target(k, mine):
            to = 4 * b + 2 * ((at_z + (k >> 1) + here) & 1) + ((at_x + 1 + k) & 1)
            return to, 2 * to + ((at_c + 1 + mine) & 1)

        def give(to, o):
            sum_copy(n, o, to, to, core).start()

        def keep(to, o):
            add_slot(n, o, to)

            @pl.when(to != chip)
            def _():
                sum_copy(n, o, 8 + chip, 8 + to, o).start()

        @pl.loop(0, 4)
        def _(i):
            to_a, o_a = target(table(i, [0, 2, 3, 2]), table(i, [0, 0, 0, 1]))
            to_b, o_b = target(table(i, [1, 0, 1, 3]), table(i, [0, 1, 1, 1]))
            sums(o_a, 0)
            sums(o_b, 1)

            @pl.when(i < 3)
            def _():
                give(to_a, o_a)

            @pl.when(i == 3)
            def _():
                keep(to_a, o_a)

            @pl.when(i == 0)
            def _():
                give(to_b, o_b)

            @pl.when(i > 0)
            def _():
                keep(to_b, o_b)

    for b in range(2):
        for j in range(1, MIC):
            wave_copy(b, j, other_m(j), mu).wait_recv()
        prepare(b)
        if b == 0:
            for j in range(1, MIC):
                head_copy(j, other_m(j), mu).wait_recv()
        encode(b)
        pass_over(0, b, masked_sums)
    for b in range(2):
        pass_over(1, b, other_sums)

    def collect(n):
        for k in range(7):
            add_slot(n, d, 8 + (others[k] >> 1))
        return sb[d, 0:64, :] if n == 0 else sb[d, 64:ROWS, :]

    pick = jnp.where(d < DP // 2, pick_ref[0], pick_ref[1])
    speech, noise, w_r, w_i = solve(collect(0), lambda: collect(1), pick)
    left_half = lane32 < 64
    pay[d, 0:32, :] = jnp.where(left_half, speech, pltpu.roll(noise, 64, axis=1))
    pay[d, 32:64, :] = jnp.where(left_half, pltpu.roll(speech, 64, axis=1), noise)
    pay[d, 64:72, :] = jnp.where(row8 == 0, w_r, jnp.where(row8 == 1, w_i, 0.0))

    def pay_copy(o, sem, dev):
        return remote(pay.at[o], pay.at[o], p_send.at[sem], p_recv.at[o], dev, mu)

    for k, dev in enumerate([core, others[0]] + others[:0:-1]):
        pay_copy(d, k, dev).start()

    def group_grads(o):
        b = o >> 3
        f0 = (o & 7) << 2
        w_r = jnp.where(own8, pay[o, 64:65, :], 0.0)
        w_i = jnp.where(own8, pay[o, 65:66, :], 0.0)
        wr_hi, wr_lo = split(w_r)
        wi_hi, wi_lo = split(w_i)

        def wide(p, q):
            return jnp.concatenate([p, q], axis=1)

        first = jnp.concatenate([wide(wr_hi, wi_hi), wide(-wi_hi, wr_hi)], axis=0)
        second = jnp.concatenate([wide(wr_lo, wi_lo), wide(-wi_lo, wr_lo)], axis=0)
        left = jnp.concatenate([first, second], axis=0)
        both = jnp.dot(left.astype(BF16), zz[o].reshape(256, TD), preferred_element_type=F32)
        enh = both[0:16] + both[16:32]
        for g in range(4):
            enh_ref[b, 0, pl.ds(f0 + g, 1), :] = enh[g : g + 1, :]
            enh_ref[b, 1, pl.ds(f0 + g, 1), :] = enh[8 + g : 9 + g, :]
        e_hi, e_lo = split(GRAD_SCALE * (enh - tt[o]))
        e_rows = jnp.concatenate([e_hi, e_hi, e_lo], axis=0).astype(BF16)
        w_cols = jnp.concatenate([first, second, first], axis=0).T
        even = (lane32 // 32) % 2 == 0
        for g in range(4):
            if g % 2 == 0:
                re, neg = unpack_four(pay[o, 16 * g : 16 * g + 32, :])
            shift = 32 if g % 2 == 0 else 96
            own = even if g % 2 == 0 else ~even
            top = jnp.where(own, re, pltpu.roll(neg, shift, axis=1))
            bottom = jnp.where(own, -neg, pltpu.roll(re, shift, axis=1))
            hi, lo = split(jnp.concatenate([top, bottom], axis=0))
            cols = jnp.concatenate(
                [w_cols[32 * g : 32 * g + 32], w_cols[128 + 32 * g : 160 + 32 * g]], axis=0
            )
            lhs_g = jnp.concatenate([wide(hi, cols), wide(lo, jnp.zeros_like(cols))], axis=0)
            rhs_g = jnp.concatenate([yy[o, g], e_rows], axis=0)
            both = jnp.dot(lhs_g.astype(BF16), rhs_g, preferred_element_type=F32)
            sg = both[0:64] + both[64:128]
            place = pl.ds(pl.multiple_of(16 * (f0 + g), 16), 16)
            for q in range(4):
                sgq[place, pl.ds(pl.multiple_of(TD * (4 * b + q), TD), TD)] = jnp.concatenate(
                    [sg[8 * q : 8 * q + 8], sg[32 + 8 * q : 40 + 8 * q]], axis=0
                ).astype(BF16)

    spread = [
        [(0, 0, 0), (0, 1, 0), (2, 0, 0), (1, 1, 0), (2, 0, 1), (1, 0, 0), (1, 1, 1), (1, 0, 1)],
        [(0, 0, 1), (0, 1, 1), (2, 1, 0), (3, 1, 0), (2, 1, 1), (3, 0, 0), (3, 1, 1), (3, 0, 1)],
    ]

    @pl.loop(0, DP // 2)
    def _(i):
        pair = []
        for column in spread:
            code = table(i, [4 * k[0] + 2 * k[1] + k[2] for k in column])
            pair.append((((d + (code & 12)) & 12) | ((d ^ code) & 3), code & 1))
        for o, dc in pair:

            @pl.when(o != d)
            def _():
                pay_copy(o, 0, core).wait_recv()

            @pl.when((o != d) & (dc == 0))
            def _():
                pay_copy(o, 8 + (o >> 1), core).start()

        for o, dc in pair:
            group_grads(o)

    enh_copy = pltpu.make_async_copy(enh_ref, enh_out, in_sem.at[6])
    enh_copy.start()
    acc = nt_dot(sgq[...], frames[...])
    keep = iota((512, 256), 0) % 8 == (iota((512, 256), 1) % 128) // 16
    rows = jnp.sum(jnp.where(keep, acc, 0.0).reshape(64, 8, 256), axis=1)
    lane16 = iota((16, 128), 1)
    halves = []
    for half in (rows[:, :128], rows[:, 128:]):
        for step in (64, 32, 16):
            half = half + pltpu.roll(half, step, axis=1)
        halves.append(half)
    part = jnp.zeros((16, 128), F32)
    for p in range(4):
        at = slice(16 * p, 16 * p + 16)
        one = jnp.where((lane16 // 16) % 2 == 0, halves[0][at], halves[1][at])
        part = jnp.where(lane16 // 32 == p, one, part)
    fg[d] = part

    def grad_copy(j, slot, dev):
        return remote(fg.at[d], fg.at[slot], f_send.at[j], f_recv.at[slot], dev, mu)

    for j in range(1, DP):
        grad_copy(j, d, other_d(j)).start()
    for j in range(1, DP):
        grad_copy(j, other_d(j), d).wait_recv()
    result = fg[0]
    for j in range(1, DP):
        result = result + fg[j]
    turned = result.T
    grad_ref[...] = jnp.concatenate([turned[32 * p : 32 * p + 32] for p in range(4)], axis=1)

    enh_copy.wait()
    head_first().wait_send()
    for j in range(1, MIC):
        wave_copy(0, j, mu, mu).wait_send()
        wave_copy(1, j, mu, mu).wait_send()
        head_copy(j, mu, mu).wait_send()
    for k in range(8):
        sum_copy(0, d, 0, k, core).wait_send()
        sum_copy(1, d, 0, k, core).wait_send()
        pay_copy(d, k, core).wait_send()
    for k in range(7):
        sum_copy(0, d, 0, 8 + (others[k] >> 1), core).wait_send()
        sum_copy(1, d, 0, 8 + (others[k] >> 1), core).wait_send()
        pay_copy(d, 8 + (others[k] >> 1), core).wait_send()
    for j in range(1, DP):
        grad_copy(j, d, d).wait_send()


def local(waveform, filters, speech_mask, noise_mask, target, ref_mic):
    held = [
        pltpu.with_memory_space_constraint(v, pltpu.HBM)
        for v in (waveform, filters.T, speech_mask, noise_mask, target, ref_mic)
    ]
    vmem = pl.BlockSpec(memory_space=pltpu.VMEM)
    anywhere = pl.BlockSpec(memory_space=pl.ANY)
    dma = pltpu.SemaphoreType.DMA
    enhanced, grad = pl.pallas_call(
        body,
        out_shape=(
            jax.ShapeDtypeStruct((2, 2, 32, TD), F32),
            jax.ShapeDtypeStruct((32, 64), F32),
        ),
        in_specs=[pl.BlockSpec(memory_space=pltpu.HBM)] * 6,
        out_specs=(anywhere, vmem),
        scratch_shapes=[
            pltpu.VMEM((2, 4, 16 * TD), BF16),
            pltpu.VMEM((32, 64), BF16),
            pltpu.VMEM((2, 32, TD), BF16),
            pltpu.VMEM((2, 32, TD), BF16),
            pltpu.VMEM((2, 2, 32, TD), F32),
            pltpu.SMEM((2,), jnp.int32),
            pltpu.VMEM((2, 2, 32, TD), F32),
            dma((7,)),
            pltpu.VMEM((2, 64, TD), BF16),
            pltpu.VMEM((8, 128), F32),
            pltpu.VMEM((MIC, 2, 64, TD), BF16),
            pltpu.VMEM((MIC, 8, 128), F32),
            pltpu.VMEM((256, 8 * TD), BF16),
            pltpu.VMEM((DP, 2, 4, 32, TD), BF16),
            pltpu.VMEM((DP, 4, 128, TD), BF16),
            pltpu.VMEM((2, 512, TD), BF16),
            pltpu.VMEM((DP, ROWS, 128), F32),
            pltpu.VMEM((DP, ROWS, 128), F32),
            pltpu.VMEM((DP, PAY, 128), F32),
            pltpu.VMEM((512, 8 * TD), BF16),
            pltpu.VMEM((DP, 16, 128), F32),
            pltpu.VMEM((DP, 16, TD), F32),
            pltpu.VMEM((64, TD), F32),
            pltpu.VMEM((64, TD), F32),
            pltpu.VMEM((512, 256), BF16),
            dma((2 * MIC,)), dma((2 * MIC,)), dma((MIC,)), dma((MIC,)),
            dma((2 * DP,)), dma((2 * DP,)), dma((DP,)), dma((DP,)), dma((DP,)), dma((DP,)),
        ],
        compiler_params=pltpu.CompilerParams(
            collective_id=0, has_side_effects=True, vmem_limit_bytes=28 * 1024 * 1024
        ),
    )(*held)
    return (enhanced, grad.T)


def solution(mesh):
    in_specs = (
        P(None, "mic", "dp"),
        P("mic", None),
        P(None, "mic", "dp"),
        P(None, "mic", "dp"),
        P(None, None, "mic", "dp"),
        P(),
    )
    out_specs = (P(None, None, "mic", "dp"), P("mic", None))
    return jax.shard_map(local, mesh=mesh, in_specs=in_specs, out_specs=out_specs, check_vma=False)
```
